32 devices in a mesh: dp: 4 (over x, core), fsdp: 8 (over z, y).
Axes of the slice: x: 2, y: 2, z: 4, core: 2. Of those that a mesh axis runs over, the one named last changes fastest.
Arguments:
- tokens: bfloat16 [8192, 2048], P(('dp', 'fsdp')), may hold values from -6 to 6
- w_q: bfloat16 [2048, 2048], P(('dp', 'fsdp')), may hold values from -0.125 to 0.125
- w_kv: bfloat16 [2048, 256], P(('dp', 'fsdp')), may hold values from -0.125 to 0.125
- g_attn: bfloat16 [2048], P(('dp', 'fsdp')), may hold values from 0.25 to 1.75
- g_mlp: bfloat16 [2048], P(('dp', 'fsdp')), may hold values from 0.25 to 1.75
- w_o: bfloat16 [2048, 2048], P(('dp', 'fsdp')), may hold values from -0.75 to 0.75
- w_gu: bfloat16 [5632, 2, 2048], P(('dp', 'fsdp')), may hold values from -0.125 to 0.125
- w_down: bfloat16 [5632, 2048], P(('dp', 'fsdp')), may hold values from -0.078125 to 0.078125
- grad_out: bfloat16 [8192, 2048], P(('dp', 'fsdp')), may hold values from -6 to 6
- grad_kv: bfloat16 [8192, 256], P(('dp', 'fsdp')), may hold values from -4 to 4
- group_id: int32 [32], P(('dp', 'fsdp')), may hold values from 0 to 7
- group_size: int32 [8], replicated, may hold values from 1 to 4
- group_weight: float32 [8], replicated, may hold values from 1 to 4
Outputs:
- output: bfloat16 [8192, 2048], P(('dp', 'fsdp'))
- d_tokens: float32 [8192, 2048], P(('dp', 'fsdp'))
- kv_out: bfloat16 [8192, 256], P(('dp', 'fsdp'))
- d_kv: float32 [8192, 256], P(('dp', 'fsdp'))
- d_w_q: float32 [2048, 2048], P(('dp', 'fsdp'))
- d_w_kv: float32 [2048, 256], P(('dp', 'fsdp'))
- d_g_attn: float32 [2048], P(('dp', 'fsdp'))
- d_g_mlp: float32 [2048], P(('dp', 'fsdp'))
- d_w_o: float32 [2048, 2048], P(('dp', 'fsdp'))
- d_w_gu: float32 [5632, 2, 2048], P(('dp', 'fsdp'))
- d_w_down: float32 [5632, 2048], P(('dp', 'fsdp'))
The draws below stay inside these ranges and needn't reach their ends.
All inputs are finite; a program needn't handle non-finite values.
Results may differ from the reference program's by a relative error of at most 0.015.
Values may be sent and summed in bfloat16 or wider, within the bound.
No kernel may reach another device: no remote copies, remote signals or barrier semaphores. Data moves between devices by JAX's collectives and lax.ppermute only.
A program may use at most 256 MiB of HBM per device.

```python
import math
import jax
import jax.numpy as jnp
from jax import lax

D = 2048
HEADS = 16
DH = 128
FF = 5632
GROUPS = 8
TOK_DEV = 256
HD = 2048
SEQS = 32
TOKENS = 8192


def with_ends(values, stream_key, low, high):
    dims = values.shape
    spot = [jax.random.randint(jax.random.fold_in(stream_key, axis), (), 0, dims[axis]) for axis in range(len(dims))]
    values = values.at[tuple(spot)].set(low)
    longest = dims.index(max(dims))
    spot[longest] = (spot[longest] + 1) % dims[longest]
    return values.at[tuple(spot)].set(high)


def levels(key, extent, pieces, low, high):
    gain, own = 1.0, jax.random.fold_in(key, 6)
    for dim, parts in pieces:
        heights = jnp.exp(jax.random.uniform(jax.random.fold_in(own, dim), (parts,), jnp.float32, low / len(pieces), high / len(pieces)))
        gain = gain * jnp.repeat(heights, extent[dim] // parts).reshape([-1 if axis == dim else 1 for axis in range(len(extent))])
    return gain


def noise(rng, extent, spread, limit, split=(), kind=jnp.bfloat16):
    values = spread * jax.random.normal(rng, extent, jnp.float32)
    if split:
        values = values * levels(rng, extent, split, -0.22, 0.18)
    return jnp.clip(values, -limit, limit).astype(kind)


def setup_inputs(seed: int = 0) -> dict:
    seeds = jax.random.split(jax.random.key(seed), 14)
    return {
        "tokens": noise(seeds[0], (TOKENS, D), 1.0, 6.0, ((0, 32),)),
        "w_q": noise(seeds[1], (D, HD), D ** -0.5, 0.125, ((0, 32),)),
        "w_kv": noise(seeds[2], (D, 2 * DH), D ** -0.5, 0.125, ((0, 32),)),
        "g_attn": jnp.clip(1.0 + 0.15 * jax.random.normal(seeds[3], (D,), jnp.float32), 0.25, 1.75).astype(jnp.bfloat16),
        "g_mlp": jnp.clip(1.0 + 0.15 * jax.random.normal(seeds[4], (D,), jnp.float32), 0.25, 1.75).astype(jnp.bfloat16),
        "w_o": noise(seeds[5], (HD, D), (HD // 32) ** -0.5, 0.75, ((0, 32),)),
        "w_gu": noise(seeds[6], (FF, 2, D), D ** -0.5, 0.125, ((0, 32),)),
        "w_down": noise(seeds[7], (FF, D), FF ** -0.5, 0.078125, ((0, 32),)),
        "grad_out": noise(seeds[8], (TOKENS, D), 1.0, 6.0, ((0, 32),)),
        "grad_kv": noise(seeds[9], (TOKENS, 2 * DH), 0.5, 4.0, ((0, 32),)),
        "group_id": with_ends(jax.random.randint(seeds[10], (SEQS,), 0, GROUPS), jax.random.fold_in(seeds[10], 1), 0, GROUPS - 1).astype(jnp.int32),
        "group_size": with_ends(jax.random.randint(seeds[11], (GROUPS,), 1, 5), jax.random.fold_in(seeds[11], 1), 1, 4).astype(jnp.int32),
        "group_weight": jnp.clip(jnp.exp(jax.random.uniform(seeds[12], (GROUPS,), jnp.float32, math.log(1.0), math.log(4.0))), 1.0, 4.0),
    }


@jax.custom_vjp
def low(v):
    return lax.optimization_barrier(v.astype(jnp.bfloat16)).astype(jnp.float32)

@jax.custom_vjp
def low_back(v):
    return v

def low_keep(v):
    return (low(v), None)

def low_pass(kept, grad):
    return (grad,)

def back_keep(v):
    return (v, None)

def back_low(kept, grad):
    return (low(grad),)
low.defvjp(low_keep, low_pass)
low_back.defvjp(back_keep, back_low)
epsilon = 1e-05
theta_base = 10000.0
highest = lax.Precision.HIGHEST

def rope_tables(length, width):
    halfway = width // 2
    freqs = theta_base ** (-(jnp.arange(halfway, dtype=jnp.float32) * 2.0 / width))
    angles = jnp.arange(length, dtype=jnp.float32)[:, None] * freqs[None, :]
    return (jnp.cos(angles), jnp.sin(angles))

def rotate(vectors, cosines, sine_part):
    halfway = vectors.shape[-1] // 2
    front = vectors[..., :halfway]
    behind = vectors[..., halfway:]
    return jnp.concatenate([front * cosines - behind * sine_part, behind * cosines + front * sine_part], axis=-1)

def attend(operands):
    queries, keys, values = operands
    length = queries.shape[0]
    raw_scores = low_back(jnp.einsum('thd,sd->hts', queries, keys, precision=highest))
    causal = jnp.arange(length)[:, None] >= jnp.arange(length)[None, :]
    logits = jnp.where(causal[None], raw_scores * DH ** (-0.5), -1e+30)
    weights = low(jax.nn.softmax(logits, axis=-1))
    mixed = jnp.einsum('hts,sd->thd', weights, values, precision=highest)
    return mixed.reshape(length, -1)

def block_forward(inputs, w_q, w_kv, g_attn, g_mlp, w_o, w_gu, w_down, k_extra, v_extra):
    batch, length, width = inputs.shape
    cosines, sine_part = rope_tables(length, DH)
    normed_one = inputs * lax.rsqrt(lax.optimization_barrier(jnp.mean(inputs * inputs, axis=-1, keepdims=True)) + epsilon)
    h_one = low(normed_one * g_attn)
    q_pre = low_back(jnp.einsum('btd,de->bte', h_one, w_q, precision=highest))
    kv_pre = low_back(jnp.einsum('btd,de->bte', h_one, w_kv, precision=highest))
    queries = low(rotate(q_pre.reshape(batch, length, HEADS, DH), cosines[None, :, None, :], sine_part[None, :, None, :]))
    keys = low(rotate(kv_pre[..., :DH], cosines[None], sine_part[None])) + k_extra
    values = low(kv_pre[..., DH:]) + v_extra
    attended = lax.map(jax.checkpoint(attend), (queries, keys, values))
    attended = low_back(low(attended))
    branch = low_back(jnp.einsum('bte,ed->btd', attended, w_o, precision=highest))
    x_mid = inputs + branch
    normed_two = x_mid * lax.rsqrt(lax.optimization_barrier(jnp.mean(x_mid * x_mid, axis=-1, keepdims=True)) + epsilon)
    h_two = low(normed_two * g_mlp)
    both_proj = low_back(jnp.einsum('btd,fkd->btkf', h_two, w_gu, precision=highest))
    hidden = low(jax.nn.silu(both_proj[:, :, 0]) * both_proj[:, :, 1])
    mlp_out = low_back(jnp.einsum('btf,fd->btd', hidden, w_down, precision=highest))
    return (x_mid + mlp_out, keys, values)

def reference(tokens, w_q, w_kv, g_attn, g_mlp, w_o, w_gu, w_down, grad_out, grad_kv, group_id, group_size, group_weight):
    matches = group_id[:, None] == jnp.arange(GROUPS, dtype=jnp.int32)[None, :]
    ratios = group_weight.astype(jnp.float32) / group_size.astype(jnp.float32)
    factors = lax.optimization_barrier(jnp.sum(jnp.where(matches, ratios[None, :], 0.0), axis=1))
    per_step = math.gcd(SEQS, 8)
    step_total = SEQS // per_step
    shaped_in = tokens.astype(jnp.float32).reshape(step_total, per_step, TOK_DEV, D)
    scaled_out = grad_out.astype(jnp.float32).reshape(SEQS, TOK_DEV, D) * factors[:, None, None]
    scaled_kv = grad_kv.astype(jnp.float32).reshape(SEQS, TOK_DEV, 2 * DH) * factors[:, None, None]
    shaped_out = scaled_out.reshape(step_total, per_step, TOK_DEV, D)
    shaped_kv = scaled_kv.reshape(step_total, per_step, TOK_DEV, 2 * DH)
    params = (w_q.astype(jnp.float32), w_kv.astype(jnp.float32), g_attn.astype(jnp.float32), g_mlp.astype(jnp.float32), w_o.astype(jnp.float32), w_gu.astype(jnp.float32), w_down.astype(jnp.float32))

    def one_step(totals, blocks):
        inputs, grad_block, kv_block = blocks
        zero_extra = jnp.zeros((per_step, TOK_DEV, DH), inputs.dtype)
        primal, pullback = jax.vjp(block_forward, inputs, params[0], params[1], params[2], params[3], params[4], params[5], params[6], zero_extra, zero_extra)
        grads = pullback((grad_block, kv_block[..., :DH], kv_block[..., DH:]))
        totals = tuple((total + grads[index + 1] for index, total in enumerate(totals)))
        result = (primal[0].astype(jnp.bfloat16), jnp.concatenate([primal[1], primal[2]], axis=-1).astype(jnp.bfloat16), grads[0], jnp.concatenate([grads[8], grads[9]], axis=-1))
        return (totals, result)
    start_totals = tuple((jnp.zeros_like(param) for param in params))
    totals, stacked = lax.scan(one_step, start_totals, (shaped_in, shaped_out, shaped_kv))
    output = stacked[0].reshape(TOKENS, D)
    kv_out = stacked[1].reshape(TOKENS, 2 * DH)
    d_tokens = stacked[2].reshape(TOKENS, D)
    d_kv = stacked[3].reshape(TOKENS, 2 * DH)
    return (output, d_tokens, kv_out, d_kv, totals[0], totals[1], totals[2], totals[3], totals[4], totals[5], totals[6])
```

```python
import jax
import jax.numpy as jnp
from jax import lax
from jax.sharding import PartitionSpec as P

epsilon = 1e-05
theta_base = 10000.0
bf16 = jnp.bfloat16
f32 = jnp.float32


def rope_tables(length, width):
    halfway = width // 2
    freqs = theta_base ** (-(jnp.arange(halfway, dtype=jnp.float32) * 2.0 / width))
    angles = jnp.arange(length, dtype=jnp.float32)[:, None] * freqs[None, :]
    return (jnp.cos(angles), jnp.sin(angles))


def rotate(vectors, cosines, sine_part):
    halfway = vectors.shape[-1] // 2
    front = vectors[..., :halfway]
    behind = vectors[..., halfway:]
    return jnp.concatenate(
        [front * cosines - behind * sine_part, behind * cosines + front * sine_part], axis=-1
    )


def contract_last(left, right):
    return lax.dot_general(
        left,
        right,
        (((left.ndim - 1,), (right.ndim - 1,)), ((), ())),
        preferred_element_type=jnp.float32,
    )


def contract_first(left, right):
    return lax.dot_general(
        left, right, (((0,), (0,)), ((), ())), preferred_element_type=jnp.float32
    )


class Grid:
    def __init__(self, dp, fsdp):
        self.dp, self.fsdp = dp, fsdp
        self.depth = fsdp // 2
        self.groups = [[f for f in range(fsdp) if f % 2 == y] for y in range(2)]
        self.dp_index = lax.axis_index("dp")
        self.fsdp_index = lax.axis_index("fsdp")
        self.y = self.fsdp_index % 2

    def core(self, value):
        return lax.ppermute(value, "dp", [(i, i ^ 1) for i in range(self.dp)])

    def x_swap(self, value):
        return lax.ppermute(value, "dp", [(i, i ^ 2) for i in range(self.dp)])

    def y_swap(self, value):
        return lax.ppermute(value, "fsdp", [(i, i ^ 1) for i in range(self.fsdp)])

    def gather_outer(self, value):
        return lax.all_gather(
            value, "fsdp", axis=0, tiled=True, axis_index_groups=self.groups
        )

    def scatter_outer(self, value):
        return lax.psum_scatter(
            value, "fsdp", scatter_dimension=0, tiled=True, axis_index_groups=self.groups
        )

    def spread(self, first, second):
        first_x = self.x_swap(first)
        second_y = self.y_swap(second)
        first_y = self.y_swap(first)
        second_x = self.x_swap(second)
        first_xy = self.y_swap(first_x)
        second_xy = self.x_swap(second_y)
        return {
            (0, 0): (first, second),
            (1, 0): (first_x, second_x),
            (0, 1): (first_y, second_y),
            (1, 1): (first_xy, second_xy),
        }

    def collect(self, parts):
        first_xy = self.y_swap(parts[1, 1][0])
        second_xy = self.x_swap(parts[1, 1][1])
        first_y = self.y_swap(parts[0, 1][0])
        second_x = self.x_swap(parts[1, 0][1])
        wide = lambda *terms: sum(term.astype(f32) for term in terms)
        first_x = self.x_swap(wide(parts[1, 0][0], first_xy).astype(bf16))
        second_y = self.y_swap(wide(parts[0, 1][1], second_xy).astype(bf16))
        return (
            wide(parts[0, 0][0], first_y, first_x),
            wide(parts[0, 0][1], second_x, second_y),
        )

    def assemble(self, shard):
        rows, columns = shard.shape
        column = self.gather_outer(shard).reshape(self.depth, rows, columns)
        cut = self.depth // 2
        pieces = self.spread(column[:cut], column[cut:])
        whole = jnp.zeros((self.dp, self.depth, 2, rows, columns), shard.dtype)
        for flip in range(2):
            for (dx, dy), halves in pieces.items():
                for place, half in ((0, halves[0]), (cut, halves[1])):
                    if flip:
                        half = self.core(half)
                    whole = lax.dynamic_update_slice(
                        whole,
                        half[None, :, None],
                        (self.dp_index ^ (2 * dx + flip), place, self.y ^ dy, 0, 0),
                    )
        return whole.reshape(self.dp * self.depth * 2 * rows, columns)

    def relative_order(self, total):
        rows = total // (self.dp * self.fsdp)
        place = jnp.arange(total, dtype=jnp.int32)
        row = place % rows
        rest = place // rows
        outer = rest % self.depth
        rest = rest // self.depth
        dy, dx, flip = rest % 2, (rest // 2) % 2, rest // 4
        source = (
            ((self.dp_index ^ (2 * dx + flip)) * self.depth + outer) * 2 + (self.y ^ dy)
        ) * rows + row
        return (place[:, None] == source[None, :]).astype(bf16)

    def reduce_rows(self, kept, received, rows):
        columns = kept.shape[1]
        cut = self.depth // 2
        shape = (2, 2, self.depth, rows, columns)
        mine, theirs = kept.reshape(shape), received.reshape(shape)

        def part(dx, dy, low, high):
            both = mine[dx, dy, low:high].astype(f32) + theirs[dx, dy, low:high].astype(f32)
            return both.astype(bf16)

        parts = {
            (dx, dy): (part(dx, dy, 0, cut), part(dx, dy, cut, self.depth))
            for dx in range(2)
            for dy in range(2)
        }
        first, second = self.collect(parts)
        column = jnp.concatenate([first, second], axis=0).astype(bf16)
        return self.scatter_outer(column.reshape(self.depth * rows, columns)).astype(f32)


def local(
    tokens,
    w_q,
    w_kv,
    g_attn,
    g_mlp,
    w_o,
    w_gu,
    w_down,
    grad_out,
    grad_kv,
    group_id,
    group_size,
    group_weight,
):
    grid = Grid(lax.axis_size("dp"), lax.axis_size("fsdp"))
    length, width = tokens.shape
    head_dim = grad_kv.shape[1] // 2
    q_width = w_q.shape[1]
    kv_width = w_kv.shape[1]
    shard_rows = w_q.shape[0]
    head_count = q_width // head_dim
    hidden_rows = w_down.shape[0]
    half = length // 2
    lanes = 128

    gains = jnp.stack([g_attn, g_mlp], axis=1)
    w_in = jnp.concatenate(
        [w_q, w_kv, jnp.pad(gains, ((0, 0), (0, lanes - 2)))], axis=1
    )
    w_in_all = grid.assemble(w_in)
    w_o_all = grid.assemble(w_o)
    gu_mine = grid.gather_outer(w_gu)
    down_mine = grid.gather_outer(w_down)
    gu_other = grid.core(gu_mine)
    down_other = grid.core(down_mine)

    matches = jnp.arange(group_size.shape[0], dtype=jnp.int32) == group_id[0]
    factor = jnp.sum(jnp.where(matches, group_weight / group_size.astype(jnp.float32), 0.0))
    grad_top = grad_out.astype(jnp.float32) * factor
    grad_low = grad_top.astype(jnp.bfloat16)

    def rows_of_plane(value):
        pieces = grid.spread(value[:half], value[half:])
        return jnp.concatenate(
            [piece for key in ((0, 0), (1, 0), (0, 1), (1, 1)) for piece in pieces[key]], axis=0
        )

    def sum_of_plane(partial):
        parts = {}
        for place, key in enumerate(((0, 0), (1, 0), (0, 1), (1, 1))):
            start = place * length
            parts[key] = (partial[start : start + half], partial[start + half : start + length])
        return jnp.concatenate(grid.collect(parts), axis=0)

    grad_rows = rows_of_plane(grad_low)
    order = grid.relative_order(width)
    order_o = order if q_width == width else grid.relative_order(q_width)

    cosines, sine_part = rope_tables(length, head_dim)
    x_full = tokens.astype(jnp.float32)
    inv_one = lax.rsqrt(jnp.mean(x_full * x_full, axis=-1, keepdims=True) + epsilon)
    normed_one = x_full * inv_one
    pick = (jnp.arange(8)[:, None] == jnp.arange(lanes)[None, :]).astype(bf16)
    gain_rows = contract_last(pick, w_in_all[:, q_width + kv_width :])
    gain_one, gain_two = gain_rows[0], gain_rows[1]
    h_one = (normed_one * gain_one).astype(jnp.bfloat16)
    wq_all = w_in_all[:, :q_width]
    wkv_all = w_in_all[:, q_width : q_width + kv_width]
    q_pre = jnp.dot(h_one, wq_all, preferred_element_type=jnp.float32)
    kv_pre = jnp.dot(h_one, wkv_all, preferred_element_type=jnp.float32)
    q_low = rotate(
        q_pre.reshape(length, head_count, head_dim), cosines[:, None, :], sine_part[:, None, :]
    ).astype(jnp.bfloat16)
    k_low = rotate(kv_pre[:, :head_dim], cosines, sine_part).astype(jnp.bfloat16)
    v_low = kv_pre[:, head_dim:].astype(jnp.bfloat16)
    score_scale = head_dim ** (-0.5)
    causal = jnp.arange(length)[:, None] >= jnp.arange(length)[None, :]

    def logits_of(queries, keys):
        raw_scores = jnp.einsum("thd,sd->hts", queries, keys, preferred_element_type=jnp.float32)
        return jnp.where(causal[None], raw_scores * score_scale, -1e30)

    logits = logits_of(q_low, k_low)
    row_top = jnp.max(logits, axis=-1, keepdims=True)
    exp_vals = jnp.exp(logits - row_top)
    row_total = jnp.sum(exp_vals, axis=-1, keepdims=True)
    prob_full = exp_vals / row_total
    log_total = row_top + jnp.log(row_total)
    prob_low = prob_full.astype(jnp.bfloat16)
    attended = jnp.einsum("hts,sd->thd", prob_low, v_low, preferred_element_type=jnp.float32)
    attn_low = attended.reshape(length, q_width).astype(jnp.bfloat16)
    branch = jnp.dot(attn_low, w_o_all, preferred_element_type=jnp.float32)
    x_mid = x_full + branch
    inv_two = lax.rsqrt(jnp.mean(x_mid * x_mid, axis=-1, keepdims=True) + epsilon)
    normed_two = x_mid * inv_two
    h_two = (normed_two * gain_two).astype(jnp.bfloat16)

    ff_rows = rows_of_plane(h_two)
    mlp_out = 0.0
    d_h_two = 0.0
    kept = []
    for gu_piece, down_piece in ((gu_mine, down_mine), (gu_other, down_other)):
        both_proj = jnp.einsum(
            "td,fkd->tkf", ff_rows, gu_piece, preferred_element_type=jnp.float32
        )
        gate_vals = both_proj[:, 0]
        up_vals = both_proj[:, 1]
        hid_cols = (jax.nn.silu(gate_vals) * up_vals).astype(jnp.bfloat16)
        mlp_out = mlp_out + jnp.dot(hid_cols, down_piece, preferred_element_type=jnp.float32)
        d_hid = contract_last(grad_rows, down_piece)
        sigmoid_vals = jax.nn.sigmoid(gate_vals)
        d_gate = d_hid * up_vals * sigmoid_vals * (1.0 + gate_vals * (1.0 - sigmoid_vals))
        d_up = d_hid * gate_vals * sigmoid_vals
        d_both = jnp.stack([d_gate, d_up], axis=1).astype(jnp.bfloat16)
        d_h_two = d_h_two + jnp.einsum(
            "tkf,fkd->td", d_both, gu_piece, preferred_element_type=jnp.float32
        )
        kept.append((hid_cols, d_both[:, 0], d_both[:, 1]))
    d_h_two = sum_of_plane(d_h_two.astype(bf16))
    mlp_out = sum_of_plane(mlp_out.astype(bf16))

    def weight_sum(index, rows):
        theirs = contract_first(kept[1][index], rows).astype(bf16)
        arrived = grid.core(theirs)
        mine = contract_first(kept[0][index], rows)
        return grid.scatter_outer((mine + arrived.astype(f32)).astype(bf16)).astype(f32)

    d_w_down = weight_sum(0, grad_rows)
    d_w_gate = weight_sum(1, ff_rows)
    d_w_up = weight_sum(2, ff_rows)
    d_w_gu = jnp.stack([d_w_gate, d_w_up], axis=1)

    output = (x_mid + mlp_out).astype(jnp.bfloat16)
    d_gain_two = jnp.sum(d_h_two * normed_two, axis=0)
    d_normed_two = d_h_two * gain_two
    d_mid = grad_top + inv_two * (
        d_normed_two - normed_two * jnp.mean(d_normed_two * normed_two, axis=-1, keepdims=True)
    )
    d_mid_low = d_mid.astype(jnp.bfloat16)
    d_attended = contract_last(d_mid_low, w_o_all)
    d_att_low = d_attended.astype(jnp.bfloat16).reshape(length, head_count, head_dim)

    def row_sums(left, right, extra, matrix):
        moved = jnp.dot(left, matrix, preferred_element_type=jnp.float32).astype(bf16)
        middle = left.shape[1] // 2
        halves = []
        for low in (middle, 0):
            block = contract_first(moved[:, low : low + middle], right).astype(bf16)
            if extra is not None:
                columns = contract_first(matrix[:, low : low + middle], extra).astype(bf16)
                block = jnp.concatenate([block, columns], axis=1)
            halves.append(block)
        return grid.reduce_rows(halves[1], grid.core(halves[0]), shard_rows)

    d_w_o = row_sums(attn_low, d_mid_low, None, order_o)
    prob_back = jnp.exp(logits_of(q_low, k_low) - log_total)
    prob_back_low = prob_back.astype(jnp.bfloat16)
    d_probs = jnp.einsum("thd,sd->hts", d_att_low, v_low, preferred_element_type=jnp.float32)
    d_v_own = jnp.einsum(
        "hts,thd->sd", prob_back_low, d_att_low, preferred_element_type=jnp.float32
    )
    d_logit = prob_back * (d_probs - jnp.sum(prob_back * d_probs, axis=-1, keepdims=True))
    d_raw = (d_logit * score_scale).astype(jnp.bfloat16)
    d_q_rot = jnp.einsum("hts,sd->thd", d_raw, k_low, preferred_element_type=jnp.float32)
    d_k_own = jnp.einsum("hts,thd->sd", d_raw, q_low, preferred_element_type=jnp.float32)
    kv_extra = grad_kv.astype(jnp.float32) * factor
    d_k_total = d_k_own + kv_extra[:, :head_dim]
    d_v_total = d_v_own + kv_extra[:, head_dim:]
    d_kv = jnp.concatenate([d_k_total, d_v_total], axis=1)
    d_kv_low = jnp.concatenate([rotate(d_k_total, cosines, -sine_part), d_v_total], axis=1).astype(
        jnp.bfloat16
    )
    d_q_low = (
        rotate(d_q_rot, cosines[:, None, :], -sine_part[:, None, :])
        .reshape(length, q_width)
        .astype(jnp.bfloat16)
    )
    d_h_one = contract_last(d_q_low, wq_all) + contract_last(d_kv_low, wkv_all)
    d_normed = d_h_one * gain_one
    d_gain = jnp.sum(d_h_one * normed_one, axis=0)
    d_tokens = d_mid + inv_one * (
        d_normed - normed_one * jnp.mean(d_normed * normed_one, axis=-1, keepdims=True)
    )
    joined = jnp.concatenate([d_q_low, d_kv_low], axis=1)
    gain_sums = jnp.pad(jnp.stack([d_gain, d_gain_two], axis=1), ((0, 0), (0, lanes - 2)))
    d_w_in = row_sums(h_one, joined, gain_sums.astype(bf16), order)
    kv_out = jnp.concatenate([k_low, v_low], axis=1)
    return (
        output,
        d_tokens,
        kv_out,
        d_kv,
        d_w_in[:, :q_width],
        d_w_in[:, q_width : q_width + kv_width],
        d_w_in[:, q_width + kv_width],
        d_w_in[:, q_width + kv_width + 1],
        d_w_o,
        d_w_gu,
        d_w_down,
    )


def solution(mesh):
    placed = (
        P(("dp", "fsdp"), None),
        P(("dp", "fsdp"), None),
        P(("dp", "fsdp"), None),
        P(("dp", "fsdp")),
        P(("dp", "fsdp")),
        P(("dp", "fsdp"), None),
        P(("dp", "fsdp"), None, None),
        P(("dp", "fsdp"), None),
        P(("dp", "fsdp"), None),
        P(("dp", "fsdp"), None),
        P(("dp", "fsdp")),
        P(),
        P(),
    )
    return jax.shard_map(
        local,
        mesh=mesh,
        in_specs=placed,
        out_specs=(
            P(("dp", "fsdp"), None),
            P(("dp", "fsdp"), None),
            P(("dp", "fsdp"), None),
            P(("dp", "fsdp"), None),
            P(("dp", "fsdp"), None),
            P(("dp", "fsdp"), None),
            P(("dp", "fsdp")),
            P(("dp", "fsdp")),
            P(("dp", "fsdp"), None),
            P(("dp", "fsdp"), None, None),
            P(("dp", "fsdp"), None),
        ),
        check_vma=False,
    )
```

```python
import functools

import jax
import jax.numpy as jnp
from jax import lax
from jax.experimental import pallas as pl
from jax.experimental.pallas import tpu as pltpu
from jax.sharding import PartitionSpec as P

epsilon = 1e-05
theta_base = 10000.0
bf16 = jnp.bfloat16
f32 = jnp.float32
lanes = 128
step = 256
vmem_limit = 60 * 1024 * 1024


def rope_tables(length, width):
    halfway = width // 2
    freqs = theta_base ** (-(jnp.arange(halfway, dtype=jnp.float32) * 2.0 / width))
    angles = jnp.arange(length, dtype=jnp.float32)[:, None] * freqs[None, :]
    cosines, sine_part = jnp.cos(angles), jnp.sin(angles)
    return (
        jnp.concatenate([cosines, cosines], axis=1),
        jnp.concatenate([-sine_part, sine_part], axis=1),
    )


def contract(left, right, left_axis, right_axis):
    return lax.dot_general(
        left, right, (((left_axis,), (right_axis,)), ((), ())), preferred_element_type=jnp.float32
    )


def contract_last(left, right):
    return contract(left, right, left.ndim - 1, right.ndim - 1)


def contract_first(left, right):
    return contract(left, right, 0, 0)


def after(value, token):
    value, _ = lax.optimization_barrier((value, token))
    return value


def vmem_spec():
    return pl.BlockSpec(memory_space=pltpu.VMEM)


def any_spec():
    return pl.BlockSpec(memory_space=pl.ANY)


def smem_spec():
    return pl.BlockSpec(memory_space=pltpu.SMEM)


def kernel_call(body, out_shapes, scratch, in_specs):
    def run(*operands):
        known, late = len(in_specs), len(operands) - len(in_specs)

        def whole_body(*refs):
            body(*refs[:known], *refs[known + late :])

        return pl.pallas_call(
            whole_body,
            out_shape=out_shapes,
            in_specs=in_specs + [any_spec()] * late,
            out_specs=jax.tree.map(lambda _: vmem_spec(), out_shapes),
            scratch_shapes=scratch,
            compiler_params=pltpu.CompilerParams(vmem_limit_bytes=vmem_limit),
            cost_estimate=pl.CostEstimate(flops=1, bytes_accessed=1, transcendentals=0),
        )(*operands)

    return run


class Pieces:
    def __init__(self, depth, rows, columns, arrays):
        self.depth, self.rows, self.columns, self.arrays = depth, rows, columns, arrays

    def start(self, refs, spot, whole, sem):
        cut = self.depth // 2
        place = 0
        for flip in range(2):
            for dx in range(2):
                for dy in range(2):
                    for low, high in ((0, cut), (cut, self.depth)):
                        for outer in range(low, high):
                            block = (
                                (spot[0] ^ (2 * dx + flip)) * self.depth + outer
                            ) * 2 + (spot[1] ^ dy)
                            row = pl.multiple_of(block * self.rows, self.rows)
                            pltpu.make_async_copy(
                                refs[place].at[outer - low], whole.at[pl.ds(row, self.rows)], sem
                            ).start()
                        place += 1

    def wait(self, whole, sem):
        pltpu.make_async_copy(whole, whole, sem).wait()


def swap_halves(value):
    return pltpu.roll(value, value.shape[-1] // 2, 1)


def relative_place(block, spot, depth):
    side = block % 2
    outer = (block // 2) % depth
    flips = (block // (2 * depth)) ^ spot[0]
    return (((flips % 2) * 2 + flips // 2) * 2 + (side ^ spot[1])) * depth + outer


def put_in_order(source, target, spot, depth, rows):
    @pl.loop(0, source.shape[0] // rows)
    def _(block):
        place = pl.multiple_of(relative_place(block, spot, depth) * rows, rows)
        target[pl.ds(place, rows), :] = source[pl.ds(pl.multiple_of(block * rows, rows), rows), :]


def project_body(pieces, q_width, kv_width, head_dim, *refs):
    count = len(pieces.arrays)
    spot, tokens, cosines, sines = refs[:4]
    shards = refs[4 : 4 + count]
    h_turned, q_out, kv_out, gain_out = refs[4 + count : 8 + count]
    whole, h_low, flat, sem = refs[8 + count :]
    pieces.start(shards, spot, whole, sem)
    width = tokens.shape[1]
    x_full = tokens[...].astype(f32)
    inverse = lax.rsqrt(jnp.mean(x_full * x_full, axis=-1, keepdims=True) + epsilon)
    pieces.wait(whole, sem)
    pick = (
        lax.broadcasted_iota(jnp.int32, (8, lanes), 0) == lax.broadcasted_iota(jnp.int32, (8, lanes), 1)
    ).astype(bf16)
    gains = contract_last(pick, whole[:, q_width + kv_width :])
    gain_out[...] = gains
    h_low[...] = (x_full * inverse * gains[0:1]).astype(bf16)
    cos, sin = cosines[...], sines[...]
    kv_pre = jnp.dot(h_low[...], whole[:, q_width : q_width + kv_width], preferred_element_type=f32)
    key_part = kv_pre[:, :head_dim]
    kv_out[:, :head_dim] = (key_part * cos + swap_halves(key_part) * sin).astype(bf16)
    kv_out[:, head_dim:] = kv_pre[:, head_dim:].astype(bf16)

    @pl.loop(0, q_width // step)
    def _(block):
        start = pl.multiple_of(block * step, step)
        q_pre = jnp.dot(h_low[...], whole[:, pl.ds(start, step)], preferred_element_type=f32)
        for head in range(step // head_dim):
            own = q_pre[:, head * head_dim : (head + 1) * head_dim]
            column = pl.multiple_of(start + head * head_dim, head_dim)
            q_out[:, pl.ds(column, head_dim)] = (own * cos + swap_halves(own) * sin).astype(bf16)

    @pl.loop(0, width // step)
    def _(block):
        start = pl.multiple_of(block * step, step)
        flat[pl.ds(start, step), :] = h_low[:, pl.ds(start, step)].T

    put_in_order(flat, h_turned, spot, pieces.depth, pieces.rows)


def project(spot, tokens, cosines, sines, pieces, q_width, kv_width, head_dim, late=()):
    length, width = tokens.shape
    count = len(pieces.arrays)
    shape = jax.ShapeDtypeStruct
    return kernel_call(
        functools.partial(project_body, pieces, q_width, kv_width, head_dim),
        (
            shape((width, length), bf16),
            shape((length, q_width), bf16),
            shape((length, kv_width), bf16),
            shape((8, width), f32),
        ),
        [
            pltpu.VMEM((width, pieces.columns), bf16),
            pltpu.VMEM((length, width), bf16),
            pltpu.VMEM((width, length), bf16),
            pltpu.SemaphoreType.DMA,
        ],
        [smem_spec(), vmem_spec(), vmem_spec(), vmem_spec()] + [any_spec()] * count,
    )(spot, tokens, cosines, sines, *pieces.arrays, *late)


def attend_body(depth, rows, head_dim, spot, q_low, kv_low, prob_out, attended_out, turned, flat):
    length, q_width = q_low.shape
    scale = head_dim ** (-0.5)
    keys = kv_low[:, :head_dim]
    values_turned = kv_low[:, head_dim:].T
    allowed = lax.broadcasted_iota(jnp.int32, (length, length), 0) <= lax.broadcasted_iota(
        jnp.int32, (length, length), 1
    )
    heads = step // head_dim

    @pl.loop(0, q_width // step)
    def _(block):
        for head in range(heads):
            column = pl.multiple_of(block * step + head * head_dim, head_dim)
            queries = q_low[:, pl.ds(column, head_dim)]
            logits = jnp.where(allowed, contract_last(keys, queries) * scale, -1e30)
            exp_vals = jnp.exp(logits - jnp.max(logits, axis=0, keepdims=True))
            prob = (exp_vals / jnp.sum(exp_vals, axis=0, keepdims=True)).astype(bf16)
            prob_out[block * heads + head] = prob
            mixed = jnp.dot(values_turned, prob, preferred_element_type=f32)
            flat[pl.ds(column, head_dim), :] = mixed.astype(bf16)
            attended_out[:, pl.ds(column, head_dim)] = mixed.T.astype(bf16)

    put_in_order(flat, turned, spot, depth, rows)


def attend(spot, q_low, kv_low, depth, rows, late=()):
    length, q_width = q_low.shape
    head_dim = kv_low.shape[1] // 2
    shape = jax.ShapeDtypeStruct
    return kernel_call(
        functools.partial(attend_body, depth, rows, head_dim),
        (
            shape((q_width // head_dim, length, length), bf16),
            shape((length, q_width), bf16),
            shape((q_width, length), bf16),
        ),
        [pltpu.VMEM((q_width, length), bf16)],
        [smem_spec(), vmem_spec(), vmem_spec()],
    )(spot, q_low, kv_low, *late)


def mix_body(pieces, *refs):
    count = len(pieces.arrays)
    spot, tokens, attended, gains = refs[:4]
    shards = refs[4 : 4 + count]
    mid_out, first_out, second_out = refs[4 + count : 7 + count]
    whole, sem = refs[7 + count :]
    pieces.start(shards, spot, whole, sem)
    length, width = tokens.shape
    pieces.wait(whole, sem)

    def add(block, total):
        start = pl.multiple_of(block * step, step)
        branch = jnp.dot(attended[...], whole[:, pl.ds(start, step)], preferred_element_type=f32)
        x_mid = tokens[:, pl.ds(start, step)].astype(f32) + branch
        mid_out[:, pl.ds(start, step)] = x_mid
        return total + jnp.sum(x_mid * x_mid, axis=-1, keepdims=True)

    total = lax.fori_loop(0, width // step, add, jnp.zeros((length, 1), f32))
    inverse = lax.rsqrt(total / width + epsilon)
    h_two = (mid_out[...] * inverse * gains[1:2, :]).astype(bf16)
    first_out[...] = h_two[: length // 2]
    second_out[...] = h_two[length // 2 :]


def mix(spot, tokens, attended, gains, pieces, late=()):
    length, width = tokens.shape
    shape = jax.ShapeDtypeStruct
    half = shape((length // 2, width), bf16)
    rows = attended.shape[1]
    return kernel_call(
        functools.partial(mix_body, pieces),
        (shape((length, width), f32), half, half),
        [pltpu.VMEM((rows, width), bf16), pltpu.SemaphoreType.DMA],
        [smem_spec(), vmem_spec(), vmem_spec(), vmem_spec()] + [any_spec()] * len(pieces.arrays),
    )(spot, tokens, attended, gains, *pieces.arrays, *late)


def norm_back_body(factor, mid, gains, grad_out, *refs):
    sums = refs[:6]
    d_mid_out, d_mid_low, gain_out = refs[6:]
    length = mid.shape[0]
    half = length // 2
    for part in range(2):
        rows = pl.ds(part * half, half)
        terms = sums[3 * part : 3 * part + 3]
        d_h = terms[0][...].astype(f32) + terms[1][...].astype(f32) + terms[2][...].astype(f32)
        x_mid = mid[rows, :]
        inverse = lax.rsqrt(jnp.mean(x_mid * x_mid, axis=-1, keepdims=True) + epsilon)
        normed = x_mid * inverse
        product = d_h * normed
        gain_sum = jnp.broadcast_to(jnp.sum(product, axis=0, keepdims=True), gain_out.shape)
        if part == 0:
            gain_out[...] = gain_sum
        else:
            gain_out[...] += gain_sum
        gain = gains[1:2, :]
        mean = jnp.mean(product * gain, axis=-1, keepdims=True)
        grad_top = grad_out[rows, :].astype(f32) * factor[0]
        d_mid = grad_top + inverse * (d_h * gain - normed * mean)
        d_mid_out[rows, :] = d_mid
        d_mid_low[rows, :] = d_mid.astype(bf16)


def norm_back(factor, mid, gains, grad_out, sums, late=()):
    length, width = mid.shape
    shape = jax.ShapeDtypeStruct
    return kernel_call(
        norm_back_body,
        (shape((length, width), f32), shape((length, width), bf16), shape((8, width), f32)),
        [],
        [smem_spec()] + [vmem_spec()] * 9,
    )(factor, mid, gains, grad_out, *sums, *late)


def attend_back_body(pieces, head_dim, *refs):
    count = len(pieces.arrays)
    (spot, factor, d_mid_low, grad_kv, q_low, kv_low, prob_ref, cosines, sines) = refs[:9]
    shards = refs[9 : 9 + count]
    joined, d_kv_out = refs[9 + count : 11 + count]
    whole, sem = refs[11 + count :]
    pieces.start(shards, spot, whole, sem)
    length = d_mid_low.shape[0]
    q_width = q_low.shape[1]
    scale = head_dim ** (-0.5)
    cos, sin = cosines[...], sines[...]
    keys, values = kv_low[:, :head_dim], kv_low[:, head_dim:]
    d_kv_out[...] = grad_kv[...].astype(f32) * factor[0]
    pieces.wait(whole, sem)
    heads = step // head_dim

    @pl.loop(0, q_width // step)
    def _(block):
        start = pl.multiple_of(block * step, step)
        d_att = contract_last(d_mid_low[...], whole[pl.ds(start, step), :]).astype(bf16)
        d_k = jnp.zeros((length, head_dim), f32)
        d_v = jnp.zeros((length, head_dim), f32)
        for head in range(heads):
            own = d_att[:, head * head_dim : (head + 1) * head_dim]
            column = pl.multiple_of(start + head * head_dim, head_dim)
            low = prob_ref[block * heads + head]
            prob = low.astype(f32)
            d_prob = contract_last(values, own)
            centre = jnp.sum(prob * d_prob, axis=0, keepdims=True)
            d_raw = (prob * (d_prob - centre) * scale).astype(bf16)
            d_v += jnp.dot(low, own, preferred_element_type=f32)
            d_k += jnp.dot(d_raw, q_low[:, pl.ds(column, head_dim)], preferred_element_type=f32)
            d_q = contract_first(d_raw, keys)
            joined[:, pl.ds(column, head_dim)] = (d_q * cos - swap_halves(d_q) * sin).astype(bf16)
        d_kv_out[:, :head_dim] += d_k
        d_kv_out[:, head_dim:] += d_v

    d_k = d_kv_out[:, :head_dim]
    joined[:, q_width : q_width + head_dim] = (d_k * cos - swap_halves(d_k) * sin).astype(bf16)
    joined[:, q_width + head_dim :] = d_kv_out[:, head_dim:].astype(bf16)


def attend_back(spot, factor, d_mid_low, grad_kv, q_low, kv_low, prob, cosines, sines, pieces, late=()):
    length, width = d_mid_low.shape
    q_width, kv_width = q_low.shape[1], kv_low.shape[1]
    head_dim = kv_width // 2
    shape = jax.ShapeDtypeStruct
    return kernel_call(
        functools.partial(attend_back_body, pieces, head_dim),
        (shape((length, q_width + kv_width), bf16), shape((length, kv_width), f32)),
        [pltpu.VMEM((q_width, width), bf16), pltpu.SemaphoreType.DMA],
        [smem_spec()] * 2 + [vmem_spec()] * 7 + [any_spec()] * len(pieces.arrays),
    )(spot, factor, d_mid_low, grad_kv, q_low, kv_low, prob, cosines, sines, *pieces.arrays, *late)


def finish_body(pieces, *refs):
    count = len(pieces.arrays)
    spot, tokens, gains, joined, d_mid = refs[:5]
    shards = refs[5 : 5 + count]
    d_tokens, gain_out = refs[5 + count : 7 + count]
    whole, sem = refs[7 + count :]
    pieces.start(shards, spot, whole, sem)
    length, width = tokens.shape
    used = joined.shape[1]
    x_full = tokens[...].astype(f32)
    inverse = lax.rsqrt(jnp.mean(x_full * x_full, axis=-1, keepdims=True) + epsilon)
    pieces.wait(whole, sem)

    def add(block, total):
        start = pl.multiple_of(block * step, step)
        columns = pl.ds(start, step)
        d_h = contract_last(joined[...], whole[columns, :used])
        normed = tokens[:, columns].astype(f32) * inverse
        gain_out[:, columns] = jnp.broadcast_to(
            jnp.sum(d_h * normed, axis=0, keepdims=True), (8, step)
        )
        d_normed = d_h * gains[0:1, columns]
        d_tokens[:, columns] = d_normed
        return total + jnp.sum(d_normed * normed, axis=-1, keepdims=True)

    total = lax.fori_loop(0, width // step, add, jnp.zeros((length, 1), f32))
    d_tokens[...] = d_mid[...] + inverse * (d_tokens[...] - x_full * inverse * (total / width))


def finish(spot, tokens, gains, joined, d_mid, pieces, late=()):
    length, width = tokens.shape
    shape = jax.ShapeDtypeStruct
    return kernel_call(
        functools.partial(finish_body, pieces),
        (shape((length, width), f32), shape((8, width), f32)),
        [pltpu.VMEM((width, pieces.columns), bf16), pltpu.SemaphoreType.DMA],
        [smem_spec()] + [vmem_spec()] * 4 + [any_spec()] * len(pieces.arrays),
    )(spot, tokens, gains, joined, d_mid, *pieces.arrays, *late)


def fetch_rows(parts, whole, sem):
    start = 0
    for part in parts:
        pltpu.make_async_copy(part, whole.at[pl.ds(start, part.shape[0])], sem).start()
        start += part.shape[0]
    return pltpu.make_async_copy(whole, whole, sem).wait


def fetch_gate_up(both, shard, first, second, first_sem, second_sem):
    waits = []
    for place, (whole, sem) in enumerate(((first, first_sem), (second, second_sem))):
        for outer in range(both.shape[0] // (2 * shard)):
            source = both.at[pl.ds((2 * outer + place) * shard, shard)]
            pltpu.make_async_copy(source, whole.at[pl.ds(outer * shard, shard)], sem).start()
        waits.append(pltpu.make_async_copy(whole, whole, sem).wait)
    return waits


def gate_body(shard, count, *refs):
    parts, both = refs[:count], refs[count]
    hid, by_gate, by_up = refs[count + 1 : count + 4]
    rows, gate_w, up_w, row_sem, gate_sem, up_sem = refs[count + 4 :]
    waits = fetch_gate_up(both, shard, gate_w, up_w, gate_sem, up_sem)
    waits.append(fetch_rows(parts, rows, row_sem))
    for wait in waits:
        wait()

    @pl.loop(0, rows.shape[0] // step)
    def _(block):
        own = pl.ds(pl.multiple_of(block * step, step), step)
        gate = contract_last(rows[own, :], gate_w[...])
        up = contract_last(rows[own, :], up_w[...])
        sigma = 1.0 / (1.0 + jnp.exp(-gate))
        silu = gate * sigma
        hid[own, :] = (silu * up).astype(bf16)
        by_gate[own, :] = (up * sigma * (1.0 + gate * (1.0 - sigma))).astype(bf16)
        by_up[own, :] = silu.astype(bf16)


def gate(parts, both, shard, late=()):
    total, width = sum(part.shape[0] for part in parts), parts[0].shape[1]
    hidden = both.shape[0] // 2
    out = jax.ShapeDtypeStruct((total, hidden), bf16)
    return kernel_call(
        functools.partial(gate_body, shard, len(parts)),
        (out, out, out),
        [pltpu.VMEM((total, width), bf16)]
        + [pltpu.VMEM((hidden, width), bf16)] * 2
        + [pltpu.SemaphoreType.DMA] * 3,
        [any_spec()] * (len(parts) + 1),
    )(*parts, both, *late)


def d_hidden(rows, weight, scales, grads):
    @pl.loop(0, rows.shape[0] // step)
    def _(block):
        own = pl.ds(pl.multiple_of(block * step, step), step)
        d_hid = contract_last(rows[own, :], weight[...])
        for scale, grad in zip(scales, grads):
            grad[own, :] = (d_hid * scale[own, :].astype(f32)).astype(bf16)


def gate_back_body(count, *refs):
    parts, weight, scales, grads = refs[:count], refs[count], refs[count + 1 : count + 3], refs[count + 3 : count + 5]
    rows, sem = refs[count + 5 :]
    fetch_rows(parts, rows, sem)()
    d_hidden(rows, weight, scales, grads)


def gate_back(parts, weight, scales, late=()):
    count = len(parts)
    total, width = sum(part.shape[0] for part in parts), parts[0].shape[1]
    grad = jax.ShapeDtypeStruct((total, weight.shape[0]), bf16)
    return kernel_call(
        functools.partial(gate_back_body, count),
        (grad, grad),
        [pltpu.VMEM((total, width), bf16), pltpu.SemaphoreType.DMA],
        [any_spec()] * count + [vmem_spec()] * 3,
    )(*parts, weight, *scales, *late)


def rows_back_body(shard, count, *refs):
    parts, weight, scales, others, boths = (
        refs[:count], refs[count], refs[count + 1 : count + 3], refs[count + 3 : count + 5],
        refs[count + 5 : count + 7],
    )
    refs = refs[count + 7 :]
    grads, outs = refs[:2], refs[2 : 2 + count]
    rows, weights, sems = refs[2 + count], refs[3 + count : 7 + count], refs[7 + count]
    row_wait = fetch_rows(parts, rows, sems.at[0])
    waits = []
    for place in range(2):
        waits += fetch_gate_up(
            boths[place], shard, weights[2 * place], weights[2 * place + 1],
            sems.at[1 + 2 * place], sems.at[2 + 2 * place],
        )
    row_wait()
    d_hidden(rows, weight, scales, grads)
    for wait in waits:
        wait()
    size = outs[0].shape[0]
    for place, out in enumerate(outs):
        own = pl.ds(place * size, size)
        total = jnp.dot(grads[0][own, :], weights[0][...], preferred_element_type=f32)
        for grad, piece in zip((grads[1], *others), weights[1:]):
            total += jnp.dot(grad[own, :], piece[...], preferred_element_type=f32)
        out[...] = total.astype(bf16)


def rows_back(parts, weight, scales, others, boths, shard, late=()):
    count = len(parts)
    total, width = sum(part.shape[0] for part in parts), parts[0].shape[1]
    hidden = weight.shape[0]
    shape = jax.ShapeDtypeStruct
    outs = kernel_call(
        functools.partial(rows_back_body, shard, count),
        (shape((total, hidden), bf16),) * 2 + tuple(shape(part.shape, bf16) for part in parts),
        [pltpu.VMEM((total, width), bf16)]
        + [pltpu.VMEM((hidden, width), bf16)] * 4
        + [pltpu.SemaphoreType.DMA((5,))],
        [any_spec()] * count + [vmem_spec()] * 5 + [any_spec()] * 2,
    )(*parts, weight, *scales, *others, *boths, *late)
    return outs[:2], outs[2:]


def down_body(count, *refs):
    hids, downs, outs = refs[:2], refs[2:4], refs[4:]
    size = outs[0].shape[0]
    for place, out in enumerate(outs):
        own = pl.ds(place * size, size)
        total = jnp.dot(hids[0][own, :], downs[0][...], preferred_element_type=f32)
        total += jnp.dot(hids[1][own, :], downs[1][...], preferred_element_type=f32)
        out[...] = total.astype(bf16)


def down(hids, downs, count, late=()):
    total, width = hids[0].shape[0], downs[0].shape[1]
    return kernel_call(
        functools.partial(down_body, count),
        (jax.ShapeDtypeStruct((total // count, width), bf16),) * count,
        [],
        [vmem_spec()] * 4,
    )(*hids, *downs, *late)


def hidden_sums_body(count, pairs, shard, received, *refs):
    lefts, parts = refs[:pairs], refs[pairs : pairs + count]
    other = refs[pairs + count] if received else None
    out, rows, sem = refs[-3], refs[-2], refs[-1]
    fetch_rows(parts, rows, sem)()
    for place, left in enumerate(lefts):
        product = contract_first(left[...], rows[...])
        for outer in range(left.shape[1] // shard):
            target = pl.ds((pairs * outer + place) * shard, shard)
            own = product[outer * shard : (outer + 1) * shard]
            if received:
                own = own + other[target, :].astype(f32)
            out[target, :] = own.astype(bf16)


def hidden_sums(lefts, parts, shard, other=None, late=()):
    total, width = lefts[0].shape[0], parts[0].shape[1]
    hidden = lefts[0].shape[1] * len(lefts)
    received = other is not None
    return kernel_call(
        functools.partial(hidden_sums_body, len(parts), len(lefts), shard, received),
        jax.ShapeDtypeStruct((hidden, width), bf16),
        [pltpu.VMEM((total, width), bf16), pltpu.SemaphoreType.DMA],
        [vmem_spec()] * len(lefts) + [any_spec()] * len(parts) + [vmem_spec()] * received,
    )(*lefts, *parts, *((other,) if received else ()), *late)


def send_sums_body(turned, right, out):
    middle = turned.shape[0] // 2

    @pl.loop(0, middle // step)
    def _(block):
        start = pl.multiple_of(block * step, step)
        product = jnp.dot(turned[pl.ds(middle + start, step), :], right[...], preferred_element_type=f32)
        out[pl.ds(start, step), :] = product.astype(bf16)


def send_sums(turned, right, late=()):
    return kernel_call(
        send_sums_body,
        jax.ShapeDtypeStruct((turned.shape[0] // 2, right.shape[1]), bf16),
        [],
        [vmem_spec()] * 2,
    )(turned, right, *late)


def keep_sums_body(turned, right, other, *outs):
    size = outs[0].shape[0]
    for place, out in enumerate(outs):
        own = pl.ds(place * size, size)
        product = jnp.dot(turned[own, :], right[...], preferred_element_type=f32)
        out[...] = (product + other[own, :].astype(f32)).astype(bf16)


def keep_sums(turned, right, other, late=()):
    size = turned.shape[0] // 16
    outs = kernel_call(
        keep_sums_body,
        (jax.ShapeDtypeStruct((size, right.shape[1]), bf16),) * 8,
        [],
        [vmem_spec()] * 3,
    )(turned, right, other, *late)
    return {
        (dx, dy): (outs[4 * dx + 2 * dy], outs[4 * dx + 2 * dy + 1])
        for dx in range(2)
        for dy in range(2)
    }


def pass_body(a, b, c, d, first, second):
    first[...] = (a[...].astype(f32) + b[...].astype(f32)).astype(bf16)
    second[...] = (c[...].astype(f32) + d[...].astype(f32)).astype(bf16)


def add_pairs(a, b, c, d, late=()):
    shape = jax.ShapeDtypeStruct
    return kernel_call(
        pass_body, (shape(a.shape, bf16), shape(c.shape, bf16)), [], [vmem_spec()] * 4
    )(a, b, c, d, *late)


class Grid:
    def __init__(self, dp, fsdp):
        self.dp, self.fsdp = dp, fsdp
        self.depth = fsdp // 2
        self.groups = [[f for f in range(fsdp) if f % 2 == y] for y in range(2)]
        self.dp_index = lax.axis_index("dp")
        self.y = lax.axis_index("fsdp") % 2
        self.spot = jnp.stack([self.dp_index, self.y]).astype(jnp.int32)
        self.outer = lax.axis_index("fsdp") // 2

    def core(self, value):
        return lax.ppermute(value, "dp", [(i, i ^ 1) for i in range(self.dp)])

    def echo(self, value, times):
        corner = value[:8, :lanes]
        for _ in range(times):
            corner = self.core(corner)
        return corner

    def x_swap(self, value):
        return lax.ppermute(value, "dp", [(i, i ^ 2) for i in range(self.dp)])

    def y_swap(self, value):
        return lax.ppermute(value, "fsdp", [(i, i ^ 1) for i in range(self.fsdp)])

    def shift(self, value, low, high, by):
        pairs = [
            (2 * outer + y, 2 * (outer + by) + y) for outer in range(low, high) for y in range(2)
        ]
        return lax.ppermute(value, "fsdp", pairs)

    def gather_outer(self, value):
        return lax.all_gather(value, "fsdp", axis=0, tiled=True, axis_index_groups=self.groups)

    def scatter_outer(self, value):
        return lax.psum_scatter(
            value, "fsdp", scatter_dimension=0, tiled=True, axis_index_groups=self.groups
        )

    def spread_first(self, first, second):
        return first, second, self.x_swap(first), self.y_swap(second)

    def spread_second(self, first, second, first_x, second_y):
        first, second, first_x, second_y = lax.optimization_barrier(
            (first, second, first_x, second_y)
        )
        first_xy = self.y_swap(first_x)
        second_xy = self.x_swap(second_y)
        first_y = self.y_swap(first)
        second_x = self.x_swap(second)
        return {
            (0, 0): (first, second),
            (1, 0): (first_x, second_x),
            (0, 1): (first_y, second_y),
            (1, 1): (first_xy, second_xy),
        }

    def collect_first(self, parts, late=()):
        first_xy = self.y_swap(parts[1, 1][0])
        second_xy = self.x_swap(parts[1, 1][1])
        first_y = self.y_swap(parts[0, 1][0])
        second_x = self.x_swap(parts[1, 0][1])
        for_x, for_y = add_pairs(parts[1, 0][0], first_xy, parts[0, 1][1], second_xy, late)
        return for_x, for_y, first_y, second_x

    def collect_second(self, parts, passed):
        for_x, for_y, first_y, second_x = passed
        return (
            (parts[0, 0][0], first_y, self.x_swap(for_x)),
            (parts[0, 0][1], second_x, self.y_swap(for_y)),
        )

    def pieces(self, planes, rows, token=None):
        keys = [(dx, dy) for dx in range(2) for dy in range(2)]
        mine = [half for key in keys for half in planes[key]]
        sent = mine if token is None else after(mine, token)
        theirs = [self.core(half) for half in sent]
        return Pieces(self.depth, rows, mine[0].shape[-1], mine + theirs)

    def column(self, sums):
        halves = [sum(term.astype(f32) for term in terms) for terms in sums]
        column = jnp.concatenate(halves, axis=0).astype(bf16)
        return column.reshape(-1, column.shape[-1])


def local(
    tokens,
    w_q,
    w_kv,
    g_attn,
    g_mlp,
    w_o,
    w_gu,
    w_down,
    grad_out,
    grad_kv,
    group_id,
    group_size,
    group_weight,
):
    grid = Grid(lax.axis_size("dp"), lax.axis_size("fsdp"))
    length, width = tokens.shape
    kv_width = w_kv.shape[1]
    head_dim = kv_width // 2
    q_width = w_q.shape[1]
    shard_rows = w_q.shape[0]
    hidden_rows = w_down.shape[0]
    half = length // 2

    matches = jnp.arange(group_size.shape[0], dtype=jnp.int32) == group_id[0]
    factor = jnp.sum(jnp.where(matches, group_weight / group_size.astype(jnp.float32), 0.0))
    grad_low = (grad_out.astype(jnp.float32) * factor).astype(jnp.bfloat16)
    cosines, sines = rope_tables(length, head_dim)

    plane_keys = ((0, 0), (1, 0), (0, 1), (1, 1))

    def in_order(planes):
        return [piece for key in plane_keys for piece in planes[key]]

    def by_key(blocks):
        return {key: (blocks[2 * i], blocks[2 * i + 1]) for i, key in enumerate(plane_keys)}

    gains = jnp.stack([g_attn, g_mlp], axis=1)
    w_in = jnp.concatenate([w_q, w_kv, jnp.pad(gains, ((0, 0), (0, lanes - 2)))], axis=1)
    w_in_column = grid.gather_outer(w_in)
    w_o_column = grid.gather_outer(after(w_o, w_in))
    grad_first = grid.spread_first(grad_low[:half], grad_low[half:])
    pairs = jnp.swapaxes(w_gu, 0, 1).reshape(2 * hidden_rows, width)
    gu_mine = grid.gather_outer(after(pairs, grad_first[2:]))
    grad_planes = grid.spread_second(*grad_first)
    grad_rows = in_order(grad_planes)
    cut = grid.depth // 2
    w_in_column = after(w_in_column, grad_planes[1, 1]).reshape(grid.depth, shard_rows, -1)
    in_planes = grid.spread_second(*grid.spread_first(w_in_column[:cut], w_in_column[cut:]))
    in_pieces = grid.pieces(in_planes, shard_rows)
    down_mine = grid.gather_outer(after(w_down, in_planes[1, 1]))
    w_o_column = after(w_o_column, in_planes[1, 1]).reshape(grid.depth, shard_rows, -1)
    o_first = grid.spread_first(w_o_column[:cut], w_o_column[cut:])
    h_turned, q_low, kv_out, gain_rows = project(
        grid.spot, tokens, cosines, sines, in_pieces, q_width, kv_width, head_dim
    )
    o_planes = grid.spread_second(*after(o_first, q_low))
    prob, attended, turned = attend(grid.spot, q_low, kv_out, grid.depth, shard_rows)
    o_pieces = grid.pieces(o_planes, shard_rows, attended)
    x_mid, h_first, h_second = mix(grid.spot, tokens, attended, gain_rows, o_pieces)

    ff_rows = in_order(grid.spread_second(*grid.spread_first(h_first, h_second)))
    gu_mine = after(gu_mine, ff_rows)
    by_shard = hidden_rows % 8 == 0
    run_rows = hidden_rows if by_shard else grid.depth * hidden_rows

    def turn(both, rows):
        return both.reshape(-1, rows, hidden_rows, width).swapaxes(0, 1).reshape(both.shape)

    if not by_shard:
        gu_mine = turn(gu_mine, 2)
    gu_other = grid.core(gu_mine)
    hid_mine, *scales_mine = gate(ff_rows, gu_mine, run_rows)
    hid_other, *scales_other = gate(ff_rows, gu_other, run_rows, [hid_mine])
    sent = hidden_sums([hid_other], grad_rows, run_rows, late=[down_mine])
    down_sum = hidden_sums([hid_mine], grad_rows, run_rows, grid.core(sent), [sent])
    d_w_down = grid.scatter_outer(down_sum).astype(f32)
    down_other = grid.core(down_mine)
    pair_other = gate_back(grad_rows, down_other, scales_other, [down_sum])
    sent = hidden_sums(pair_other, ff_rows, run_rows)
    pair_mine, d_h_blocks = rows_back(
        grad_rows, down_mine, scales_mine, pair_other, (gu_mine, gu_other), run_rows, [sent]
    )
    d_h_parts = by_key(d_h_blocks)
    pair_sum = hidden_sums(pair_mine, ff_rows, run_rows, grid.core(sent))
    d_w_gu = grid.scatter_outer(pair_sum if by_shard else turn(pair_sum, grid.depth)).astype(f32)
    d_h_passed = grid.collect_first(d_h_parts, [pair_sum, grid.echo(d_w_down, 2)])
    d_h_first, d_h_second = grid.collect_second(d_h_parts, d_h_passed)
    d_h_sums = [*d_h_first, *d_h_second]

    d_mid, d_mid_low, gain_two_sum = norm_back(
        factor.reshape(1), x_mid, gain_rows, grad_out, d_h_sums
    )
    sent = send_sums(turned, d_mid_low)
    o_parts = keep_sums(turned, d_mid_low, grid.core(sent))
    joined, d_kv = attend_back(
        grid.spot, factor.reshape(1), d_mid_low, grad_kv, q_low, kv_out,
        prob, cosines, sines, o_pieces, [o_parts[0, 0][0]],
    )
    o_passed = grid.collect_first(o_parts, [joined])
    sent = send_sums(h_turned, joined)
    d_w_o = grid.scatter_outer(grid.column(grid.collect_second(o_parts, o_passed))).astype(f32)
    d_tokens, gain_one_sum = finish(grid.spot, tokens, gain_rows, joined, d_mid, in_pieces, [sent])
    in_parts = keep_sums(
        h_turned, joined, grid.core(sent), [o_passed[0], gain_one_sum, grid.echo(d_w_gu, 2)]
    )
    in_passed = grid.collect_first(in_parts)
    d_w_in = grid.column(grid.collect_second(in_parts, in_passed))
    d_w_gu = jnp.stack([d_w_gu[:hidden_rows], d_w_gu[hidden_rows:]], axis=1)
    mlp_parts = by_key(
        down((hid_mine, hid_other), (down_mine, down_other), len(ff_rows), [in_passed[0]])
    )
    mlp_sum = grid.collect_second(mlp_parts, grid.collect_first(mlp_parts))
    mlp_sum = jnp.concatenate([sum(term.astype(f32) for term in terms) for terms in mlp_sum], axis=0)
    output = (x_mid + mlp_sum).astype(jnp.bfloat16)
    gain_sums = jnp.stack([gain_one_sum[0], gain_two_sum[0]], axis=0)
    for swap in (grid.core, grid.x_swap, grid.y_swap):
        gain_sums = gain_sums + swap(gain_sums)
    own_gains = lax.dynamic_slice(
        gain_sums.reshape(2, grid.dp, grid.depth, 2, shard_rows),
        (0, grid.dp_index, 0, grid.y, 0),
        (2, 1, grid.depth, 1, shard_rows),
    ).reshape(2, grid.depth * shard_rows)
    extra = jnp.pad(own_gains.T, ((0, 0), (0, lanes - 2))).astype(bf16)
    d_w_in = grid.scatter_outer(jnp.concatenate([d_w_in, extra], axis=1)).astype(f32)
    return (
        output,
        d_tokens,
        kv_out,
        d_kv,
        d_w_in[:, :q_width],
        d_w_in[:, q_width : q_width + kv_width],
        d_w_in[:, q_width + kv_width],
        d_w_in[:, q_width + kv_width + 1],
        d_w_o,
        d_w_gu,
        d_w_down,
    )


def solution(mesh):
    placed = (
        P(("dp", "fsdp"), None),
        P(("dp", "fsdp"), None),
        P(("dp", "fsdp"), None),
        P(("dp", "fsdp")),
        P(("dp", "fsdp")),
        P(("dp", "fsdp"), None),
        P(("dp", "fsdp"), None, None),
        P(("dp", "fsdp"), None),
        P(("dp", "fsdp"), None),
        P(("dp", "fsdp"), None),
        P(("dp", "fsdp")),
        P(),
        P(),
    )
    return jax.shard_map(
        local,
        mesh=mesh,
        in_specs=placed,
        out_specs=(
            P(("dp", "fsdp"), None),
            P(("dp", "fsdp"), None),
            P(("dp", "fsdp"), None),
            P(("dp", "fsdp"), None),
            P(("dp", "fsdp"), None),
            P(("dp", "fsdp"), None),
            P(("dp", "fsdp")),
            P(("dp", "fsdp")),
            P(("dp", "fsdp"), None),
            P(("dp", "fsdp"), None, None),
            P(("dp", "fsdp"), None),
        ),
        check_vma=False,
    )
```

```python
import functools

import jax
import jax.numpy as jnp
from jax import lax
from jax.experimental import pallas as pl
from jax.experimental.pallas import tpu as pltpu
from jax.sharding import PartitionSpec as P

epsilon = 1e-05
theta_base = 10000.0
bf16 = jnp.bfloat16
f32 = jnp.float32
lanes = 128
step = 256
vmem_limit = 60 * 1024 * 1024


def rope_tables(length, width):
    halfway = width // 2
    freqs = theta_base ** (-(jnp.arange(halfway, dtype=jnp.float32) * 2.0 / width))
    angles = jnp.arange(length, dtype=jnp.float32)[:, None] * freqs[None, :]
    cosines, sine_part = jnp.cos(angles), jnp.sin(angles)
    return (
        jnp.concatenate([cosines, cosines], axis=1),
        jnp.concatenate([-sine_part, sine_part], axis=1),
    )


def contract(left, right, left_axis, right_axis):
    return lax.dot_general(
        left, right, (((left_axis,), (right_axis,)), ((), ())), preferred_element_type=jnp.float32
    )


def contract_last(left, right):
    return contract(left, right, left.ndim - 1, right.ndim - 1)


def contract_first(left, right):
    return contract(left, right, 0, 0)


def after(value, token):
    value, _ = lax.optimization_barrier((value, token))
    return value


def vmem_spec():
    return pl.BlockSpec(memory_space=pltpu.VMEM)


def any_spec():
    return pl.BlockSpec(memory_space=pl.ANY)


def smem_spec():
    return pl.BlockSpec(memory_space=pltpu.SMEM)


def kernel_call(body, out_shapes, scratch, in_specs):
    def run(*operands):
        known, late = len(in_specs), len(operands) - len(in_specs)

        def whole_body(*refs):
            body(*refs[:known], *refs[known + late :])

        return pl.pallas_call(
            whole_body,
            out_shape=out_shapes,
            in_specs=in_specs + [any_spec()] * late,
            out_specs=jax.tree.map(lambda _: vmem_spec(), out_shapes),
            scratch_shapes=scratch,
            compiler_params=pltpu.CompilerParams(vmem_limit_bytes=vmem_limit),
            cost_estimate=pl.CostEstimate(flops=1, bytes_accessed=1, transcendentals=0),
            name=getattr(body, "func", body).__name__[: -len("_body")],
        )(*operands)

    return run


def route(keys):
    place = {(key, half): 2 * i + half for i, key in enumerate(keys) for half in range(2)}
    own, x, y, both = (0, 0), (1, 0), (0, 1), (1, 1)
    return (
        (place[own, 0],),
        (place[own, 1],),
        (place[x, 0],),
        (place[y, 1],),
        (place[both, 1], place[x, 1]),
        (place[both, 0], place[y, 0]),
    )


row_route = route(((0, 0), (1, 0), (0, 1), (1, 1)))
column_route = route(((0, 0), (0, 1), (1, 0), (1, 1)))


def routed(size, columns):
    return tuple(
        jax.ShapeDtypeStruct((size * len(blocks), columns), bf16) for blocks in row_route
    )


def store_routed(way, outs, size, block):
    for blocks, out in zip(way, outs):
        for spot, place in enumerate(blocks):
            out[spot * size : (spot + 1) * size, :] = block(place).astype(bf16)


class Pieces:
    def __init__(self, depth, rows, columns, arrays):
        self.depth, self.rows, self.columns, self.arrays = depth, rows, columns, arrays

    def start(self, refs, spot, whole, sem):
        cut = self.depth // 2
        place = 0
        for flip in range(2):
            for dx in range(2):
                for dy in range(2):
                    for low, high in ((0, cut), (cut, self.depth)):
                        for outer in range(low, high):
                            block = (
                                (spot[0] ^ (2 * dx + flip)) * self.depth + outer
                            ) * 2 + (spot[1] ^ dy)
                            row = pl.multiple_of(block * self.rows, self.rows)
                            pltpu.make_async_copy(
                                refs[place].at[outer - low], whole.at[pl.ds(row, self.rows)], sem
                            ).start()
                        place += 1

    def wait(self, whole, sem):
        pltpu.make_async_copy(whole, whole, sem).wait()


def swap_halves(value):
    return pltpu.roll(value, value.shape[-1] // 2, 1)


def relative_place(block, spot, depth):
    side = block % 2
    outer = (block // 2) % depth
    flips = (block // (2 * depth)) ^ spot[0]
    return (((flips % 2) * 2 + flips // 2) * 2 + (side ^ spot[1])) * depth + outer


def put_in_order(source, target, spot, depth, rows):
    @pl.loop(0, source.shape[0] // rows)
    def _(block):
        place = pl.multiple_of(relative_place(block, spot, depth) * rows, rows)
        target[pl.ds(place, rows), :] = source[pl.ds(pl.multiple_of(block * rows, rows), rows), :]


def project_body(pieces, q_width, kv_width, head_dim, *refs):
    count = len(pieces.arrays)
    spot, tokens, cosines, sines = refs[:4]
    shards = refs[4 : 4 + count]
    h_turned, q_out, kv_out, gain_out = refs[4 + count : 8 + count]
    whole, h_low, flat, sem = refs[8 + count :]
    pieces.start(shards, spot, whole, sem)
    width = tokens.shape[1]
    x_full = tokens[...].astype(f32)
    inverse = lax.rsqrt(jnp.mean(x_full * x_full, axis=-1, keepdims=True) + epsilon)
    pieces.wait(whole, sem)
    pick = (
        lax.broadcasted_iota(jnp.int32, (8, lanes), 0) == lax.broadcasted_iota(jnp.int32, (8, lanes), 1)
    ).astype(bf16)
    gains = contract_last(pick, whole[:, q_width + kv_width :])
    gain_out[...] = gains
    h_low[...] = (x_full * inverse * gains[0:1]).astype(bf16)
    cos, sin = cosines[...], sines[...]
    kv_pre = jnp.dot(h_low[...], whole[:, q_width : q_width + kv_width], preferred_element_type=f32)
    key_part = kv_pre[:, :head_dim]
    kv_out[:, :head_dim] = (key_part * cos + swap_halves(key_part) * sin).astype(bf16)
    kv_out[:, head_dim:] = kv_pre[:, head_dim:].astype(bf16)

    @pl.loop(0, q_width // step)
    def _(block):
        start = pl.multiple_of(block * step, step)
        q_pre = jnp.dot(h_low[...], whole[:, pl.ds(start, step)], preferred_element_type=f32)
        for head in range(step // head_dim):
            own = q_pre[:, head * head_dim : (head + 1) * head_dim]
            column = pl.multiple_of(start + head * head_dim, head_dim)
            q_out[:, pl.ds(column, head_dim)] = (own * cos + swap_halves(own) * sin).astype(bf16)

    @pl.loop(0, width // step)
    def _(block):
        start = pl.multiple_of(block * step, step)
        flat[pl.ds(start, step), :] = h_low[:, pl.ds(start, step)].T

    put_in_order(flat, h_turned, spot, pieces.depth, pieces.rows)


def project(spot, tokens, cosines, sines, pieces, q_width, kv_width, head_dim, late=()):
    length, width = tokens.shape
    count = len(pieces.arrays)
    shape = jax.ShapeDtypeStruct
    return kernel_call(
        functools.partial(project_body, pieces, q_width, kv_width, head_dim),
        (
            shape((width, length), bf16),
            shape((length, q_width), bf16),
            shape((length, kv_width), bf16),
            shape((8, width), f32),
        ),
        [
            pltpu.VMEM((width, pieces.columns), bf16),
            pltpu.VMEM((length, width), bf16),
            pltpu.VMEM((width, length), bf16),
            pltpu.SemaphoreType.DMA,
        ],
        [smem_spec(), vmem_spec(), vmem_spec(), vmem_spec()] + [any_spec()] * count,
    )(spot, tokens, cosines, sines, *pieces.arrays, *late)


def attend_body(depth, rows, head_dim, spot, q_low, kv_low, prob_out, attended_out, turned, flat):
    length, q_width = q_low.shape
    scale = head_dim ** (-0.5)
    keys = kv_low[:, :head_dim]
    values_turned = kv_low[:, head_dim:].T
    allowed = lax.broadcasted_iota(jnp.int32, (length, length), 0) <= lax.broadcasted_iota(
        jnp.int32, (length, length), 1
    )
    heads = step // head_dim

    @pl.loop(0, q_width // step)
    def _(block):
        for head in range(heads):
            column = pl.multiple_of(block * step + head * head_dim, head_dim)
            queries = q_low[:, pl.ds(column, head_dim)]
            logits = jnp.where(allowed, contract_last(keys, queries) * scale, -1e30)
            exp_vals = jnp.exp(logits - jnp.max(logits, axis=0, keepdims=True))
            prob = (exp_vals / jnp.sum(exp_vals, axis=0, keepdims=True)).astype(bf16)
            prob_out[block * heads + head] = prob
            mixed = jnp.dot(values_turned, prob, preferred_element_type=f32)
            flat[pl.ds(column, head_dim), :] = mixed.astype(bf16)
            attended_out[:, pl.ds(column, head_dim)] = mixed.T.astype(bf16)

    put_in_order(flat, turned, spot, depth, rows)


def attend(spot, q_low, kv_low, depth, rows, late=()):
    length, q_width = q_low.shape
    head_dim = kv_low.shape[1] // 2
    shape = jax.ShapeDtypeStruct
    return kernel_call(
        functools.partial(attend_body, depth, rows, head_dim),
        (
            shape((q_width // head_dim, length, length), bf16),
            shape((length, q_width), bf16),
            shape((q_width, length), bf16),
        ),
        [pltpu.VMEM((q_width, length), bf16)],
        [smem_spec(), vmem_spec(), vmem_spec()],
    )(spot, q_low, kv_low, *late)


def mix_body(pieces, *refs):
    count = len(pieces.arrays)
    spot, tokens, attended, gains = refs[:4]
    shards = refs[4 : 4 + count]
    mid_out, first_out, second_out = refs[4 + count : 7 + count]
    whole, sem = refs[7 + count :]
    pieces.start(shards, spot, whole, sem)
    length, width = tokens.shape
    pieces.wait(whole, sem)

    def add(block, total):
        start = pl.multiple_of(block * step, step)
        branch = jnp.dot(attended[...], whole[:, pl.ds(start, step)], preferred_element_type=f32)
        x_mid = tokens[:, pl.ds(start, step)].astype(f32) + branch
        mid_out[:, pl.ds(start, step)] = x_mid
        return total + jnp.sum(x_mid * x_mid, axis=-1, keepdims=True)

    total = lax.fori_loop(0, width // step, add, jnp.zeros((length, 1), f32))
    inverse = lax.rsqrt(total / width + epsilon)
    h_two = (mid_out[...] * inverse * gains[1:2, :]).astype(bf16)
    first_out[...] = h_two[: length // 2]
    second_out[...] = h_two[length // 2 :]


def mix(spot, tokens, attended, gains, pieces, late=()):
    length, width = tokens.shape
    shape = jax.ShapeDtypeStruct
    half = shape((length // 2, width), bf16)
    rows = attended.shape[1]
    return kernel_call(
        functools.partial(mix_body, pieces),
        (shape((length, width), f32), half, half),
        [pltpu.VMEM((rows, width), bf16), pltpu.SemaphoreType.DMA],
        [smem_spec(), vmem_spec(), vmem_spec(), vmem_spec()] + [any_spec()] * len(pieces.arrays),
    )(spot, tokens, attended, gains, *pieces.arrays, *late)


def norm_back_body(factor, mid, gains, grad_out, *refs):
    sums = refs[:6]
    d_mid_out, d_mid_low, gain_out = refs[6:]
    length = mid.shape[0]
    half = length // 2
    for part in range(2):
        rows = pl.ds(part * half, half)
        terms = sums[3 * part : 3 * part + 3]
        d_h = terms[0][...].astype(f32) + terms[1][half:, :].astype(f32) + terms[2][...].astype(f32)
        x_mid = mid[rows, :]
        inverse = lax.rsqrt(jnp.mean(x_mid * x_mid, axis=-1, keepdims=True) + epsilon)
        normed = x_mid * inverse
        product = d_h * normed
        gain_sum = jnp.broadcast_to(jnp.sum(product, axis=0, keepdims=True), gain_out.shape)
        if part == 0:
            gain_out[...] = gain_sum
        else:
            gain_out[...] += gain_sum
        gain = gains[1:2, :]
        mean = jnp.mean(product * gain, axis=-1, keepdims=True)
        grad_top = grad_out[rows, :].astype(f32) * factor[0]
        d_mid = grad_top + inverse * (d_h * gain - normed * mean)
        d_mid_out[rows, :] = d_mid
        d_mid_low[rows, :] = d_mid.astype(bf16)


def norm_back(factor, mid, gains, grad_out, sums, late=()):
    length, width = mid.shape
    shape = jax.ShapeDtypeStruct
    return kernel_call(
        norm_back_body,
        (shape((length, width), f32), shape((length, width), bf16), shape((8, width), f32)),
        [],
        [smem_spec()] + [vmem_spec()] * 9,
    )(factor, mid, gains, grad_out, *sums, *late)


def attend_back_body(pieces, head_dim, *refs):
    count = len(pieces.arrays)
    (spot, factor, d_mid_low, grad_kv, q_low, kv_low, prob_ref, cosines, sines) = refs[:9]
    shards = refs[9 : 9 + count]
    joined, d_kv_out = refs[9 + count : 11 + count]
    whole, sem = refs[11 + count :]
    pieces.start(shards, spot, whole, sem)
    length = d_mid_low.shape[0]
    q_width = q_low.shape[1]
    scale = head_dim ** (-0.5)
    cos, sin = cosines[...], sines[...]
    keys, values = kv_low[:, :head_dim], kv_low[:, head_dim:]
    d_kv_out[...] = grad_kv[...].astype(f32) * factor[0]
    pieces.wait(whole, sem)
    heads = step // head_dim

    @pl.loop(0, q_width // step)
    def _(block):
        start = pl.multiple_of(block * step, step)
        d_att = contract_last(d_mid_low[...], whole[pl.ds(start, step), :]).astype(bf16)
        d_k = jnp.zeros((length, head_dim), f32)
        d_v = jnp.zeros((length, head_dim), f32)
        for head in range(heads):
            own = d_att[:, head * head_dim : (head + 1) * head_dim]
            column = pl.multiple_of(start + head * head_dim, head_dim)
            low = prob_ref[block * heads + head]
            prob = low.astype(f32)
            d_prob = contract_last(values, own)
            centre = jnp.sum(prob * d_prob, axis=0, keepdims=True)
            d_raw = (prob * (d_prob - centre) * scale).astype(bf16)
            d_v += jnp.dot(low, own, preferred_element_type=f32)
            d_k += jnp.dot(d_raw, q_low[:, pl.ds(column, head_dim)], preferred_element_type=f32)
            d_q = contract_first(d_raw, keys)
            joined[:, pl.ds(column, head_dim)] = (d_q * cos - swap_halves(d_q) * sin).astype(bf16)
        d_kv_out[:, :head_dim] += d_k
        d_kv_out[:, head_dim:] += d_v

    d_k = d_kv_out[:, :head_dim]
    joined[:, q_width : q_width + head_dim] = (d_k * cos - swap_halves(d_k) * sin).astype(bf16)
    joined[:, q_width + head_dim :] = d_kv_out[:, head_dim:].astype(bf16)


def attend_back(spot, factor, d_mid_low, grad_kv, q_low, kv_low, prob, cosines, sines, pieces, late=()):
    length, width = d_mid_low.shape
    q_width, kv_width = q_low.shape[1], kv_low.shape[1]
    head_dim = kv_width // 2
    shape = jax.ShapeDtypeStruct
    return kernel_call(
        functools.partial(attend_back_body, pieces, head_dim),
        (shape((length, q_width + kv_width), bf16), shape((length, kv_width), f32)),
        [pltpu.VMEM((q_width, width), bf16), pltpu.SemaphoreType.DMA],
        [smem_spec()] * 2 + [vmem_spec()] * 7 + [any_spec()] * len(pieces.arrays),
    )(spot, factor, d_mid_low, grad_kv, q_low, kv_low, prob, cosines, sines, *pieces.arrays, *late)


def finish_body(pieces, *refs):
    count = len(pieces.arrays)
    spot, tokens, gains, joined, d_mid = refs[:5]
    shards = refs[5 : 5 + count]
    d_tokens, gain_out = refs[5 + count : 7 + count]
    whole, sem = refs[7 + count :]
    pieces.start(shards, spot, whole, sem)
    length, width = tokens.shape
    used = joined.shape[1]
    x_full = tokens[...].astype(f32)
    inverse = lax.rsqrt(jnp.mean(x_full * x_full, axis=-1, keepdims=True) + epsilon)
    pieces.wait(whole, sem)

    def add(block, total):
        start = pl.multiple_of(block * step, step)
        columns = pl.ds(start, step)
        d_h = contract_last(joined[...], whole[columns, :used])
        normed = tokens[:, columns].astype(f32) * inverse
        gain_out[:, columns] = jnp.broadcast_to(
            jnp.sum(d_h * normed, axis=0, keepdims=True), (8, step)
        )
        d_normed = d_h * gains[0:1, columns]
        d_tokens[:, columns] = d_normed
        return total + jnp.sum(d_normed * normed, axis=-1, keepdims=True)

    total = lax.fori_loop(0, width // step, add, jnp.zeros((length, 1), f32))
    d_tokens[...] = d_mid[...] + inverse * (d_tokens[...] - x_full * inverse * (total / width))


def finish(spot, tokens, gains, joined, d_mid, pieces, late=()):
    length, width = tokens.shape
    shape = jax.ShapeDtypeStruct
    return kernel_call(
        functools.partial(finish_body, pieces),
        (shape((length, width), f32), shape((8, width), f32)),
        [pltpu.VMEM((width, pieces.columns), bf16), pltpu.SemaphoreType.DMA],
        [smem_spec()] + [vmem_spec()] * 4 + [any_spec()] * len(pieces.arrays),
    )(spot, tokens, gains, joined, d_mid, *pieces.arrays, *late)


def fetch_rows(parts, whole, sem):
    start = 0
    for part in parts:
        pltpu.make_async_copy(part, whole.at[pl.ds(start, part.shape[0])], sem).start()
        start += part.shape[0]
    return pltpu.make_async_copy(whole, whole, sem).wait


def fetch_gate_up(both, shard, first, second, first_sem, second_sem):
    waits = []
    for place, (whole, sem) in enumerate(((first, first_sem), (second, second_sem))):
        for outer in range(both.shape[0] // (2 * shard)):
            source = both.at[pl.ds((2 * outer + place) * shard, shard)]
            pltpu.make_async_copy(source, whole.at[pl.ds(outer * shard, shard)], sem).start()
        waits.append(pltpu.make_async_copy(whole, whole, sem).wait)
    return waits


def gate_body(shard, count, *refs):
    parts, both = refs[:count], refs[count]
    hid, by_gate, by_up = refs[count + 1 : count + 4]
    rows, gate_w, up_w, row_sem, gate_sem, up_sem = refs[count + 4 :]
    waits = fetch_gate_up(both, shard, gate_w, up_w, gate_sem, up_sem)
    waits.append(fetch_rows(parts, rows, row_sem))
    for wait in waits:
        wait()

    @pl.loop(0, rows.shape[0] // step)
    def _(block):
        own = pl.ds(pl.multiple_of(block * step, step), step)
        gate = contract_last(rows[own, :], gate_w[...])
        up = contract_last(rows[own, :], up_w[...])
        sigma = 1.0 / (1.0 + jnp.exp(-gate))
        silu = gate * sigma
        hid[own, :] = (silu * up).astype(bf16)
        by_gate[own, :] = (up * sigma * (1.0 + gate * (1.0 - sigma))).astype(bf16)
        by_up[own, :] = silu.astype(bf16)


def gate(parts, both, shard, late=()):
    total, width = sum(part.shape[0] for part in parts), parts[0].shape[1]
    hidden = both.shape[0] // 2
    out = jax.ShapeDtypeStruct((total, hidden), bf16)
    return kernel_call(
        functools.partial(gate_body, shard, len(parts)),
        (out, out, out),
        [pltpu.VMEM((total, width), bf16)]
        + [pltpu.VMEM((hidden, width), bf16)] * 2
        + [pltpu.SemaphoreType.DMA] * 3,
        [any_spec()] * (len(parts) + 1),
    )(*parts, both, *late)


def d_hidden(rows, weight, scales, grads):
    @pl.loop(0, rows.shape[0] // step)
    def _(block):
        own = pl.ds(pl.multiple_of(block * step, step), step)
        d_hid = contract_last(rows[own, :], weight[...])
        for scale, grad in zip(scales, grads):
            grad[own, :] = (d_hid * scale[own, :].astype(f32)).astype(bf16)


def gate_back_body(count, *refs):
    parts, weight, scales, grads = refs[:count], refs[count], refs[count + 1 : count + 3], refs[count + 3 : count + 5]
    rows, sem = refs[count + 5 :]
    fetch_rows(parts, rows, sem)()
    d_hidden(rows, weight, scales, grads)


def gate_back(parts, weight, scales, late=()):
    count = len(parts)
    total, width = sum(part.shape[0] for part in parts), parts[0].shape[1]
    grad = jax.ShapeDtypeStruct((total, weight.shape[0]), bf16)
    return kernel_call(
        functools.partial(gate_back_body, count),
        (grad, grad),
        [pltpu.VMEM((total, width), bf16), pltpu.SemaphoreType.DMA],
        [any_spec()] * count + [vmem_spec()] * 3,
    )(*parts, weight, *scales, *late)


def rows_back_body(shard, size, *refs):
    grads, boths, outs = refs[:4], refs[4:6], refs[6:12]
    weights, sems = refs[12:16], refs[16]
    waits = []
    for place in range(2):
        waits += fetch_gate_up(
            boths[place], shard, weights[2 * place], weights[2 * place + 1],
            sems.at[2 * place], sems.at[2 * place + 1],
        )
    for wait in waits:
        wait()

    def block(place):
        own = pl.ds(place * size, size)
        total = jnp.dot(grads[0][own, :], weights[0][...], preferred_element_type=f32)
        for grad, piece in zip(grads[1:], weights[1:]):
            total += jnp.dot(grad[own, :], piece[...], preferred_element_type=f32)
        return total

    store_routed(row_route, outs, size, block)


def rows_back(grads, boths, shard, late=()):
    total, hidden = grads[0].shape
    width = boths[0].shape[1]
    return kernel_call(
        functools.partial(rows_back_body, shard, total // 8),
        routed(total // 8, width),
        [pltpu.VMEM((hidden, width), bf16)] * 4 + [pltpu.SemaphoreType.DMA((4,))],
        [vmem_spec()] * 4 + [any_spec()] * 2,
    )(*grads, *boths, *late)


def down_body(size, *refs):
    hids, downs, outs = refs[:2], refs[2:4], refs[4:]

    def block(place):
        own = pl.ds(place * size, size)
        total = jnp.dot(hids[0][own, :], downs[0][...], preferred_element_type=f32)
        return total + jnp.dot(hids[1][own, :], downs[1][...], preferred_element_type=f32)

    store_routed(row_route, outs, size, block)


def down(hids, downs, late=()):
    total, width = hids[0].shape[0], downs[0].shape[1]
    return kernel_call(
        functools.partial(down_body, total // 8), routed(total // 8, width), [], [vmem_spec()] * 4
    )(*hids, *downs, *late)


def hidden_sums_body(count, pairs, shard, pieces, received, *refs):
    lefts, parts = refs[:pairs], refs[pairs : pairs + count]
    others = refs[pairs + count : pairs + count + pieces * received]
    refs = refs[pairs + count + pieces * received :]
    outs, rows, sem = refs[:-2], refs[-2], refs[-1]
    fetch_rows(parts, rows, sem)()
    for place, left in enumerate(lefts):
        product = contract_first(left[...], rows[...])
        for outer in range(left.shape[1] // shard):
            start = (pairs * outer + place) * shard
            own = product[outer * shard : (outer + 1) * shard]
            if received:
                piece, row = start // others[0].shape[0], start % others[0].shape[0]
                outs[0][start : start + shard, :] = (
                    own + others[piece][row : row + shard, :].astype(f32)
                ).astype(bf16)
            else:
                piece, row = start // outs[0].shape[0], start % outs[0].shape[0]
                outs[piece][row : row + shard, :] = own.astype(bf16)


def hidden_sums(lefts, parts, shard, pieces, others=None, late=()):
    total, width = lefts[0].shape[0], parts[0].shape[1]
    hidden = lefts[0].shape[1] * len(lefts)
    received = others is not None
    count = 1 if received else pieces
    outs = kernel_call(
        functools.partial(hidden_sums_body, len(parts), len(lefts), shard, pieces, received),
        (jax.ShapeDtypeStruct((hidden // count, width), bf16),) * count,
        [pltpu.VMEM((total, width), bf16), pltpu.SemaphoreType.DMA],
        [vmem_spec()] * len(lefts) + [any_spec()] * len(parts) + [vmem_spec()] * (pieces * received),
    )(*lefts, *parts, *(others or ()), *late)
    return outs[0] if received else outs


def send_sums_body(turned, right, *outs):
    middle, size = turned.shape[0] // 2, outs[0].shape[0]
    for place, out in enumerate(outs):
        own = pl.ds(middle + place * size, size)
        out[...] = jnp.dot(turned[own, :], right[...], preferred_element_type=f32).astype(bf16)


def send_sums(turned, right, late=()):
    return kernel_call(
        send_sums_body,
        (jax.ShapeDtypeStruct((turned.shape[0] // 4, right.shape[1]), bf16),) * 2,
        [],
        [vmem_spec()] * 2,
    )(turned, right, *late)


def keep_sums_body(turned, right, *refs):
    others, outs = refs[:2], refs[2:]
    size = turned.shape[0] // 16

    def block(place):
        own = pl.ds(place * size, size)
        half = pl.ds((place % 4) * size, size)
        product = jnp.dot(turned[own, :], right[...], preferred_element_type=f32)
        return product + others[place // 4][half, :].astype(f32)

    store_routed(column_route, outs, size, block)


def keep_sums(turned, right, others, late=()):
    return kernel_call(
        keep_sums_body,
        routed(turned.shape[0] // 16, right.shape[1]),
        [],
        [vmem_spec()] * 4,
    )(turned, right, *others, *late)


def pass_body(keep_x, keep_y, from_x, from_y, for_x, for_y):
    size = keep_x.shape[0]
    for_x[...] = (keep_x[...].astype(f32) + from_y[:size, :].astype(f32)).astype(bf16)
    for_y[...] = (keep_y[...].astype(f32) + from_x[:size, :].astype(f32)).astype(bf16)


def pass_on(keep_x, keep_y, from_x, from_y, late=()):
    out = jax.ShapeDtypeStruct(keep_x.shape, bf16)
    return kernel_call(pass_body, (out, out), [], [vmem_spec()] * 4)(
        keep_x, keep_y, from_x, from_y, *late
    )


class Grid:
    def __init__(self, dp, fsdp):
        self.dp, self.fsdp = dp, fsdp
        self.depth = fsdp // 2
        self.groups = [[f for f in range(fsdp) if f % 2 == y] for y in range(2)]
        self.dp_index = lax.axis_index("dp")
        self.y = lax.axis_index("fsdp") % 2
        self.spot = jnp.stack([self.dp_index, self.y]).astype(jnp.int32)
        self.outer = lax.axis_index("fsdp") // 2

    def core(self, value):
        return lax.ppermute(value, "dp", [(i, i ^ 1) for i in range(self.dp)])

    def cores(self, values):
        return [self.core(value) for value in values]

    def echo(self, value, times):
        for _ in range(times):
            value = self.core(value)
        return value

    def x_swap(self, value):
        return lax.ppermute(value, "dp", [(i, i ^ 2) for i in range(self.dp)])

    def y_swap(self, value):
        return lax.ppermute(value, "fsdp", [(i, i ^ 1) for i in range(self.fsdp)])

    def plane_sum(self, value):
        value = value + self.core(value)
        pairs = [
            (dp * self.fsdp + f, (dp ^ 2) * self.fsdp + (f ^ 1))
            for dp in range(self.dp)
            for f in range(self.fsdp)
        ]
        across = lax.ppermute(value, ("dp", "fsdp"), pairs)
        return value + self.x_swap(value) + self.y_swap(value) + across

    def shift(self, value, low, high, by):
        pairs = [
            (2 * outer + y, 2 * (outer + by) + y) for outer in range(low, high) for y in range(2)
        ]
        return lax.ppermute(value, "fsdp", pairs)

    def gather_outer(self, value):
        return lax.all_gather(value, "fsdp", axis=0, tiled=True, axis_index_groups=self.groups)

    def scatter_outer(self, value):
        return lax.psum_scatter(
            value, "fsdp", scatter_dimension=0, tiled=True, axis_index_groups=self.groups
        )

    def spread_first(self, first, second):
        return first, second, self.x_swap(first), self.y_swap(second)

    def spread_second(self, first, second, first_x, second_y):
        first, second, first_x, second_y = lax.optimization_barrier(
            (first, second, first_x, second_y)
        )
        first_xy = self.y_swap(first_x)
        second_xy = self.x_swap(second_y)
        first_y = self.y_swap(first)
        second_x = self.x_swap(second)
        return {
            (0, 0): (first, second),
            (1, 0): (first_x, second_x),
            (0, 1): (first_y, second_y),
            (1, 1): (first_xy, second_xy),
        }

    def collect_first(self, parts, late=()):
        _, _, keep_x, keep_y, to_x, to_y = parts
        from_x, from_y = self.x_swap(to_x), self.y_swap(to_y)
        return (*pass_on(keep_x, keep_y, from_x, from_y, late), from_x, from_y)

    def collect_second(self, parts, passed):
        for_x, for_y, from_x, from_y = passed
        return (parts[0], from_y, self.x_swap(for_x)), (parts[1], from_x, self.y_swap(for_y))

    def pieces(self, planes, rows, token=None):
        keys = [(dx, dy) for dx in range(2) for dy in range(2)]
        mine = [half for key in keys for half in planes[key]]
        sent = mine if token is None else after(mine, token)
        theirs = [self.core(half) for half in sent]
        return Pieces(self.depth, rows, mine[0].shape[-1], mine + theirs)

    def total(self, sums):
        halves = []
        for own, middle, last in sums:
            middle = middle[own.shape[0] :]
            halves.append(own.astype(f32) + middle.astype(f32) + last.astype(f32))
        return jnp.concatenate(halves, axis=0)


def local(
    tokens,
    w_q,
    w_kv,
    g_attn,
    g_mlp,
    w_o,
    w_gu,
    w_down,
    grad_out,
    grad_kv,
    group_id,
    group_size,
    group_weight,
):
    grid = Grid(lax.axis_size("dp"), lax.axis_size("fsdp"))
    length, width = tokens.shape
    kv_width = w_kv.shape[1]
    head_dim = kv_width // 2
    q_width = w_q.shape[1]
    shard_rows = w_q.shape[0]
    hidden_rows = w_down.shape[0]
    half = length // 2

    matches = jnp.arange(group_size.shape[0], dtype=jnp.int32) == group_id[0]
    factor = jnp.sum(jnp.where(matches, group_weight / group_size.astype(jnp.float32), 0.0))
    grad_low = (grad_out.astype(jnp.float32) * factor).astype(jnp.bfloat16)
    cosines, sines = rope_tables(length, head_dim)

    plane_keys = ((0, 0), (1, 0), (0, 1), (1, 1))

    def in_order(planes):
        return [piece for key in plane_keys for piece in planes[key]]

    gains = jnp.stack([g_attn, g_mlp], axis=1)
    w_in = jnp.concatenate([w_q, w_kv, jnp.pad(gains, ((0, 0), (0, lanes - 2)))], axis=1)
    w_in_column = grid.gather_outer(w_in)
    w_o_column = grid.gather_outer(w_o)
    grad_first = grid.spread_first(grad_low[:half], grad_low[half:])
    pairs = jnp.swapaxes(w_gu, 0, 1).reshape(2 * hidden_rows, width)
    gu_mine = grid.gather_outer(pairs)
    grad_planes = grid.spread_second(*grad_first)
    grad_rows = in_order(grad_planes)
    cut = grid.depth // 2
    w_in_column = after(w_in_column, grad_planes[1, 1]).reshape(grid.depth, shard_rows, -1)
    in_planes = grid.spread_second(*grid.spread_first(w_in_column[:cut], w_in_column[cut:]))
    in_pieces = grid.pieces(in_planes, shard_rows)
    down_mine = grid.gather_outer(w_down)
    w_o_column = after(w_o_column, in_planes[1, 1]).reshape(grid.depth, shard_rows, -1)
    o_first = grid.spread_first(w_o_column[:cut], w_o_column[cut:])
    h_turned, q_low, kv_out, gain_rows = project(
        grid.spot, tokens, cosines, sines, in_pieces, q_width, kv_width, head_dim
    )
    o_planes = grid.spread_second(*after(o_first, q_low))
    prob, attended, turned = attend(grid.spot, q_low, kv_out, grid.depth, shard_rows)
    o_pieces = grid.pieces(o_planes, shard_rows, attended)
    x_mid, h_first, h_second = mix(grid.spot, tokens, attended, gain_rows, o_pieces)

    ff_rows = in_order(grid.spread_second(*grid.spread_first(h_first, h_second)))
    gu_mine = after(gu_mine, ff_rows)
    by_shard = hidden_rows % 8 == 0
    run_rows = hidden_rows if by_shard else grid.depth * hidden_rows

    def turn(both, rows):
        return both.reshape(-1, rows, hidden_rows, width).swapaxes(0, 1).reshape(both.shape)

    if not by_shard:
        gu_mine = turn(gu_mine, 2)
    gu_other = grid.core(gu_mine)
    hid_mine, *scales_mine = gate(ff_rows, gu_mine, run_rows)
    hid_other, *scales_other = gate(ff_rows, gu_other, run_rows, [hid_mine])
    runs = grid.depth if by_shard else 1
    sent = hidden_sums([hid_other], grad_rows, run_rows, runs)
    down_sum = hidden_sums([hid_mine], grad_rows, run_rows, runs, grid.cores(sent), [sent[0]])
    down_sum, down_mine = lax.optimization_barrier((down_sum, down_mine))
    d_w_down = grid.scatter_outer(down_sum)
    down_other = grid.core(down_mine)
    pair_mine = gate_back(grad_rows, down_mine, scales_mine)
    pair_other = gate_back(grad_rows, down_other, scales_other, [pair_mine[0]])
    d_h_parts = rows_back((*pair_mine, *pair_other), (gu_mine, gu_other), run_rows)
    sent = hidden_sums(pair_other, ff_rows, run_rows, 2*runs, late=[d_h_parts[0]])
    d_h_passed = grid.collect_first(d_h_parts, [sent[0]])
    pair_sum = hidden_sums(
        pair_mine, ff_rows, run_rows, 2*runs, grid.cores(sent), [d_h_passed[0]]
    )
    pair_sum, d_w_down = lax.optimization_barrier((pair_sum, d_w_down))
    d_w_gu = grid.scatter_outer(pair_sum if by_shard else turn(pair_sum, grid.depth))
    d_h_first, d_h_second = grid.collect_second(d_h_parts, d_h_passed)
    d_h_sums = [*d_h_first, *d_h_second]

    d_mid, d_mid_low, gain_two_sum = norm_back(
        factor.reshape(1), x_mid, gain_rows, grad_out, d_h_sums, [pair_sum]
    )
    sent = send_sums(turned, d_mid_low)
    o_parts = keep_sums(turned, d_mid_low, grid.cores(sent))
    joined, d_kv = attend_back(
        grid.spot, factor.reshape(1), d_mid_low, grad_kv, q_low, kv_out,
        prob, cosines, sines, o_pieces, [o_parts[0]],
    )
    o_passed = grid.collect_first(o_parts, [joined])
    sent = send_sums(h_turned, joined, [o_passed[0]])
    d_w_o = grid.total(grid.collect_second(o_parts, o_passed)).astype(bf16)
    d_w_o = grid.scatter_outer(d_w_o).astype(f32)
    in_parts = keep_sums(h_turned, joined, grid.cores(sent), [o_passed[0]])
    d_tokens, gain_one_sum = finish(
        grid.spot, tokens, gain_rows, joined, d_mid, in_pieces, [in_parts[0]]
    )
    in_passed = grid.collect_first(in_parts, [gain_one_sum, d_w_gu])
    d_w_in = grid.total(grid.collect_second(in_parts, in_passed)).astype(bf16)
    d_w_gu = jnp.stack([d_w_gu[:hidden_rows], d_w_gu[hidden_rows:]], axis=1).astype(f32)
    d_w_down = d_w_down.astype(f32)
    mlp_parts = down((hid_mine, hid_other), (down_mine, down_other), [in_passed[0]])
    d_w_in, mlp_parts = lax.optimization_barrier((d_w_in, mlp_parts))
    mlp_sum = grid.total(grid.collect_second(mlp_parts, grid.collect_first(mlp_parts)))
    output = (x_mid + mlp_sum).astype(jnp.bfloat16)
    gain_sums = jnp.stack([gain_one_sum[0], gain_two_sum[0]], axis=0)
    gain_sums = grid.plane_sum(gain_sums)
    own_gains = lax.dynamic_slice(
        gain_sums.reshape(2, grid.dp, grid.depth, 2, shard_rows),
        (0, grid.dp_index, 0, grid.y, 0),
        (2, 1, grid.depth, 1, shard_rows),
    ).reshape(2, grid.depth * shard_rows)
    extra = jnp.pad(own_gains.T, ((0, 0), (0, lanes - 2))).astype(bf16)
    d_w_in = grid.scatter_outer(jnp.concatenate([d_w_in, extra], axis=1)).astype(f32)
    return (
        output,
        d_tokens,
        kv_out,
        d_kv,
        d_w_in[:, :q_width],
        d_w_in[:, q_width : q_width + kv_width],
        d_w_in[:, q_width + kv_width],
        d_w_in[:, q_width + kv_width + 1],
        d_w_o,
        d_w_gu,
        d_w_down,
    )


def solution(mesh):
    placed = (
        P(("dp", "fsdp"), None),
        P(("dp", "fsdp"), None),
        P(("dp", "fsdp"), None),
        P(("dp", "fsdp")),
        P(("dp", "fsdp")),
        P(("dp", "fsdp"), None),
        P(("dp", "fsdp"), None, None),
        P(("dp", "fsdp"), None),
        P(("dp", "fsdp"), None),
        P(("dp", "fsdp"), None),
        P(("dp", "fsdp")),
        P(),
        P(),
    )
    return jax.shard_map(
        local,
        mesh=mesh,
        in_specs=placed,
        out_specs=(
            P(("dp", "fsdp"), None),
            P(("dp", "fsdp"), None),
            P(("dp", "fsdp"), None),
            P(("dp", "fsdp"), None),
            P(("dp", "fsdp"), None),
            P(("dp", "fsdp"), None),
            P(("dp", "fsdp")),
            P(("dp", "fsdp")),
            P(("dp", "fsdp"), None),
            P(("dp", "fsdp"), None, None),
            P(("dp", "fsdp"), None),
        ),
        check_vma=False,
    )
```

```python
import functools

import jax
import jax.numpy as jnp
from jax import lax
from jax.experimental import pallas as pl
from jax.experimental.pallas import tpu as pltpu
from jax.sharding import PartitionSpec as P

epsilon = 1e-05
theta_base = 10000.0
bf16 = jnp.bfloat16
f32 = jnp.float32
lanes = 128
step = 256
vmem_limit = 60 * 1024 * 1024


def rope_tables(length, width):
    halfway = width // 2
    freqs = theta_base ** (-(jnp.arange(halfway, dtype=jnp.float32) * 2.0 / width))
    angles = jnp.arange(length, dtype=jnp.float32)[:, None] * freqs[None, :]
    cosines, sine_part = jnp.cos(angles), jnp.sin(angles)
    return (
        jnp.concatenate([cosines, cosines], axis=1),
        jnp.concatenate([-sine_part, sine_part], axis=1),
    )


def contract(left, right, left_axis, right_axis):
    return lax.dot_general(
        left, right, (((left_axis,), (right_axis,)), ((), ())), preferred_element_type=jnp.float32
    )


def contract_last(left, right):
    return contract(left, right, left.ndim - 1, right.ndim - 1)


def contract_first(left, right):
    return contract(left, right, 0, 0)


def after(value, token):
    value, _ = lax.optimization_barrier((value, token))
    return value


def vmem_spec():
    return pl.BlockSpec(memory_space=pltpu.VMEM)


def any_spec():
    return pl.BlockSpec(memory_space=pl.ANY)


def smem_spec():
    return pl.BlockSpec(memory_space=pltpu.SMEM)


def kernel_call(body, out_shapes, scratch, in_specs, out_spec=vmem_spec):
    def run(*operands):
        known, late = len(in_specs), len(operands) - len(in_specs)

        def whole_body(*refs):
            body(*refs[:known], *refs[known + late :])

        return pl.pallas_call(
            whole_body,
            out_shape=out_shapes,
            in_specs=in_specs + [any_spec()] * late,
            out_specs=jax.tree.map(lambda _: out_spec(), out_shapes),
            scratch_shapes=scratch,
            compiler_params=pltpu.CompilerParams(vmem_limit_bytes=vmem_limit),
            cost_estimate=pl.CostEstimate(flops=1, bytes_accessed=1, transcendentals=0),
            name=getattr(body, "func", body).__name__[: -len("_body")],
        )(*operands)

    return run


def route(keys):
    place = {(key, half): 2 * i + half for i, key in enumerate(keys) for half in range(2)}
    own, x, y, both = (0, 0), (1, 0), (0, 1), (1, 1)
    return (
        (place[own, 0],),
        (place[own, 1],),
        (place[x, 0],),
        (place[y, 1],),
        (place[both, 1], place[x, 1]),
        (place[both, 0], place[y, 0]),
    )


row_route = route(((0, 0), (1, 0), (0, 1), (1, 1)))
column_route = route(((0, 0), (0, 1), (1, 0), (1, 1)))


def routed(size, columns):
    return tuple(
        jax.ShapeDtypeStruct((size * len(blocks), columns), bf16) for blocks in row_route
    )


def send_blocks(way, outs, held, index, size, sem):
    for blocks, out in zip(way, outs):
        for spot, place in enumerate(blocks):

            @pl.when(index == place // 2)
            def _():
                pltpu.make_async_copy(
                    held.at[pl.ds(place * size, size)], out.at[pl.ds(spot * size, size)], sem
                ).start()


def wait_all(whole, sem):
    pltpu.make_async_copy(whole, whole, sem).wait()


class Pieces:
    def __init__(self, depth, rows, columns, arrays):
        self.depth, self.rows, self.columns, self.arrays = depth, rows, columns, arrays

    def start(self, refs, spot, whole, sem):
        cut = self.depth // 2
        place = 0
        for flip in range(2):
            for dx in range(2):
                for dy in range(2):
                    for low, high in ((0, cut), (cut, self.depth)):
                        for outer in range(low, high):
                            block = (
                                (spot[0] ^ (2 * dx + flip)) * self.depth + outer
                            ) * 2 + (spot[1] ^ dy)
                            row = pl.multiple_of(block * self.rows, self.rows)
                            pltpu.make_async_copy(
                                refs[place].at[outer - low], whole.at[pl.ds(row, self.rows)], sem
                            ).start()
                        place += 1

    def wait(self, whole, sem):
        pltpu.make_async_copy(whole, whole, sem).wait()


def swap_halves(value):
    return pltpu.roll(value, value.shape[-1] // 2, 1)


def relative_place(block, spot, depth):
    side = block % 2
    outer = (block // 2) % depth
    flips = (block // (2 * depth)) ^ spot[0]
    return (((flips % 2) * 2 + flips // 2) * 2 + (side ^ spot[1])) * depth + outer


def put_in_order(source, target, spot, depth, rows):
    @pl.loop(0, source.shape[0] // rows)
    def _(block):
        place = pl.multiple_of(relative_place(block, spot, depth) * rows, rows)
        target[pl.ds(place, rows), :] = source[pl.ds(pl.multiple_of(block * rows, rows), rows), :]


def project_body(pieces, q_width, kv_width, head_dim, *refs):
    count = len(pieces.arrays)
    spot, tokens, cosines, sines = refs[:4]
    shards = refs[4 : 4 + count]
    h_turned, q_out, kv_out, gain_out = refs[4 + count : 8 + count]
    whole, h_low, flat, sem = refs[8 + count :]
    pieces.start(shards, spot, whole, sem)
    width = tokens.shape[1]
    x_full = tokens[...].astype(f32)
    inverse = lax.rsqrt(jnp.mean(x_full * x_full, axis=-1, keepdims=True) + epsilon)
    pieces.wait(whole, sem)
    pick = (
        lax.broadcasted_iota(jnp.int32, (8, lanes), 0) == lax.broadcasted_iota(jnp.int32, (8, lanes), 1)
    ).astype(bf16)
    gains = contract_last(pick, whole[:, q_width + kv_width :])
    gain_out[...] = gains
    h_low[...] = (x_full * inverse * gains[0:1]).astype(bf16)
    cos, sin = cosines[...], sines[...]
    kv_pre = jnp.dot(h_low[...], whole[:, q_width : q_width + kv_width], preferred_element_type=f32)
    key_part = kv_pre[:, :head_dim]
    kv_out[:, :head_dim] = (key_part * cos + swap_halves(key_part) * sin).astype(bf16)
    kv_out[:, head_dim:] = kv_pre[:, head_dim:].astype(bf16)

    @pl.loop(0, q_width // step)
    def _(block):
        start = pl.multiple_of(block * step, step)
        q_pre = jnp.dot(h_low[...], whole[:, pl.ds(start, step)], preferred_element_type=f32)
        for head in range(step // head_dim):
            own = q_pre[:, head * head_dim : (head + 1) * head_dim]
            column = pl.multiple_of(start + head * head_dim, head_dim)
            q_out[:, pl.ds(column, head_dim)] = (own * cos + swap_halves(own) * sin).astype(bf16)

    @pl.loop(0, width // step)
    def _(block):
        start = pl.multiple_of(block * step, step)
        flat[pl.ds(start, step), :] = h_low[:, pl.ds(start, step)].T

    put_in_order(flat, h_turned, spot, pieces.depth, pieces.rows)


def project(spot, tokens, cosines, sines, pieces, q_width, kv_width, head_dim, late=()):
    length, width = tokens.shape
    count = len(pieces.arrays)
    shape = jax.ShapeDtypeStruct
    return kernel_call(
        functools.partial(project_body, pieces, q_width, kv_width, head_dim),
        (
            shape((width, length), bf16),
            shape((length, q_width), bf16),
            shape((length, kv_width), bf16),
            shape((8, width), f32),
        ),
        [
            pltpu.VMEM((width, pieces.columns), bf16),
            pltpu.VMEM((length, width), bf16),
            pltpu.VMEM((width, length), bf16),
            pltpu.SemaphoreType.DMA,
        ],
        [smem_spec(), vmem_spec(), vmem_spec(), vmem_spec()] + [any_spec()] * count,
    )(spot, tokens, cosines, sines, *pieces.arrays, *late)


def attend_body(depth, rows, head_dim, spot, q_low, kv_low, prob_out, attended_out, turned, flat):
    length, q_width = q_low.shape
    scale = head_dim ** (-0.5)
    keys = kv_low[:, :head_dim]
    values_turned = kv_low[:, head_dim:].T
    allowed = lax.broadcasted_iota(jnp.int32, (length, length), 0) <= lax.broadcasted_iota(
        jnp.int32, (length, length), 1
    )
    heads = step // head_dim

    @pl.loop(0, q_width // step)
    def _(block):
        for head in range(heads):
            column = pl.multiple_of(block * step + head * head_dim, head_dim)
            queries = q_low[:, pl.ds(column, head_dim)]
            logits = jnp.where(allowed, contract_last(keys, queries) * scale, -1e30)
            exp_vals = jnp.exp(logits - jnp.max(logits, axis=0, keepdims=True))
            prob = (exp_vals / jnp.sum(exp_vals, axis=0, keepdims=True)).astype(bf16)
            prob_out[block * heads + head] = prob
            mixed = jnp.dot(values_turned, prob, preferred_element_type=f32)
            flat[pl.ds(column, head_dim), :] = mixed.astype(bf16)
            attended_out[:, pl.ds(column, head_dim)] = mixed.T.astype(bf16)

    put_in_order(flat, turned, spot, depth, rows)


def attend(spot, q_low, kv_low, depth, rows, late=()):
    length, q_width = q_low.shape
    head_dim = kv_low.shape[1] // 2
    shape = jax.ShapeDtypeStruct
    return kernel_call(
        functools.partial(attend_body, depth, rows, head_dim),
        (
            shape((q_width // head_dim, length, length), bf16),
            shape((length, q_width), bf16),
            shape((q_width, length), bf16),
        ),
        [pltpu.VMEM((q_width, length), bf16)],
        [smem_spec(), vmem_spec(), vmem_spec()],
    )(spot, q_low, kv_low, *late)


def mix_body(pieces, *refs):
    count = len(pieces.arrays)
    spot, tokens, attended, gains = refs[:4]
    shards = refs[4 : 4 + count]
    mid_out, first_out, second_out = refs[4 + count : 7 + count]
    whole, sem = refs[7 + count :]
    pieces.start(shards, spot, whole, sem)
    length, width = tokens.shape
    pieces.wait(whole, sem)

    def add(block, total):
        start = pl.multiple_of(block * step, step)
        branch = jnp.dot(attended[...], whole[:, pl.ds(start, step)], preferred_element_type=f32)
        x_mid = tokens[:, pl.ds(start, step)].astype(f32) + branch
        mid_out[:, pl.ds(start, step)] = x_mid
        return total + jnp.sum(x_mid * x_mid, axis=-1, keepdims=True)

    total = lax.fori_loop(0, width // step, add, jnp.zeros((length, 1), f32))
    inverse = lax.rsqrt(total / width + epsilon)
    h_two = (mid_out[...] * inverse * gains[1:2, :]).astype(bf16)
    first_out[...] = h_two[: length // 2]
    second_out[...] = h_two[length // 2 :]


def mix(spot, tokens, attended, gains, pieces, late=()):
    length, width = tokens.shape
    shape = jax.ShapeDtypeStruct
    half = shape((length // 2, width), bf16)
    rows = attended.shape[1]
    return kernel_call(
        functools.partial(mix_body, pieces),
        (shape((length, width), f32), half, half),
        [pltpu.VMEM((rows, width), bf16), pltpu.SemaphoreType.DMA],
        [smem_spec(), vmem_spec(), vmem_spec(), vmem_spec()] + [any_spec()] * len(pieces.arrays),
    )(spot, tokens, attended, gains, *pieces.arrays, *late)


def norm_back_body(factor, mid, gains, grad_out, *refs):
    sums = refs[:6]
    d_mid_out, d_mid_low, gain_out = refs[6:]
    half = mid.shape[0] // 2
    size = half // 4
    gain = gains[1:2, :]
    gain_out[...] = jnp.zeros_like(gain_out)
    for part in range(2):
        own, middle, last = sums[3 * part : 3 * part + 3]

        @pl.loop(0, 4)
        def _(block):
            start = pl.multiple_of(block * size, size)
            here, there = pl.ds(start, size), pl.ds(half + start, size)
            rows = pl.ds(part * half + start, size)
            d_h = own[here, :].astype(f32) + middle[there, :].astype(f32) + last[here, :].astype(f32)
            x_mid = mid[rows, :]
            inverse = lax.rsqrt(jnp.mean(x_mid * x_mid, axis=-1, keepdims=True) + epsilon)
            normed = x_mid * inverse
            product = d_h * normed
            gain_out[0:1, :] += jnp.sum(product, axis=0, keepdims=True)
            mean = jnp.mean(product * gain, axis=-1, keepdims=True)
            grad_top = grad_out[rows, :].astype(f32) * factor[0]
            d_mid = grad_top + inverse * (d_h * gain - normed * mean)
            d_mid_out[rows, :] = d_mid
            d_mid_low[rows, :] = d_mid.astype(bf16)


def norm_back(factor, mid, gains, grad_out, sums, late=()):
    length, width = mid.shape
    shape = jax.ShapeDtypeStruct
    return kernel_call(
        norm_back_body,
        (shape((length, width), f32), shape((length, width), bf16), shape((8, width), f32)),
        [],
        [smem_spec()] + [vmem_spec()] * 9,
    )(factor, mid, gains, grad_out, *sums, *late)


def attend_back_body(pieces, head_dim, *refs):
    count = len(pieces.arrays)
    (spot, factor, d_mid_low, grad_kv, q_low, kv_low, prob_ref, cosines, sines) = refs[:9]
    shards = refs[9 : 9 + count]
    joined, d_kv_out = refs[9 + count : 11 + count]
    whole, sem = refs[11 + count :]
    pieces.start(shards, spot, whole, sem)
    length = d_mid_low.shape[0]
    q_width = q_low.shape[1]
    scale = head_dim ** (-0.5)
    cos, sin = cosines[...], sines[...]
    keys, values = kv_low[:, :head_dim], kv_low[:, head_dim:]
    d_kv_out[...] = grad_kv[...].astype(f32) * factor[0]
    pieces.wait(whole, sem)
    heads = step // head_dim

    @pl.loop(0, q_width // step)
    def _(block):
        start = pl.multiple_of(block * step, step)
        d_att = contract_last(d_mid_low[...], whole[pl.ds(start, step), :]).astype(bf16)
        d_k = jnp.zeros((length, head_dim), f32)
        d_v = jnp.zeros((length, head_dim), f32)
        for head in range(heads):
            own = d_att[:, head * head_dim : (head + 1) * head_dim]
            column = pl.multiple_of(start + head * head_dim, head_dim)
            low = prob_ref[block * heads + head]
            prob = low.astype(f32)
            d_prob = contract_last(values, own)
            centre = jnp.sum(prob * d_prob, axis=0, keepdims=True)
            d_raw = (prob * (d_prob - centre) * scale).astype(bf16)
            d_v += jnp.dot(low, own, preferred_element_type=f32)
            d_k += jnp.dot(d_raw, q_low[:, pl.ds(column, head_dim)], preferred_element_type=f32)
            d_q = contract_first(d_raw, keys)
            joined[:, pl.ds(column, head_dim)] = (d_q * cos - swap_halves(d_q) * sin).astype(bf16)
        d_kv_out[:, :head_dim] += d_k
        d_kv_out[:, head_dim:] += d_v

    d_k = d_kv_out[:, :head_dim]
    joined[:, q_width : q_width + head_dim] = (d_k * cos - swap_halves(d_k) * sin).astype(bf16)
    joined[:, q_width + head_dim :] = d_kv_out[:, head_dim:].astype(bf16)


def attend_back(spot, factor, d_mid_low, grad_kv, q_low, kv_low, prob, cosines, sines, pieces, late=()):
    length, width = d_mid_low.shape
    q_width, kv_width = q_low.shape[1], kv_low.shape[1]
    head_dim = kv_width // 2
    shape = jax.ShapeDtypeStruct
    return kernel_call(
        functools.partial(attend_back_body, pieces, head_dim),
        (shape((length, q_width + kv_width), bf16), shape((length, kv_width), f32)),
        [pltpu.VMEM((q_width, width), bf16), pltpu.SemaphoreType.DMA],
        [smem_spec()] * 2 + [vmem_spec()] * 7 + [any_spec()] * len(pieces.arrays),
    )(spot, factor, d_mid_low, grad_kv, q_low, kv_low, prob, cosines, sines, *pieces.arrays, *late)


def finish_body(pieces, *refs):
    count = len(pieces.arrays)
    spot, tokens, gains, joined, d_mid = refs[:5]
    shards = refs[5 : 5 + count]
    d_tokens, gain_out = refs[5 + count : 7 + count]
    whole, sem = refs[7 + count :]
    pieces.start(shards, spot, whole, sem)
    length, width = tokens.shape
    used = joined.shape[1]
    x_full = tokens[...].astype(f32)
    inverse = lax.rsqrt(jnp.mean(x_full * x_full, axis=-1, keepdims=True) + epsilon)
    pieces.wait(whole, sem)

    def add(block, total):
        start = pl.multiple_of(block * step, step)
        columns = pl.ds(start, step)
        d_h = contract_last(joined[...], whole[columns, :used])
        normed = tokens[:, columns].astype(f32) * inverse
        gain_out[:, columns] = jnp.broadcast_to(
            jnp.sum(d_h * normed, axis=0, keepdims=True), (8, step)
        )
        d_normed = d_h * gains[0:1, columns]
        d_tokens[:, columns] = d_normed
        return total + jnp.sum(d_normed * normed, axis=-1, keepdims=True)

    total = lax.fori_loop(0, width // step, add, jnp.zeros((length, 1), f32))
    d_tokens[...] = d_mid[...] + inverse * (d_tokens[...] - x_full * inverse * (total / width))


def finish(spot, tokens, gains, joined, d_mid, pieces, late=()):
    length, width = tokens.shape
    shape = jax.ShapeDtypeStruct
    return kernel_call(
        functools.partial(finish_body, pieces),
        (shape((length, width), f32), shape((8, width), f32)),
        [pltpu.VMEM((width, pieces.columns), bf16), pltpu.SemaphoreType.DMA],
        [smem_spec()] + [vmem_spec()] * 4 + [any_spec()] * len(pieces.arrays),
    )(spot, tokens, gains, joined, d_mid, *pieces.arrays, *late)


def fetch_rows(parts, whole, sem):
    start = 0
    for part in parts:
        pltpu.make_async_copy(part, whole.at[pl.ds(start, part.shape[0])], sem).start()
        start += part.shape[0]
    return pltpu.make_async_copy(whole, whole, sem).wait


def fetch_gate_up(both, shard, first, second, first_sem, second_sem):
    waits = []
    for place, (whole, sem) in enumerate(((first, first_sem), (second, second_sem))):
        for outer in range(both.shape[0] // (2 * shard)):
            source = both.at[pl.ds((2 * outer + place) * shard, shard)]
            pltpu.make_async_copy(source, whole.at[pl.ds(outer * shard, shard)], sem).start()
        waits.append(pltpu.make_async_copy(whole, whole, sem).wait)
    return waits


def fetch_row_blocks(parts, whole, sems):
    size = parts[0].shape[0]
    for place, part in enumerate(parts):
        sem = sems.at[place * size // step]
        pltpu.make_async_copy(part, whole.at[pl.ds(place * size, size)], sem).start()


def gate_body(shard, count, *refs):
    parts, both = refs[:count], refs[count]
    hid, by_gate, by_up = refs[count + 1 : count + 4]
    rows, gate_w, up_w, row_sems, gate_sem, up_sem = refs[count + 4 :]
    waits = fetch_gate_up(both, shard, gate_w, up_w, gate_sem, up_sem)
    fetch_row_blocks(parts, rows, row_sems)
    for wait in waits:
        wait()

    @pl.loop(0, rows.shape[0] // step)
    def _(block):
        own = pl.ds(pl.multiple_of(block * step, step), step)
        wait_all(rows.at[own], row_sems.at[block])
        gate = contract_last(rows[own, :], gate_w[...])
        up = contract_last(rows[own, :], up_w[...])
        sigma = 1.0 / (1.0 + jnp.exp(-gate))
        silu = gate * sigma
        hid[own, :] = (silu * up).astype(bf16)
        by_gate[own, :] = (up * sigma * (1.0 + gate * (1.0 - sigma))).astype(bf16)
        by_up[own, :] = silu.astype(bf16)


def gate(parts, both, shard, late=()):
    total, width = sum(part.shape[0] for part in parts), parts[0].shape[1]
    hidden = both.shape[0] // 2
    out = jax.ShapeDtypeStruct((total, hidden), bf16)
    return kernel_call(
        functools.partial(gate_body, shard, len(parts)),
        (out, out, out),
        [pltpu.VMEM((total, width), bf16)]
        + [pltpu.VMEM((hidden, width), bf16)] * 2
        + [pltpu.SemaphoreType.DMA((total // step,)), pltpu.SemaphoreType.DMA, pltpu.SemaphoreType.DMA],
        [any_spec()] * (len(parts) + 1),
    )(*parts, both, *late)


def gate_back_body(count, *refs):
    parts, weight, scales, grads = refs[:count], refs[count], refs[count + 1 : count + 3], refs[count + 3 : count + 5]
    rows, row_sems = refs[count + 5 :]
    fetch_row_blocks(parts, rows, row_sems)

    @pl.loop(0, rows.shape[0] // step)
    def _(block):
        own = pl.ds(pl.multiple_of(block * step, step), step)
        wait_all(rows.at[own], row_sems.at[block])
        d_hid = contract_last(rows[own, :], weight[...])
        for scale, grad in zip(scales, grads):
            grad[own, :] = (d_hid * scale[own, :].astype(f32)).astype(bf16)


def gate_back(parts, weight, scales, late=()):
    count = len(parts)
    total, width = sum(part.shape[0] for part in parts), parts[0].shape[1]
    grad = jax.ShapeDtypeStruct((total, weight.shape[0]), bf16)
    return kernel_call(
        functools.partial(gate_back_body, count),
        (grad, grad),
        [pltpu.VMEM((total, width), bf16), pltpu.SemaphoreType.DMA((total // step,))],
        [any_spec()] * count + [vmem_spec()] * 3,
    )(*parts, weight, *scales, *late)


def rows_back_body(shard, *refs):
    grads, boths, outs = refs[:4], refs[4:6], refs[6:12]
    weights, held, sems = refs[12:16], refs[16], refs[17]
    waits = []
    for place in range(2):
        waits += fetch_gate_up(
            boths[place], shard, weights[2 * place], weights[2 * place + 1],
            sems.at[2 * place], sems.at[2 * place + 1],
        )
    for wait in waits:
        wait()
    size = held.shape[0] // 8

    @pl.loop(0, 4)
    def _(index):
        own = pl.ds(pl.multiple_of(index * 2 * size, 2 * size), 2 * size)

        @pl.loop(0, held.shape[1] // (4 * step))
        def _(block):
            columns = pl.ds(pl.multiple_of(block * 4 * step, 4 * step), 4 * step)
            total = jnp.dot(grads[0][own, :], weights[0][:, columns], preferred_element_type=f32)
            for grad, piece in zip(grads[1:], weights[1:]):
                total += jnp.dot(grad[own, :], piece[:, columns], preferred_element_type=f32)
            held[own, columns] = total.astype(bf16)

        send_blocks(row_route, outs, held, index, size, sems.at[4])

    wait_all(held, sems.at[4])


def rows_back(grads, boths, shard, late=()):
    total, hidden = grads[0].shape
    width = boths[0].shape[1]
    return kernel_call(
        functools.partial(rows_back_body, shard),
        routed(total // 8, width),
        [pltpu.VMEM((hidden, width), bf16)] * 4
        + [pltpu.VMEM((total, width), bf16), pltpu.SemaphoreType.DMA((5,))],
        [vmem_spec()] * 4 + [any_spec()] * 2,
        any_spec,
    )(*grads, *boths, *late)


def down_body(*refs):
    hids, downs, outs, held, sem = refs[:2], refs[2:4], refs[4:10], refs[10], refs[11]
    size = held.shape[0] // 8

    @pl.loop(0, 4)
    def _(index):
        own = pl.ds(pl.multiple_of(index * 2 * size, 2 * size), 2 * size)
        total = jnp.dot(hids[0][own, :], downs[0][...], preferred_element_type=f32)
        total += jnp.dot(hids[1][own, :], downs[1][...], preferred_element_type=f32)
        held[own, :] = total.astype(bf16)
        send_blocks(row_route, outs, held, index, size, sem)

    wait_all(held, sem)


def down(hids, downs, late=()):
    total, width = hids[0].shape[0], downs[0].shape[1]
    return kernel_call(
        down_body,
        routed(total // 8, width),
        [pltpu.VMEM((total, width), bf16), pltpu.SemaphoreType.DMA],
        [vmem_spec()] * 4,
        any_spec,
    )(*hids, *downs, *late)


def hidden_sums_body(count, pairs, shard, pieces, received, *refs):
    lefts, parts = refs[:pairs], refs[pairs : pairs + count]
    others = refs[pairs + count : pairs + count + pieces * received]
    refs = refs[pairs + count + pieces * received :]
    outs, turned, rows, sem = refs[: -pairs - 2], refs[-pairs - 2 : -2], refs[-2], refs[-1]
    wait = fetch_rows(parts, rows, sem)

    @pl.loop(0, rows.shape[0] // step)
    def _(block):
        own = pl.ds(pl.multiple_of(block * step, step), step)
        for left, flat in zip(lefts, turned):
            flat[:, own] = left[own, :].T

    wait()

    @pl.loop(0, rows.shape[1] // step)
    def _(block):
        columns = pl.ds(pl.multiple_of(block * step, step), step)
        for place, flat in enumerate(turned):
            product = jnp.dot(flat[...], rows[:, columns], preferred_element_type=f32)
            for outer in range(flat.shape[0] // shard):
                start = (pairs * outer + place) * shard
                own = product[outer * shard : (outer + 1) * shard]
                if received:
                    piece, row = start // others[0].shape[0], start % others[0].shape[0]
                    outs[0][start : start + shard, columns] = (
                        own + others[piece][row : row + shard, columns].astype(f32)
                    ).astype(bf16)
                else:
                    piece, row = start // outs[0].shape[0], start % outs[0].shape[0]
                    outs[piece][row : row + shard, columns] = own.astype(bf16)


def hidden_sums(lefts, parts, shard, pieces, others=None, late=()):
    total, width = lefts[0].shape[0], parts[0].shape[1]
    hidden = lefts[0].shape[1] * len(lefts)
    received = others is not None
    count = 1 if received else pieces
    outs = kernel_call(
        functools.partial(hidden_sums_body, len(parts), len(lefts), shard, pieces, received),
        (jax.ShapeDtypeStruct((hidden // count, width), bf16),) * count,
        [pltpu.VMEM((left.shape[1], total), bf16) for left in lefts]
        + [pltpu.VMEM((total, width), bf16), pltpu.SemaphoreType.DMA],
        [vmem_spec()] * len(lefts) + [any_spec()] * len(parts) + [vmem_spec()] * (pieces * received),
    )(*lefts, *parts, *(others or ()), *late)
    return outs[0] if received else outs


def send_sums_body(turned, right, first, second, held, sem):
    middle = turned.shape[0] // 2
    size = middle // 4

    @pl.loop(0, 4)
    def _(index):
        start = pl.multiple_of(index * size, size)
        own = turned[pl.ds(middle + start, size), :]
        held[pl.ds(start, size), :] = jnp.dot(own, right[...], preferred_element_type=f32).astype(bf16)
        for place, out in enumerate((first, first, second, second)):

            @pl.when(index == place)
            def _():
                target = out.at[pl.ds((place % 2) * size, size)]
                pltpu.make_async_copy(held.at[pl.ds(place * size, size)], target, sem).start()

    wait_all(held, sem)


def send_sums(turned, right, late=()):
    rows, columns = turned.shape[0] // 2, right.shape[1]
    return kernel_call(
        send_sums_body,
        (jax.ShapeDtypeStruct((rows // 2, columns), bf16),) * 2,
        [pltpu.VMEM((rows, columns), bf16), pltpu.SemaphoreType.DMA],
        [vmem_spec()] * 2,
        any_spec,
    )(turned, right, *late)


def keep_sums_body(turned, right, first, second, *refs):
    outs, arrived, held, in_sem, out_sem = refs[:6], refs[6], refs[7], refs[8], refs[9]
    fetch_rows((first, second), arrived, in_sem)()
    size = turned.shape[0] // 16

    @pl.loop(0, 4)
    def _(index):
        own = pl.ds(pl.multiple_of(index * 2 * size, 2 * size), 2 * size)
        product = jnp.dot(turned[own, :], right[...], preferred_element_type=f32)
        held[own, :] = (product + arrived[own, :].astype(f32)).astype(bf16)
        send_blocks(column_route, outs, held, index, size, out_sem)

    wait_all(held, out_sem)


def keep_sums(turned, right, others, late=()):
    rows, columns = turned.shape[0] // 2, right.shape[1]
    return kernel_call(
        keep_sums_body,
        routed(rows // 8, columns),
        [pltpu.VMEM((rows, columns), bf16)] * 2 + [pltpu.SemaphoreType.DMA] * 2,
        [vmem_spec()] * 2 + [any_spec()] * 2,
        any_spec,
    )(turned, right, *others, *late)


def alternate_body(both, out):
    rows = out.shape[0]

    @pl.loop(0, rows // 8)
    def _(block):
        start = pl.multiple_of(block * 8, 8)
        for place in range(2):
            out[pl.ds(start, 8), place, :] = both[pl.ds(place * rows + start, 8), :].astype(f32)


def alternate(both):
    rows, columns = both.shape[0] // 2, both.shape[1]
    out = jax.ShapeDtypeStruct((rows, 2, columns), f32)
    return kernel_call(alternate_body, out, [], [vmem_spec()])(both)


def pass_body(keep_x, keep_y, from_x, from_y, for_x, for_y):
    size = keep_x.shape[0]
    for_x[...] = (keep_x[...].astype(f32) + from_y[:size, :].astype(f32)).astype(bf16)
    for_y[...] = (keep_y[...].astype(f32) + from_x[:size, :].astype(f32)).astype(bf16)


def pass_on(keep_x, keep_y, from_x, from_y, late=()):
    out = jax.ShapeDtypeStruct(keep_x.shape, bf16)
    return kernel_call(pass_body, (out, out), [], [vmem_spec()] * 4)(
        keep_x, keep_y, from_x, from_y, *late
    )


class Grid:
    def __init__(self, dp, fsdp):
        self.dp, self.fsdp = dp, fsdp
        self.depth = fsdp // 2
        self.groups = [[f for f in range(fsdp) if f % 2 == y] for y in range(2)]
        self.dp_index = lax.axis_index("dp")
        self.y = lax.axis_index("fsdp") % 2
        self.spot = jnp.stack([self.dp_index, self.y]).astype(jnp.int32)
        self.outer = lax.axis_index("fsdp") // 2

    def core(self, value):
        return lax.ppermute(value, "dp", [(i, i ^ 1) for i in range(self.dp)])

    def cores(self, values):
        return [self.core(value) for value in values]

    def echo(self, value, times):
        for _ in range(times):
            value = self.core(value)
        return value

    def x_swap(self, value):
        return lax.ppermute(value, "dp", [(i, i ^ 2) for i in range(self.dp)])

    def y_swap(self, value):
        return lax.ppermute(value, "fsdp", [(i, i ^ 1) for i in range(self.fsdp)])

    def plane_sum(self, value):
        value = value + self.core(value)
        pairs = [
            (dp * self.fsdp + f, (dp ^ 2) * self.fsdp + (f ^ 1))
            for dp in range(self.dp)
            for f in range(self.fsdp)
        ]
        across = lax.ppermute(value, ("dp", "fsdp"), pairs)
        return value + self.x_swap(value) + self.y_swap(value) + across

    def shift(self, value, low, high, by):
        pairs = [
            (2 * outer + y, 2 * (outer + by) + y) for outer in range(low, high) for y in range(2)
        ]
        return lax.ppermute(value, "fsdp", pairs)

    def gather_outer(self, value):
        return lax.all_gather(value, "fsdp", axis=0, tiled=True, axis_index_groups=self.groups)

    def scatter_outer(self, value):
        return lax.psum_scatter(
            value, "fsdp", scatter_dimension=0, tiled=True, axis_index_groups=self.groups
        )

    def spread_first(self, first, second):
        return first, second, self.x_swap(first), self.y_swap(second)

    def spread_second(self, first, second, first_x, second_y):
        first, second, first_x, second_y = lax.optimization_barrier(
            (first, second, first_x, second_y)
        )
        first_xy = self.y_swap(first_x)
        second_xy = self.x_swap(second_y)
        first_y = self.y_swap(first)
        second_x = self.x_swap(second)
        return {
            (0, 0): (first, second),
            (1, 0): (first_x, second_x),
            (0, 1): (first_y, second_y),
            (1, 1): (first_xy, second_xy),
        }

    def collect_first(self, parts, late=()):
        _, _, keep_x, keep_y, to_x, to_y = parts
        from_x, from_y = self.x_swap(to_x), self.y_swap(to_y)
        return (*pass_on(keep_x, keep_y, from_x, from_y, late), from_x, from_y)

    def collect_second(self, parts, passed):
        for_x, for_y, from_x, from_y = passed
        return (parts[0], from_y, self.x_swap(for_x)), (parts[1], from_x, self.y_swap(for_y))

    def pieces(self, planes, rows, token=None):
        keys = [(dx, dy) for dx in range(2) for dy in range(2)]
        mine = [half for key in keys for half in planes[key]]
        sent = mine if token is None else after(mine, token)
        theirs = [self.core(half) for half in sent]
        return Pieces(self.depth, rows, mine[0].shape[-1], mine + theirs)

    def total(self, sums):
        halves = []
        for own, middle, last in sums:
            middle = middle[own.shape[0] :]
            halves.append(own.astype(f32) + middle.astype(f32) + last.astype(f32))
        return jnp.concatenate(halves, axis=0)


def local(
    tokens,
    w_q,
    w_kv,
    g_attn,
    g_mlp,
    w_o,
    w_gu,
    w_down,
    grad_out,
    grad_kv,
    group_id,
    group_size,
    group_weight,
):
    grid = Grid(lax.axis_size("dp"), lax.axis_size("fsdp"))
    length, width = tokens.shape
    kv_width = w_kv.shape[1]
    head_dim = kv_width // 2
    q_width = w_q.shape[1]
    shard_rows = w_q.shape[0]
    hidden_rows = w_down.shape[0]
    half = length // 2

    matches = jnp.arange(group_size.shape[0], dtype=jnp.int32) == group_id[0]
    factor = jnp.sum(jnp.where(matches, group_weight / group_size.astype(jnp.float32), 0.0))
    grad_low = (grad_out.astype(jnp.float32) * factor).astype(jnp.bfloat16)
    cosines, sines = rope_tables(length, head_dim)

    plane_keys = ((0, 0), (1, 0), (0, 1), (1, 1))

    def in_order(planes):
        return [piece for key in plane_keys for piece in planes[key]]

    gains = jnp.stack([g_attn, g_mlp], axis=1)
    w_in = jnp.concatenate([w_q, w_kv, jnp.pad(gains, ((0, 0), (0, lanes - 2)))], axis=1)
    w_in_column = grid.gather_outer(w_in)
    w_o_column = grid.gather_outer(w_o)
    grad_first = grid.spread_first(grad_low[:half], grad_low[half:])
    pairs = jnp.swapaxes(w_gu, 0, 1).reshape(2 * hidden_rows, width)
    gu_mine = grid.gather_outer(pairs)
    grad_planes = grid.spread_second(*grad_first)
    grad_rows = in_order(grad_planes)
    cut = grid.depth // 2
    w_in_column = after(w_in_column, grad_planes[1, 1]).reshape(grid.depth, shard_rows, -1)
    in_planes = grid.spread_second(*grid.spread_first(w_in_column[:cut], w_in_column[cut:]))
    in_pieces = grid.pieces(in_planes, shard_rows)
    down_mine = grid.gather_outer(w_down)
    w_o_column = after(w_o_column, in_planes[1, 1]).reshape(grid.depth, shard_rows, -1)
    o_first = grid.spread_first(w_o_column[:cut], w_o_column[cut:])
    h_turned, q_low, kv_out, gain_rows = project(
        grid.spot, tokens, cosines, sines, in_pieces, q_width, kv_width, head_dim
    )
    o_planes = grid.spread_second(*after(o_first, q_low))
    prob, attended, turned = attend(grid.spot, q_low, kv_out, grid.depth, shard_rows)
    o_pieces = grid.pieces(o_planes, shard_rows, attended)
    x_mid, h_first, h_second = mix(grid.spot, tokens, attended, gain_rows, o_pieces)

    ff_rows = in_order(grid.spread_second(*grid.spread_first(h_first, h_second)))
    gu_mine = after(gu_mine, ff_rows)
    by_shard = hidden_rows % 8 == 0
    run_rows = hidden_rows if by_shard else grid.depth * hidden_rows

    def turn(both, rows):
        return both.reshape(-1, rows, hidden_rows, width).swapaxes(0, 1).reshape(both.shape)

    if not by_shard:
        gu_mine = turn(gu_mine, 2)
    gu_other = grid.core(gu_mine)
    hid_mine, *scales_mine = gate(ff_rows, gu_mine, run_rows)
    hid_other, *scales_other = gate(ff_rows, gu_other, run_rows, [hid_mine])
    runs = grid.depth if by_shard else 1
    sent = hidden_sums([hid_other], grad_rows, run_rows, runs)
    down_sum = hidden_sums([hid_mine], grad_rows, run_rows, runs, grid.cores(sent), [sent[0]])
    down_sum, down_mine = lax.optimization_barrier((down_sum, down_mine))
    d_w_down = grid.scatter_outer(down_sum)
    down_other = grid.core(down_mine)
    pair_mine = gate_back(grad_rows, down_mine, scales_mine)
    pair_other = gate_back(grad_rows, down_other, scales_other, [pair_mine[0]])
    d_h_parts = rows_back((*pair_mine, *pair_other), (gu_mine, gu_other), run_rows)
    sent = hidden_sums(pair_other, ff_rows, run_rows, 2*runs, late=[d_h_parts[0]])
    d_h_passed = grid.collect_first(d_h_parts, [sent[0]])
    pair_sum = hidden_sums(
        pair_mine, ff_rows, run_rows, 2*runs, grid.cores(sent), [d_h_passed[0]]
    )
    pair_sum, d_w_down = lax.optimization_barrier((pair_sum, d_w_down))
    d_w_gu = grid.scatter_outer(pair_sum if by_shard else turn(pair_sum, grid.depth))
    d_h_first, d_h_second = grid.collect_second(d_h_parts, d_h_passed)
    d_h_sums = [*d_h_first, *d_h_second]

    d_mid, d_mid_low, gain_two_sum = norm_back(
        factor.reshape(1), x_mid, gain_rows, grad_out, d_h_sums, [pair_sum]
    )
    sent = send_sums(turned, d_mid_low)
    o_parts = keep_sums(turned, d_mid_low, grid.cores(sent))
    joined, d_kv = attend_back(
        grid.spot, factor.reshape(1), d_mid_low, grad_kv, q_low, kv_out,
        prob, cosines, sines, o_pieces, [o_parts[0]],
    )
    o_passed = grid.collect_first(o_parts, [joined])
    sent = send_sums(h_turned, joined, [o_passed[0]])
    d_w_o = grid.total(grid.collect_second(o_parts, o_passed)).astype(bf16)
    d_w_o = grid.scatter_outer(d_w_o).astype(f32)
    in_parts = keep_sums(h_turned, joined, grid.cores(sent), [o_passed[0]])
    d_tokens, gain_one_sum = finish(
        grid.spot, tokens, gain_rows, joined, d_mid, in_pieces, [in_parts[0]]
    )
    in_passed = grid.collect_first(in_parts, [gain_one_sum, d_w_gu])
    d_w_in = grid.total(grid.collect_second(in_parts, in_passed)).astype(bf16)
    if by_shard:
        d_w_gu = alternate(d_w_gu)
    else:
        d_w_gu = jnp.stack([d_w_gu[:hidden_rows], d_w_gu[hidden_rows:]], axis=1).astype(f32)
    d_w_down = d_w_down.astype(f32)
    mlp_parts = down((hid_mine, hid_other), (down_mine, down_other), [in_passed[0]])
    d_w_in, mlp_parts = lax.optimization_barrier((d_w_in, mlp_parts))
    mlp_sum = grid.total(grid.collect_second(mlp_parts, grid.collect_first(mlp_parts)))
    output = (x_mid + mlp_sum).astype(jnp.bfloat16)
    gain_sums = jnp.stack([gain_one_sum[0], gain_two_sum[0]], axis=0)
    gain_sums = grid.plane_sum(gain_sums)
    own_gains = lax.dynamic_slice(
        gain_sums.reshape(2, grid.dp, grid.depth, 2, shard_rows),
        (0, grid.dp_index, 0, grid.y, 0),
        (2, 1, grid.depth, 1, shard_rows),
    ).reshape(2, grid.depth * shard_rows)
    extra = jnp.pad(own_gains.T, ((0, 0), (0, lanes - 2))).astype(bf16)
    d_w_in = grid.scatter_outer(jnp.concatenate([d_w_in, extra], axis=1))
    return (
        output,
        d_tokens,
        kv_out,
        d_kv,
        d_w_in[:, :q_width].astype(f32),
        d_w_in[:, q_width : q_width + kv_width].astype(f32),
        d_w_in[:, q_width + kv_width].astype(f32),
        d_w_in[:, q_width + kv_width + 1].astype(f32),
        d_w_o,
        d_w_gu,
        d_w_down,
    )


def solution(mesh):
    placed = (
        P(("dp", "fsdp"), None),
        P(("dp", "fsdp"), None),
        P(("dp", "fsdp"), None),
        P(("dp", "fsdp")),
        P(("dp", "fsdp")),
        P(("dp", "fsdp"), None),
        P(("dp", "fsdp"), None, None),
        P(("dp", "fsdp"), None),
        P(("dp", "fsdp"), None),
        P(("dp", "fsdp"), None),
        P(("dp", "fsdp")),
        P(),
        P(),
    )
    return jax.shard_map(
        local,
        mesh=mesh,
        in_specs=placed,
        out_specs=(
            P(("dp", "fsdp"), None),
            P(("dp", "fsdp"), None),
            P(("dp", "fsdp"), None),
            P(("dp", "fsdp"), None),
            P(("dp", "fsdp"), None),
            P(("dp", "fsdp"), None),
            P(("dp", "fsdp")),
            P(("dp", "fsdp")),
            P(("dp", "fsdp"), None),
            P(("dp", "fsdp"), None, None),
            P(("dp", "fsdp"), None),
        ),
        check_vma=False,
    )
```

```python
import functools

import jax
import jax.numpy as jnp
from jax import lax
from jax.experimental import pallas as pl
from jax.experimental.pallas import tpu as pltpu
from jax.sharding import PartitionSpec as P

epsilon = 1e-05
theta_base = 10000.0
bf16 = jnp.bfloat16
f32 = jnp.float32
lanes = 128
step = 256
vmem_limit = 60 * 1024 * 1024


def rope_tables(length, width):
    halfway = width // 2
    freqs = theta_base ** (-(jnp.arange(halfway, dtype=jnp.float32) * 2.0 / width))
    angles = jnp.arange(length, dtype=jnp.float32)[:, None] * freqs[None, :]
    cosines, sine_part = jnp.cos(angles), jnp.sin(angles)
    return (
        jnp.concatenate([cosines, cosines], axis=1),
        jnp.concatenate([-sine_part, sine_part], axis=1),
    )


def contract(left, right, left_axis, right_axis):
    return lax.dot_general(
        left, right, (((left_axis,), (right_axis,)), ((), ())), preferred_element_type=jnp.float32
    )


def contract_last(left, right):
    return contract(left, right, left.ndim - 1, right.ndim - 1)


def contract_first(left, right):
    return contract(left, right, 0, 0)


def after(value, token):
    value, _ = lax.optimization_barrier((value, token))
    return value


def vmem_spec():
    return pl.BlockSpec(memory_space=pltpu.VMEM)


def any_spec():
    return pl.BlockSpec(memory_space=pl.ANY)


def smem_spec():
    return pl.BlockSpec(memory_space=pltpu.SMEM)


def kernel_call(body, out_shapes, scratch, in_specs, out_spec=vmem_spec):
    def run(*operands):
        known, late = len(in_specs), len(operands) - len(in_specs)

        def whole_body(*refs):
            body(*refs[:known], *refs[known + late :])

        return pl.pallas_call(
            whole_body,
            out_shape=out_shapes,
            in_specs=in_specs + [any_spec()] * late,
            out_specs=jax.tree.map(lambda _: out_spec(), out_shapes),
            scratch_shapes=scratch,
            compiler_params=pltpu.CompilerParams(vmem_limit_bytes=vmem_limit),
            cost_estimate=pl.CostEstimate(flops=1, bytes_accessed=1, transcendentals=0),
            name=getattr(body, "func", body).__name__[: -len("_body")],
        )(*operands)

    return run


def route(keys):
    place = {(key, half): 2 * i + half for i, key in enumerate(keys) for half in range(2)}
    own, x, y, both = (0, 0), (1, 0), (0, 1), (1, 1)
    return (
        (place[own, 0],),
        (place[own, 1],),
        (place[x, 0],),
        (place[y, 1],),
        (place[both, 1], place[x, 1]),
        (place[both, 0], place[y, 0]),
    )


row_route = route(((0, 0), (1, 0), (0, 1), (1, 1)))
column_route = route(((0, 0), (0, 1), (1, 0), (1, 1)))


def routed(size, columns):
    return tuple(
        jax.ShapeDtypeStruct((size * len(blocks), columns), bf16) for blocks in row_route
    )


def send_blocks(way, outs, held, index, size, sem):
    for blocks, out in zip(way, outs):
        for spot, place in enumerate(blocks):

            @pl.when(index == place // 2)
            def _():
                pltpu.make_async_copy(
                    held.at[pl.ds(place * size, size)], out.at[pl.ds(spot * size, size)], sem
                ).start()


def wait_all(whole, sem):
    pltpu.make_async_copy(whole, whole, sem).wait()


class Pieces:
    def __init__(self, depth, rows, columns, arrays):
        self.depth, self.rows, self.columns, self.arrays = depth, rows, columns, arrays

    def start(self, refs, spot, whole, sem, apart=False):
        cut = self.depth // 2
        place = 0
        for flip in range(2):
            for dx in range(2):
                for dy in range(2):
                    for low, high in ((0, cut), (cut, self.depth)):
                        for outer in range(low, high):
                            block = (
                                (spot[0] ^ (2 * dx + flip)) * self.depth + outer
                            ) * 2 + (spot[1] ^ dy)
                            row = pl.multiple_of(block * self.rows, self.rows)
                            pltpu.make_async_copy(
                                refs[place].at[outer - low],
                                whole.at[pl.ds(row, self.rows)],
                                sem.at[2 * dx + flip] if apart else sem,
                            ).start()
                        place += 1

    def wait(self, whole, sem):
        pltpu.make_async_copy(whole, whole, sem).wait()

    def group(self, whole, spot, index):
        flip = (index % 2) * 2 + index // 2
        size = whole.shape[0] // 4
        return pl.multiple_of((spot[0] ^ flip) * size, size), size, flip


def swap_halves(value):
    return pltpu.roll(value, value.shape[-1] // 2, 1)


def relative_place(block, spot, depth):
    side = block % 2
    outer = (block // 2) % depth
    flips = (block // (2 * depth)) ^ spot[0]
    return (((flips % 2) * 2 + flips // 2) * 2 + (side ^ spot[1])) * depth + outer


def put_in_order(source, target, spot, depth, rows):
    @pl.loop(0, source.shape[0] // rows)
    def _(block):
        place = pl.multiple_of(relative_place(block, spot, depth) * rows, rows)
        target[pl.ds(place, rows), :] = source[pl.ds(pl.multiple_of(block * rows, rows), rows), :]


def project_body(pieces, q_width, kv_width, head_dim, *refs):
    count = len(pieces.arrays)
    spot, tokens, cosines, sines = refs[:4]
    shards = refs[4 : 4 + count]
    h_turned, q_out, kv_out, gain_out = refs[4 + count : 8 + count]
    whole, h_low, flat, sem = refs[8 + count :]
    pieces.start(shards, spot, whole, sem)
    width = tokens.shape[1]
    x_full = tokens[...].astype(f32)
    inverse = lax.rsqrt(jnp.mean(x_full * x_full, axis=-1, keepdims=True) + epsilon)
    pieces.wait(whole, sem)
    pick = (
        lax.broadcasted_iota(jnp.int32, (8, lanes), 0) == lax.broadcasted_iota(jnp.int32, (8, lanes), 1)
    ).astype(bf16)
    gains = contract_last(pick, whole[:, q_width + kv_width :])
    gain_out[...] = gains
    h_low[...] = (x_full * inverse * gains[0:1]).astype(bf16)
    cos, sin = cosines[...], sines[...]
    kv_pre = jnp.dot(h_low[...], whole[:, q_width : q_width + kv_width], preferred_element_type=f32)
    key_part = kv_pre[:, :head_dim]
    kv_out[:, :head_dim] = (key_part * cos + swap_halves(key_part) * sin).astype(bf16)
    kv_out[:, head_dim:] = kv_pre[:, head_dim:].astype(bf16)

    @pl.loop(0, q_width // step)
    def _(block):
        start = pl.multiple_of(block * step, step)
        q_pre = jnp.dot(h_low[...], whole[:, pl.ds(start, step)], preferred_element_type=f32)
        for head in range(step // head_dim):
            own = q_pre[:, head * head_dim : (head + 1) * head_dim]
            column = pl.multiple_of(start + head * head_dim, head_dim)
            q_out[:, pl.ds(column, head_dim)] = (own * cos + swap_halves(own) * sin).astype(bf16)

    @pl.loop(0, width // step)
    def _(block):
        start = pl.multiple_of(block * step, step)
        flat[pl.ds(start, step), :] = h_low[:, pl.ds(start, step)].T

    put_in_order(flat, h_turned, spot, pieces.depth, pieces.rows)


def project(spot, tokens, cosines, sines, pieces, q_width, kv_width, head_dim, late=()):
    length, width = tokens.shape
    count = len(pieces.arrays)
    shape = jax.ShapeDtypeStruct
    return kernel_call(
        functools.partial(project_body, pieces, q_width, kv_width, head_dim),
        (
            shape((width, length), bf16),
            shape((length, q_width), bf16),
            shape((length, kv_width), bf16),
            shape((8, width), f32),
        ),
        [
            pltpu.VMEM((width, pieces.columns), bf16),
            pltpu.VMEM((length, width), bf16),
            pltpu.VMEM((width, length), bf16),
            pltpu.SemaphoreType.DMA,
        ],
        [smem_spec(), vmem_spec(), vmem_spec(), vmem_spec()] + [any_spec()] * count,
    )(spot, tokens, cosines, sines, *pieces.arrays, *late)


def attend_body(depth, rows, head_dim, spot, q_low, kv_low, prob_out, attended_out, turned, flat):
    length, q_width = q_low.shape
    scale = head_dim ** (-0.5)
    keys = kv_low[:, :head_dim]
    values_turned = kv_low[:, head_dim:].T
    allowed = lax.broadcasted_iota(jnp.int32, (length, length), 0) <= lax.broadcasted_iota(
        jnp.int32, (length, length), 1
    )
    heads = step // head_dim

    @pl.loop(0, q_width // step)
    def _(block):
        for head in range(heads):
            column = pl.multiple_of(block * step + head * head_dim, head_dim)
            queries = q_low[:, pl.ds(column, head_dim)]
            logits = jnp.where(allowed, contract_last(keys, queries) * scale, -1e30)
            exp_vals = jnp.exp(logits - jnp.max(logits, axis=0, keepdims=True))
            prob = (exp_vals / jnp.sum(exp_vals, axis=0, keepdims=True)).astype(bf16)
            prob_out[block * heads + head] = prob
            mixed = jnp.dot(values_turned, prob, preferred_element_type=f32)
            flat[pl.ds(column, head_dim), :] = mixed.astype(bf16)
            attended_out[:, pl.ds(column, head_dim)] = mixed.T.astype(bf16)

    put_in_order(flat, turned, spot, depth, rows)


def attend(spot, q_low, kv_low, depth, rows, late=()):
    length, q_width = q_low.shape
    head_dim = kv_low.shape[1] // 2
    shape = jax.ShapeDtypeStruct
    return kernel_call(
        functools.partial(attend_body, depth, rows, head_dim),
        (
            shape((q_width // head_dim, length, length), bf16),
            shape((length, q_width), bf16),
            shape((q_width, length), bf16),
        ),
        [pltpu.VMEM((q_width, length), bf16)],
        [smem_spec(), vmem_spec(), vmem_spec()],
    )(spot, q_low, kv_low, *late)


def mix_body(pieces, *refs):
    count = len(pieces.arrays)
    spot, tokens, attended, gains = refs[:4]
    shards = refs[4 : 4 + count]
    mid_out, first_out, second_out = refs[4 + count : 7 + count]
    whole, sem = refs[7 + count :]
    pieces.start(shards, spot, whole, sem, True)
    length, width = tokens.shape
    mid_out[...] = tokens[...].astype(f32)

    @pl.loop(0, 4)
    def _(index):
        row, size, flip = pieces.group(whole, spot, index)
        rows = pl.ds(row, size)
        wait_all(whole.at[rows], sem.at[flip])

        @pl.loop(0, width // (2 * step))
        def _(block):
            columns = pl.ds(pl.multiple_of(block * 2 * step, 2 * step), 2 * step)
            mid_out[:, columns] += jnp.dot(
                attended[:, rows], whole[rows, columns], preferred_element_type=f32
            )

    x_mid = mid_out[...]
    inverse = lax.rsqrt(jnp.mean(x_mid * x_mid, axis=-1, keepdims=True) + epsilon)
    h_two = (x_mid * inverse * gains[1:2, :]).astype(bf16)
    first_out[...] = h_two[: length // 2]
    second_out[...] = h_two[length // 2 :]


def mix(spot, tokens, attended, gains, pieces, late=()):
    length, width = tokens.shape
    shape = jax.ShapeDtypeStruct
    half = shape((length // 2, width), bf16)
    rows = attended.shape[1]
    return kernel_call(
        functools.partial(mix_body, pieces),
        (shape((length, width), f32), half, half),
        [pltpu.VMEM((rows, width), bf16), pltpu.SemaphoreType.DMA((4,))],
        [smem_spec(), vmem_spec(), vmem_spec(), vmem_spec()] + [any_spec()] * len(pieces.arrays),
    )(spot, tokens, attended, gains, *pieces.arrays, *late)


def norm_back_body(factor, mid, gains, grad_out, *refs):
    sums = refs[:6]
    d_mid_out, d_mid_low, gain_out = refs[6:]
    half = mid.shape[0] // 2
    size = half // 4
    gain = gains[1:2, :]
    gain_out[...] = jnp.zeros_like(gain_out)
    for part in range(2):
        own, middle, last = sums[3 * part : 3 * part + 3]

        @pl.loop(0, 4)
        def _(block):
            start = pl.multiple_of(block * size, size)
            here, there = pl.ds(start, size), pl.ds(half + start, size)
            rows = pl.ds(part * half + start, size)
            d_h = own[here, :].astype(f32) + middle[there, :].astype(f32) + last[here, :].astype(f32)
            x_mid = mid[rows, :]
            inverse = lax.rsqrt(jnp.mean(x_mid * x_mid, axis=-1, keepdims=True) + epsilon)
            normed = x_mid * inverse
            product = d_h * normed
            gain_out[0:1, :] += jnp.sum(product, axis=0, keepdims=True)
            mean = jnp.mean(product * gain, axis=-1, keepdims=True)
            grad_top = grad_out[rows, :].astype(f32) * factor[0]
            d_mid = grad_top + inverse * (d_h * gain - normed * mean)
            d_mid_out[rows, :] = d_mid
            d_mid_low[rows, :] = d_mid.astype(bf16)


def norm_back(factor, mid, gains, grad_out, sums, late=()):
    length, width = mid.shape
    shape = jax.ShapeDtypeStruct
    return kernel_call(
        norm_back_body,
        (shape((length, width), f32), shape((length, width), bf16), shape((8, width), f32)),
        [],
        [smem_spec()] + [vmem_spec()] * 9,
    )(factor, mid, gains, grad_out, *sums, *late)


def attend_back_body(pieces, head_dim, *refs):
    count = len(pieces.arrays)
    (spot, factor, d_mid_low, grad_kv, q_low, kv_low, prob_ref, cosines, sines) = refs[:9]
    shards = refs[9 : 9 + count]
    joined, d_kv_out = refs[9 + count : 11 + count]
    whole, sem = refs[11 + count :]
    pieces.start(shards, spot, whole, sem, True)
    length = d_mid_low.shape[0]
    q_width = q_low.shape[1]
    scale = head_dim ** (-0.5)
    cos, sin = cosines[...], sines[...]
    keys, values = kv_low[:, :head_dim], kv_low[:, head_dim:]
    d_kv_out[...] = grad_kv[...].astype(f32) * factor[0]
    heads = step // head_dim

    @pl.loop(0, q_width // step)
    def _(block):
        row, size, flip = pieces.group(whole, spot, block // (whole.shape[0] // 4 // step))
        inside = block % (size // step)

        @pl.when(inside == 0)
        def _():
            wait_all(whole.at[pl.ds(row, size)], sem.at[flip])

        start = pl.multiple_of(row + inside * step, step)
        d_att = contract_last(d_mid_low[...], whole[pl.ds(start, step), :]).astype(bf16)
        d_k = jnp.zeros((length, head_dim), f32)
        d_v = jnp.zeros((length, head_dim), f32)
        for head in range(heads):
            own = d_att[:, head * head_dim : (head + 1) * head_dim]
            column = pl.multiple_of(start + head * head_dim, head_dim)
            low = prob_ref[start // head_dim + head]
            prob = low.astype(f32)
            d_prob = contract_last(values, own)
            centre = jnp.sum(prob * d_prob, axis=0, keepdims=True)
            d_raw = (prob * (d_prob - centre) * scale).astype(bf16)
            d_v += jnp.dot(low, own, preferred_element_type=f32)
            d_k += jnp.dot(d_raw, q_low[:, pl.ds(column, head_dim)], preferred_element_type=f32)
            d_q = contract_first(d_raw, keys)
            joined[:, pl.ds(column, head_dim)] = (d_q * cos - swap_halves(d_q) * sin).astype(bf16)
        d_kv_out[:, :head_dim] += d_k
        d_kv_out[:, head_dim:] += d_v

    d_k = d_kv_out[:, :head_dim]
    joined[:, q_width : q_width + head_dim] = (d_k * cos - swap_halves(d_k) * sin).astype(bf16)
    joined[:, q_width + head_dim :] = d_kv_out[:, head_dim:].astype(bf16)


def attend_back(spot, factor, d_mid_low, grad_kv, q_low, kv_low, prob, cosines, sines, pieces, late=()):
    length, width = d_mid_low.shape
    q_width, kv_width = q_low.shape[1], kv_low.shape[1]
    head_dim = kv_width // 2
    shape = jax.ShapeDtypeStruct
    return kernel_call(
        functools.partial(attend_back_body, pieces, head_dim),
        (shape((length, q_width + kv_width), bf16), shape((length, kv_width), f32)),
        [pltpu.VMEM((q_width, width), bf16), pltpu.SemaphoreType.DMA((4,))],
        [smem_spec()] * 2 + [vmem_spec()] * 7 + [any_spec()] * len(pieces.arrays),
    )(spot, factor, d_mid_low, grad_kv, q_low, kv_low, prob, cosines, sines, *pieces.arrays, *late)


def finish_body(pieces, *refs):
    count = len(pieces.arrays)
    spot, tokens, gains, joined, d_mid = refs[:5]
    shards = refs[5 : 5 + count]
    d_tokens, gain_out = refs[5 + count : 7 + count]
    whole, sem = refs[7 + count :]
    pieces.start(shards, spot, whole, sem)
    length, width = tokens.shape
    used = joined.shape[1]
    x_full = tokens[...].astype(f32)
    inverse = lax.rsqrt(jnp.mean(x_full * x_full, axis=-1, keepdims=True) + epsilon)
    pieces.wait(whole, sem)

    def add(block, total):
        start = pl.multiple_of(block * step, step)
        columns = pl.ds(start, step)
        d_h = contract_last(joined[...], whole[columns, :used])
        normed = tokens[:, columns].astype(f32) * inverse
        gain_out[:, columns] = jnp.broadcast_to(
            jnp.sum(d_h * normed, axis=0, keepdims=True), (8, step)
        )
        d_normed = d_h * gains[0:1, columns]
        d_tokens[:, columns] = d_normed
        return total + jnp.sum(d_normed * normed, axis=-1, keepdims=True)

    total = lax.fori_loop(0, width // step, add, jnp.zeros((length, 1), f32))
    d_tokens[...] = d_mid[...] + inverse * (d_tokens[...] - x_full * inverse * (total / width))


def finish(spot, tokens, gains, joined, d_mid, pieces, late=()):
    length, width = tokens.shape
    shape = jax.ShapeDtypeStruct
    return kernel_call(
        functools.partial(finish_body, pieces),
        (shape((length, width), f32), shape((8, width), f32)),
        [pltpu.VMEM((width, pieces.columns), bf16), pltpu.SemaphoreType.DMA],
        [smem_spec()] + [vmem_spec()] * 4 + [any_spec()] * len(pieces.arrays),
    )(spot, tokens, gains, joined, d_mid, *pieces.arrays, *late)


def fetch_rows(parts, whole, sem):
    start = 0
    for part in parts:
        pltpu.make_async_copy(part, whole.at[pl.ds(start, part.shape[0])], sem).start()
        start += part.shape[0]
    return pltpu.make_async_copy(whole, whole, sem).wait


def fetch_gate_up(both, shard, first, second, first_sem, second_sem):
    waits = []
    for place, (whole, sem) in enumerate(((first, first_sem), (second, second_sem))):
        for outer in range(both.shape[0] // (2 * shard)):
            source = both.at[pl.ds((2 * outer + place) * shard, shard)]
            pltpu.make_async_copy(source, whole.at[pl.ds(outer * shard, shard)], sem).start()
        waits.append(pltpu.make_async_copy(whole, whole, sem).wait)
    return waits


def fetch_row_blocks(parts, whole, sems):
    size = parts[0].shape[0]
    for place, part in enumerate(parts):
        sem = sems.at[place * size // step]
        pltpu.make_async_copy(part, whole.at[pl.ds(place * size, size)], sem).start()


def gate_body(shard, count, *refs):
    parts, both, outs = refs[:count], refs[count], refs[count + 1 : count + 4]
    held, refs = refs[count + 4 : count + 7], refs[count + 7 :]
    rows, gate_w, up_w, row_sems, gate_sem, up_sem, out_sem = refs
    waits = fetch_gate_up(both, shard, gate_w, up_w, gate_sem, up_sem)
    fetch_row_blocks(parts, rows, row_sems)
    for wait in waits:
        wait()

    @pl.loop(0, rows.shape[0] // step)
    def _(block):
        own = pl.ds(pl.multiple_of(block * step, step), step)
        wait_all(rows.at[own], row_sems.at[block])
        gate = contract_last(rows[own, :], gate_w[...])
        up = contract_last(rows[own, :], up_w[...])
        sigma = 1.0 / (1.0 + jnp.exp(-gate))
        silu = gate * sigma
        held[0][own, :] = (silu * up).astype(bf16)
        held[1][own, :] = (up * sigma * (1.0 + gate * (1.0 - sigma))).astype(bf16)
        held[2][own, :] = silu.astype(bf16)
        for source, out in zip(held, outs):
            pltpu.make_async_copy(source.at[own], out.at[own], out_sem).start()

    for source in held:
        wait_all(source, out_sem)


def gate(parts, both, shard, late=()):
    total, width = sum(part.shape[0] for part in parts), parts[0].shape[1]
    hidden = both.shape[0] // 2
    out = jax.ShapeDtypeStruct((total, hidden), bf16)
    return kernel_call(
        functools.partial(gate_body, shard, len(parts)),
        (out, out, out),
        [pltpu.VMEM((total, hidden), bf16)] * 3
        + [pltpu.VMEM((total, width), bf16)]
        + [pltpu.VMEM((hidden, width), bf16)] * 2
        + [pltpu.SemaphoreType.DMA((total // step,))]
        + [pltpu.SemaphoreType.DMA] * 3,
        [any_spec()] * (len(parts) + 1),
        any_spec,
    )(*parts, both, *late)


def gate_back_body(count, *refs):
    parts, weight, scales, grads = refs[:count], refs[count], refs[count + 1 : count + 3], refs[count + 3 : count + 5]
    rows, weight_in, first, second, row_sems, weight_sem, out_sem = refs[count + 5 :]
    wait = fetch_rows([weight], weight_in, weight_sem)
    scaled = (first, second)
    for source, held in zip(scales, scaled):
        for block in range(rows.shape[0] // step):
            own = pl.ds(block * step, step)
            pltpu.make_async_copy(source.at[own], held.at[own], row_sems.at[block]).start()
    fetch_row_blocks(parts, rows, row_sems)
    wait()

    @pl.loop(0, rows.shape[0] // step)
    def _(block):
        own = pl.ds(pl.multiple_of(block * step, step), step)
        for whole in (rows, first, second):
            wait_all(whole.at[own], row_sems.at[block])
        d_hid = contract_last(rows[own, :], weight_in[...])
        for held, grad in zip(scaled, grads):
            held[own, :] = (d_hid * held[own, :].astype(f32)).astype(bf16)
            pltpu.make_async_copy(held.at[own], grad.at[own], out_sem).start()

    for held in scaled:
        wait_all(held, out_sem)


def gate_back(parts, weight, scales, late=()):
    count = len(parts)
    total, width = sum(part.shape[0] for part in parts), parts[0].shape[1]
    hidden = weight.shape[0]
    grad = jax.ShapeDtypeStruct((total, hidden), bf16)
    return kernel_call(
        functools.partial(gate_back_body, count),
        (grad, grad),
        [pltpu.VMEM((total, width), bf16), pltpu.VMEM((hidden, width), bf16)]
        + [pltpu.VMEM((total, hidden), bf16)] * 2
        + [pltpu.SemaphoreType.DMA((total // step,))]
        + [pltpu.SemaphoreType.DMA] * 2,
        [any_spec()] * (count + 3),
        any_spec,
    )(*parts, weight, *scales, *late)


def rows_back_body(shard, *refs):
    grads, boths, outs = refs[:4], refs[4:6], refs[6:12]
    weights, held, sems, out_sem = refs[12:16], refs[16], refs[17], refs[18]
    size, chunk = held.shape[0] // 8, 2 * step
    chunks = held.shape[1] // chunk

    @pl.loop(0, chunks)
    def _(block):
        columns = pl.ds(pl.multiple_of(block * chunk, chunk), chunk)
        for place, weight in enumerate(weights):
            for outer in range(weight.shape[0] // shard):
                source = boths[place // 2].at[pl.ds((2 * outer + place % 2) * shard, shard), columns]
                target = weight.at[pl.ds(outer * shard, shard), columns]
                pltpu.make_async_copy(source, target, sems.at[block]).start()

    @pl.loop(0, chunks)
    def _(block):
        columns = pl.ds(pl.multiple_of(block * chunk, chunk), chunk)
        for weight in weights:
            wait_all(weight.at[:, columns], sems.at[block])

        @pl.loop(0, 4)
        def _(index):
            own = pl.ds(pl.multiple_of(index * 2 * size, 2 * size), 2 * size)
            total = jnp.dot(grads[0][own, :], weights[0][:, columns], preferred_element_type=f32)
            for grad, piece in zip(grads[1:], weights[1:]):
                total += jnp.dot(grad[own, :], piece[:, columns], preferred_element_type=f32)
            held[own, columns] = total.astype(bf16)

        for blocks, out in zip(row_route, outs):
            for spot, place in enumerate(blocks):
                source = held.at[pl.ds(place * size, size), columns]
                target = out.at[pl.ds(spot * size, size), columns]
                pltpu.make_async_copy(source, target, out_sem).start()

    wait_all(held, out_sem)


def rows_back(grads, boths, shard, late=()):
    total, hidden = grads[0].shape
    width = boths[0].shape[1]
    return kernel_call(
        functools.partial(rows_back_body, shard),
        routed(total // 8, width),
        [pltpu.VMEM((hidden, width), bf16)] * 4
        + [
            pltpu.VMEM((total, width), bf16),
            pltpu.SemaphoreType.DMA((width // (2 * step),)),
            pltpu.SemaphoreType.DMA,
        ],
        [vmem_spec()] * 4 + [any_spec()] * 2,
        any_spec,
    )(*grads, *boths, *late)


def down_body(*refs):
    hids, downs, outs, held, sem = refs[:2], refs[2:4], refs[4:10], refs[10], refs[11]
    size = held.shape[0] // 8

    @pl.loop(0, 4)
    def _(index):
        own = pl.ds(pl.multiple_of(index * 2 * size, 2 * size), 2 * size)
        total = jnp.dot(hids[0][own, :], downs[0][...], preferred_element_type=f32)
        total += jnp.dot(hids[1][own, :], downs[1][...], preferred_element_type=f32)
        held[own, :] = total.astype(bf16)
        send_blocks(row_route, outs, held, index, size, sem)

    wait_all(held, sem)


def down(hids, downs, late=()):
    total, width = hids[0].shape[0], downs[0].shape[1]
    return kernel_call(
        down_body,
        routed(total // 8, width),
        [pltpu.VMEM((total, width), bf16), pltpu.SemaphoreType.DMA],
        [vmem_spec()] * 4,
        any_spec,
    )(*hids, *downs, *late)


def hidden_sums_body(count, pairs, shard, pieces, received, *refs):
    lefts, parts = refs[:pairs], refs[pairs : pairs + count]
    others = refs[pairs + count : pairs + count + pieces * received]
    refs = refs[pairs + count + pieces * received :]
    if received:
        refs, arrived, other_sem, out_sem = refs[:-3], refs[-3], refs[-2], refs[-1]
    outs, turned, rows, sem = refs[: -pairs - 2], refs[-pairs - 2 : -2], refs[-2], refs[-1]
    waits = [fetch_rows(parts, rows, sem)]
    if received:
        waits.append(fetch_rows(others, arrived, other_sem))

    @pl.loop(0, rows.shape[0] // step)
    def _(block):
        own = pl.ds(pl.multiple_of(block * step, step), step)
        for left, flat in zip(lefts, turned):
            flat[:, own] = left[own, :].T

    for wait in waits:
        wait()

    @pl.loop(0, rows.shape[1] // step)
    def _(block):
        columns = pl.ds(pl.multiple_of(block * step, step), step)
        for place, flat in enumerate(turned):
            product = jnp.dot(flat[...], rows[:, columns], preferred_element_type=f32)
            for outer in range(flat.shape[0] // shard):
                start = (pairs * outer + place) * shard
                own = product[outer * shard : (outer + 1) * shard]
                if received:
                    here = pl.ds(start, shard)
                    arrived[here, columns] = (own + arrived[here, columns].astype(f32)).astype(bf16)
                else:
                    piece, row = start // outs[0].shape[0], start % outs[0].shape[0]
                    outs[piece][row : row + shard, columns] = own.astype(bf16)
        if received:
            pltpu.make_async_copy(
                arrived.at[:, columns], outs[0].at[:, columns], out_sem
            ).start()

    if received:
        wait_all(arrived, out_sem)


def hidden_sums(lefts, parts, shard, pieces, others=None, late=()):
    total, width = lefts[0].shape[0], parts[0].shape[1]
    hidden = lefts[0].shape[1] * len(lefts)
    received = others is not None
    count = 1 if received else pieces
    scratch = [pltpu.VMEM((left.shape[1], total), bf16) for left in lefts]
    scratch += [pltpu.VMEM((total, width), bf16), pltpu.SemaphoreType.DMA]
    if received:
        scratch += [pltpu.VMEM((hidden, width), bf16)] + [pltpu.SemaphoreType.DMA] * 2
    outs = kernel_call(
        functools.partial(hidden_sums_body, len(parts), len(lefts), shard, pieces, received),
        (jax.ShapeDtypeStruct((hidden // count, width), bf16),) * count,
        scratch,
        [vmem_spec()] * len(lefts) + [any_spec()] * (len(parts) + pieces * received),
        any_spec if received else vmem_spec,
    )(*lefts, *parts, *(others or ()), *late)
    return outs[0] if received else outs


def send_sums_body(turned, right, first, second, held, sem):
    middle = turned.shape[0] // 2
    size = middle // 4

    @pl.loop(0, 4)
    def _(index):
        start = pl.multiple_of(index * size, size)
        own = turned[pl.ds(middle + start, size), :]
        held[pl.ds(start, size), :] = jnp.dot(own, right[...], preferred_element_type=f32).astype(bf16)
        for place, out in enumerate((first, first, second, second)):

            @pl.when(index == place)
            def _():
                target = out.at[pl.ds((place % 2) * size, size)]
                pltpu.make_async_copy(held.at[pl.ds(place * size, size)], target, sem).start()

    wait_all(held, sem)


def send_sums(turned, right, late=()):
    rows, columns = turned.shape[0] // 2, right.shape[1]
    return kernel_call(
        send_sums_body,
        (jax.ShapeDtypeStruct((rows // 2, columns), bf16),) * 2,
        [pltpu.VMEM((rows, columns), bf16), pltpu.SemaphoreType.DMA],
        [vmem_spec()] * 2,
        any_spec,
    )(turned, right, *late)


def keep_sums_body(turned, right, first, second, *refs):
    outs, arrived, held, in_sems, out_sem = refs[:6], refs[6], refs[7], refs[8], refs[9]
    size = turned.shape[0] // 16
    for place, part in enumerate((first, first, second, second)):
        source = part.at[pl.ds((place % 2) * 2 * size, 2 * size)]
        target = arrived.at[pl.ds(place * 2 * size, 2 * size)]
        pltpu.make_async_copy(source, target, in_sems.at[place]).start()

    @pl.loop(0, 4)
    def _(index):
        own = pl.ds(pl.multiple_of(index * 2 * size, 2 * size), 2 * size)
        product = jnp.dot(turned[own, :], right[...], preferred_element_type=f32)
        wait_all(arrived.at[own], in_sems.at[index])
        held[own, :] = (product + arrived[own, :].astype(f32)).astype(bf16)
        send_blocks(column_route, outs, held, index, size, out_sem)

    wait_all(held, out_sem)


def keep_sums(turned, right, others, late=()):
    rows, columns = turned.shape[0] // 2, right.shape[1]
    return kernel_call(
        keep_sums_body,
        routed(rows // 8, columns),
        [pltpu.VMEM((rows, columns), bf16)] * 2
        + [pltpu.SemaphoreType.DMA((4,)), pltpu.SemaphoreType.DMA],
        [vmem_spec()] * 2 + [any_spec()] * 2,
        any_spec,
    )(turned, right, *others, *late)


def alternate_body(both, out):
    rows = out.shape[0]

    @pl.loop(0, rows // 8)
    def _(block):
        start = pl.multiple_of(block * 8, 8)
        for place in range(2):
            out[pl.ds(start, 8), place, :] = both[pl.ds(place * rows + start, 8), :].astype(f32)


def alternate(both):
    rows, columns = both.shape[0] // 2, both.shape[1]
    out = jax.ShapeDtypeStruct((rows, 2, columns), f32)
    return kernel_call(alternate_body, out, [], [vmem_spec()])(both)


def pass_body(keep_x, keep_y, from_x, from_y, for_x, for_y):
    size = keep_x.shape[0]
    for_x[...] = (keep_x[...].astype(f32) + from_y[:size, :].astype(f32)).astype(bf16)
    for_y[...] = (keep_y[...].astype(f32) + from_x[:size, :].astype(f32)).astype(bf16)


def pass_on(keep_x, keep_y, from_x, from_y, late=()):
    out = jax.ShapeDtypeStruct(keep_x.shape, bf16)
    return kernel_call(pass_body, (out, out), [], [vmem_spec()] * 4)(
        keep_x, keep_y, from_x, from_y, *late
    )


class Grid:
    def __init__(self, dp, fsdp):
        self.dp, self.fsdp = dp, fsdp
        self.depth = fsdp // 2
        self.groups = [[f for f in range(fsdp) if f % 2 == y] for y in range(2)]
        self.dp_index = lax.axis_index("dp")
        self.y = lax.axis_index("fsdp") % 2
        self.spot = jnp.stack([self.dp_index, self.y]).astype(jnp.int32)
        self.outer = lax.axis_index("fsdp") // 2

    def core(self, value):
        return lax.ppermute(value, "dp", [(i, i ^ 1) for i in range(self.dp)])

    def cores(self, values):
        return [self.core(value) for value in values]

    def echo(self, value, times):
        for _ in range(times):
            value = self.core(value)
        return value

    def x_swap(self, value):
        return lax.ppermute(value, "dp", [(i, i ^ 2) for i in range(self.dp)])

    def y_swap(self, value):
        return lax.ppermute(value, "fsdp", [(i, i ^ 1) for i in range(self.fsdp)])

    def plane_sum(self, value):
        value = value + self.core(value)
        pairs = [
            (dp * self.fsdp + f, (dp ^ 2) * self.fsdp + (f ^ 1))
            for dp in range(self.dp)
            for f in range(self.fsdp)
        ]
        across = lax.ppermute(value, ("dp", "fsdp"), pairs)
        return value + self.x_swap(value) + self.y_swap(value) + across

    def shift(self, value, low, high, by):
        pairs = [
            (2 * outer + y, 2 * (outer + by) + y) for outer in range(low, high) for y in range(2)
        ]
        return lax.ppermute(value, "fsdp", pairs)

    def gather_outer(self, value):
        return lax.all_gather(value, "fsdp", axis=0, tiled=True, axis_index_groups=self.groups)

    def scatter_outer(self, value):
        return lax.psum_scatter(
            value, "fsdp", scatter_dimension=0, tiled=True, axis_index_groups=self.groups
        )

    def spread_first(self, first, second):
        return first, second, self.x_swap(first), self.y_swap(second)

    def spread_second(self, first, second, first_x, second_y):
        first, second, first_x, second_y = lax.optimization_barrier(
            (first, second, first_x, second_y)
        )
        first_xy = self.y_swap(first_x)
        second_xy = self.x_swap(second_y)
        first_y = self.y_swap(first)
        second_x = self.x_swap(second)
        return {
            (0, 0): (first, second),
            (1, 0): (first_x, second_x),
            (0, 1): (first_y, second_y),
            (1, 1): (first_xy, second_xy),
        }

    def collect_first(self, parts, late=()):
        _, _, keep_x, keep_y, to_x, to_y = parts
        from_x, from_y = self.x_swap(to_x), self.y_swap(to_y)
        return (*pass_on(keep_x, keep_y, from_x, from_y, late), from_x, from_y)

    def collect_second(self, parts, passed):
        for_x, for_y, from_x, from_y = passed
        return (parts[0], from_y, self.x_swap(for_x)), (parts[1], from_x, self.y_swap(for_y))

    def pieces(self, planes, rows, token=None):
        keys = [(dx, dy) for dx in range(2) for dy in range(2)]
        mine = [half for key in keys for half in planes[key]]
        sent = mine if token is None else after(mine, token)
        theirs = [self.core(half) for half in sent]
        return Pieces(self.depth, rows, mine[0].shape[-1], mine + theirs)

    def total(self, sums):
        halves = []
        for own, middle, last in sums:
            middle = middle[own.shape[0] :]
            halves.append(own.astype(f32) + middle.astype(f32) + last.astype(f32))
        return jnp.concatenate(halves, axis=0)


def local(
    tokens,
    w_q,
    w_kv,
    g_attn,
    g_mlp,
    w_o,
    w_gu,
    w_down,
    grad_out,
    grad_kv,
    group_id,
    group_size,
    group_weight,
):
    grid = Grid(lax.axis_size("dp"), lax.axis_size("fsdp"))
    length, width = tokens.shape
    kv_width = w_kv.shape[1]
    head_dim = kv_width // 2
    q_width = w_q.shape[1]
    shard_rows = w_q.shape[0]
    hidden_rows = w_down.shape[0]
    half = length // 2

    matches = jnp.arange(group_size.shape[0], dtype=jnp.int32) == group_id[0]
    factor = jnp.sum(jnp.where(matches, group_weight / group_size.astype(jnp.float32), 0.0))
    grad_low = (grad_out.astype(jnp.float32) * factor).astype(jnp.bfloat16)
    cosines, sines = rope_tables(length, head_dim)

    plane_keys = ((0, 0), (1, 0), (0, 1), (1, 1))

    def in_order(planes):
        return [piece for key in plane_keys for piece in planes[key]]

    gains = jnp.stack([g_attn, g_mlp], axis=1)
    w_in = jnp.concatenate([w_q, w_kv, jnp.pad(gains, ((0, 0), (0, lanes - 2)))], axis=1)
    w_in_column = grid.gather_outer(w_in)
    w_o_column = grid.gather_outer(w_o)
    grad_first = grid.spread_first(grad_low[:half], grad_low[half:])
    pairs = jnp.swapaxes(w_gu, 0, 1).reshape(2 * hidden_rows, width)
    gu_mine = grid.gather_outer(pairs)
    grad_planes = grid.spread_second(*grad_first)
    grad_rows = in_order(grad_planes)
    cut = grid.depth // 2
    w_in_column = after(w_in_column, grad_planes[1, 1]).reshape(grid.depth, shard_rows, -1)
    in_planes = grid.spread_second(*grid.spread_first(w_in_column[:cut], w_in_column[cut:]))
    in_pieces = grid.pieces(in_planes, shard_rows)
    down_mine = grid.gather_outer(w_down)
    w_o_column = after(w_o_column, in_planes[1, 1]).reshape(grid.depth, shard_rows, -1)
    o_first = grid.spread_first(w_o_column[:cut], w_o_column[cut:])
    h_turned, q_low, kv_out, gain_rows = project(
        grid.spot, tokens, cosines, sines, in_pieces, q_width, kv_width, head_dim
    )
    o_planes = grid.spread_second(*after(o_first, q_low))
    prob, attended, turned = attend(grid.spot, q_low, kv_out, grid.depth, shard_rows)
    o_pieces = grid.pieces(o_planes, shard_rows, attended)
    x_mid, h_first, h_second = mix(grid.spot, tokens, attended, gain_rows, o_pieces)

    ff_rows = in_order(grid.spread_second(*grid.spread_first(h_first, h_second)))
    gu_mine = after(gu_mine, ff_rows)
    by_shard = hidden_rows % 8 == 0
    run_rows = hidden_rows if by_shard else grid.depth * hidden_rows

    def turn(both, rows):
        return both.reshape(-1, rows, hidden_rows, width).swapaxes(0, 1).reshape(both.shape)

    if not by_shard:
        gu_mine = turn(gu_mine, 2)
    gu_other = grid.core(gu_mine)
    hid_mine, *scales_mine = gate(ff_rows, gu_mine, run_rows)
    hid_other, *scales_other = gate(ff_rows, gu_other, run_rows, [hid_mine])
    runs = grid.depth if by_shard else 1
    sent = hidden_sums([hid_other], grad_rows, run_rows, runs)
    down_sum = hidden_sums([hid_mine], grad_rows, run_rows, runs, grid.cores(sent), [sent[0]])
    down_sum, down_mine = lax.optimization_barrier((down_sum, down_mine))
    d_w_down = grid.scatter_outer(down_sum)
    down_other = grid.core(down_mine)
    pair_mine = gate_back(grad_rows, down_mine, scales_mine)
    pair_other = gate_back(grad_rows, down_other, scales_other, [pair_mine[0]])
    d_h_parts = rows_back((*pair_mine, *pair_other), (gu_mine, gu_other), run_rows)
    sent = hidden_sums(pair_other, ff_rows, run_rows, 2*runs, late=[d_h_parts[0]])
    d_h_passed = grid.collect_first(d_h_parts, [sent[0]])
    pair_sum = hidden_sums(
        pair_mine, ff_rows, run_rows, 2*runs, grid.cores(sent), [d_h_passed[0]]
    )
    pair_sum, d_w_down = lax.optimization_barrier((pair_sum, d_w_down))
    d_w_gu = grid.scatter_outer(pair_sum if by_shard else turn(pair_sum, grid.depth))
    d_h_first, d_h_second = grid.collect_second(d_h_parts, d_h_passed)
    d_h_sums = [*d_h_first, *d_h_second]

    d_mid, d_mid_low, gain_two_sum = norm_back(
        factor.reshape(1), x_mid, gain_rows, grad_out, d_h_sums, [pair_sum]
    )
    sent = send_sums(turned, d_mid_low)
    o_parts = keep_sums(turned, d_mid_low, grid.cores(sent))
    joined, d_kv = attend_back(
        grid.spot, factor.reshape(1), d_mid_low, grad_kv, q_low, kv_out,
        prob, cosines, sines, o_pieces, [o_parts[0]],
    )
    o_passed = grid.collect_first(o_parts, [joined])
    sent = send_sums(h_turned, joined, [o_passed[0]])
    d_w_o = grid.total(grid.collect_second(o_parts, o_passed)).astype(bf16)
    d_w_o = grid.scatter_outer(d_w_o).astype(f32)
    in_parts = keep_sums(h_turned, joined, grid.cores(sent), [o_passed[0]])
    d_tokens, gain_one_sum = finish(
        grid.spot, tokens, gain_rows, joined, d_mid, in_pieces, [in_parts[0]]
    )
    in_passed = grid.collect_first(in_parts, [gain_one_sum, d_w_gu])
    d_w_in = grid.total(grid.collect_second(in_parts, in_passed)).astype(bf16)
    if by_shard:
        d_w_gu = alternate(d_w_gu)
    else:
        d_w_gu = jnp.stack([d_w_gu[:hidden_rows], d_w_gu[hidden_rows:]], axis=1).astype(f32)
    d_w_down = d_w_down.astype(f32)
    mlp_parts = down((hid_mine, hid_other), (down_mine, down_other), [in_passed[0]])
    d_w_in, mlp_parts = lax.optimization_barrier((d_w_in, mlp_parts))
    mlp_sum = grid.total(grid.collect_second(mlp_parts, grid.collect_first(mlp_parts)))
    output = (x_mid + mlp_sum).astype(jnp.bfloat16)
    gain_sums = jnp.stack([gain_one_sum[0], gain_two_sum[0]], axis=0)
    gain_sums = grid.plane_sum(gain_sums)
    own_gains = lax.dynamic_slice(
        gain_sums.reshape(2, grid.dp, grid.depth, 2, shard_rows),
        (0, grid.dp_index, 0, grid.y, 0),
        (2, 1, grid.depth, 1, shard_rows),
    ).reshape(2, grid.depth * shard_rows)
    extra = jnp.pad(own_gains.T, ((0, 0), (0, lanes - 2))).astype(bf16)
    d_w_in = grid.scatter_outer(jnp.concatenate([d_w_in, extra], axis=1))
    return (
        output,
        d_tokens,
        kv_out,
        d_kv,
        d_w_in[:, :q_width].astype(f32),
        d_w_in[:, q_width : q_width + kv_width].astype(f32),
        d_w_in[:, q_width + kv_width].astype(f32),
        d_w_in[:, q_width + kv_width + 1].astype(f32),
        d_w_o,
        d_w_gu,
        d_w_down,
    )


def solution(mesh):
    placed = (
        P(("dp", "fsdp"), None),
        P(("dp", "fsdp"), None),
        P(("dp", "fsdp"), None),
        P(("dp", "fsdp")),
        P(("dp", "fsdp")),
        P(("dp", "fsdp"), None),
        P(("dp", "fsdp"), None, None),
        P(("dp", "fsdp"), None),
        P(("dp", "fsdp"), None),
        P(("dp", "fsdp"), None),
        P(("dp", "fsdp")),
        P(),
        P(),
    )
    return jax.shard_map(
        local,
        mesh=mesh,
        in_specs=placed,
        out_specs=(
            P(("dp", "fsdp"), None),
            P(("dp", "fsdp"), None),
            P(("dp", "fsdp"), None),
            P(("dp", "fsdp"), None),
            P(("dp", "fsdp"), None),
            P(("dp", "fsdp"), None),
            P(("dp", "fsdp")),
            P(("dp", "fsdp")),
            P(("dp", "fsdp"), None),
            P(("dp", "fsdp"), None, None),
            P(("dp", "fsdp"), None),
        ),
        check_vma=False,
    )
```

```python
import functools

import jax
import jax.numpy as jnp
from jax import lax
from jax.experimental import pallas as pl
from jax.experimental.pallas import tpu as pltpu
from jax.sharding import PartitionSpec as P

epsilon = 1e-05
theta_base = 10000.0
bf16 = jnp.bfloat16
f32 = jnp.float32
lanes = 128
step = 256
vmem_limit = 60 * 1024 * 1024


def rope_tables(length, width):
    halfway = width // 2
    freqs = theta_base ** (-(jnp.arange(halfway, dtype=jnp.float32) * 2.0 / width))
    angles = jnp.arange(length, dtype=jnp.float32)[:, None] * freqs[None, :]
    cosines, sine_part = jnp.cos(angles), jnp.sin(angles)
    return (
        jnp.concatenate([cosines, cosines], axis=1),
        jnp.concatenate([-sine_part, sine_part], axis=1),
    )


def contract(left, right, left_axis, right_axis):
    return lax.dot_general(
        left, right, (((left_axis,), (right_axis,)), ((), ())), preferred_element_type=jnp.float32
    )


def contract_last(left, right):
    return contract(left, right, left.ndim - 1, right.ndim - 1)


def contract_first(left, right):
    return contract(left, right, 0, 0)


def after(value, token):
    value, _ = lax.optimization_barrier((value, token))
    return value


def vmem_spec():
    return pl.BlockSpec(memory_space=pltpu.VMEM)


def any_spec():
    return pl.BlockSpec(memory_space=pl.ANY)


def smem_spec():
    return pl.BlockSpec(memory_space=pltpu.SMEM)


def kernel_call(body, out_shapes, scratch, in_specs, out_spec=vmem_spec):
    def run(*operands):
        known, late = len(in_specs), len(operands) - len(in_specs)

        def whole_body(*refs):
            body(*refs[:known], *refs[known + late :])

        return pl.pallas_call(
            whole_body,
            out_shape=out_shapes,
            in_specs=in_specs + [any_spec()] * late,
            out_specs=jax.tree.map(lambda _: out_spec(), out_shapes),
            scratch_shapes=scratch,
            compiler_params=pltpu.CompilerParams(vmem_limit_bytes=vmem_limit),
            cost_estimate=pl.CostEstimate(flops=1, bytes_accessed=1, transcendentals=0),
            name=getattr(body, "func", body).__name__[: -len("_body")],
        )(*operands)

    return run


def route(keys):
    place = {(key, half): 2 * i + half for i, key in enumerate(keys) for half in range(2)}
    own, x, y, both = (0, 0), (1, 0), (0, 1), (1, 1)
    return (
        (place[own, 0],),
        (place[own, 1],),
        (place[x, 0],),
        (place[y, 1],),
        (place[both, 1], place[x, 1]),
        (place[both, 0], place[y, 0]),
    )


row_route = route(((0, 0), (1, 0), (0, 1), (1, 1)))
column_route = route(((0, 0), (0, 1), (1, 0), (1, 1)))


def routed(size, columns):
    return tuple(
        jax.ShapeDtypeStruct((size * len(blocks), columns), bf16) for blocks in row_route
    )


def send_blocks(way, outs, held, index, size, sem):
    for blocks, out in zip(way, outs):
        for spot, place in enumerate(blocks):

            @pl.when(index == place // 2)
            def _():
                pltpu.make_async_copy(
                    held.at[pl.ds(place * size, size)], out.at[pl.ds(spot * size, size)], sem
                ).start()


def wait_all(whole, sem):
    pltpu.make_async_copy(whole, whole, sem).wait()


class Pieces:
    def __init__(self, depth, rows, columns, arrays):
        self.depth, self.rows, self.columns, self.arrays = depth, rows, columns, arrays

    def start(self, refs, spot, whole, sem, apart=False):
        cut = self.depth // 2
        place = 0
        for flip in range(2):
            for dx in range(2):
                for dy in range(2):
                    for low, high in ((0, cut), (cut, self.depth)):
                        for outer in range(low, high):
                            block = (
                                (spot[0] ^ (2 * dx + flip)) * self.depth + outer
                            ) * 2 + (spot[1] ^ dy)
                            row = pl.multiple_of(block * self.rows, self.rows)
                            pltpu.make_async_copy(
                                refs[place].at[outer - low],
                                whole.at[pl.ds(row, self.rows)],
                                sem.at[2 * dx + flip] if apart else sem,
                            ).start()
                        place += 1

    def wait(self, whole, sem):
        pltpu.make_async_copy(whole, whole, sem).wait()

    def group(self, whole, spot, index):
        flip = (index % 2) * 2 + index // 2
        size = whole.shape[0] // 4
        return pl.multiple_of((spot[0] ^ flip) * size, size), size, flip


def swap_halves(value):
    return pltpu.roll(value, value.shape[-1] // 2, 1)


def relative_place(block, spot, depth):
    side = block % 2
    outer = (block // 2) % depth
    flips = (block // (2 * depth)) ^ spot[0]
    return (((flips % 2) * 2 + flips // 2) * 2 + (side ^ spot[1])) * depth + outer


def put_in_order(source, target, spot, depth, rows):
    @pl.loop(0, source.shape[0] // rows)
    def _(block):
        place = pl.multiple_of(relative_place(block, spot, depth) * rows, rows)
        target[pl.ds(place, rows), :] = source[pl.ds(pl.multiple_of(block * rows, rows), rows), :]


def project_body(pieces, q_width, kv_width, head_dim, *refs):
    count = len(pieces.arrays)
    spot, tokens, cosines, sines = refs[:4]
    shards = refs[4 : 4 + count]
    h_turned, q_out, kv_out, gain_out = refs[4 + count : 8 + count]
    whole, h_low, flat, sem = refs[8 + count :]
    pieces.start(shards, spot, whole, sem)
    width = tokens.shape[1]
    x_full = tokens[...].astype(f32)
    inverse = lax.rsqrt(jnp.mean(x_full * x_full, axis=-1, keepdims=True) + epsilon)
    pieces.wait(whole, sem)
    pick = (
        lax.broadcasted_iota(jnp.int32, (8, lanes), 0) == lax.broadcasted_iota(jnp.int32, (8, lanes), 1)
    ).astype(bf16)
    gains = contract_last(pick, whole[:, q_width + kv_width :])
    gain_out[...] = gains
    h_low[...] = (x_full * inverse * gains[0:1]).astype(bf16)
    cos, sin = cosines[...], sines[...]
    kv_pre = jnp.dot(h_low[...], whole[:, q_width : q_width + kv_width], preferred_element_type=f32)
    key_part = kv_pre[:, :head_dim]
    kv_out[:, :head_dim] = (key_part * cos + swap_halves(key_part) * sin).astype(bf16)
    kv_out[:, head_dim:] = kv_pre[:, head_dim:].astype(bf16)

    @pl.loop(0, q_width // step)
    def _(block):
        start = pl.multiple_of(block * step, step)
        q_pre = jnp.dot(h_low[...], whole[:, pl.ds(start, step)], preferred_element_type=f32)
        for head in range(step // head_dim):
            own = q_pre[:, head * head_dim : (head + 1) * head_dim]
            column = pl.multiple_of(start + head * head_dim, head_dim)
            q_out[:, pl.ds(column, head_dim)] = (own * cos + swap_halves(own) * sin).astype(bf16)

    @pl.loop(0, width // step)
    def _(block):
        start = pl.multiple_of(block * step, step)
        flat[pl.ds(start, step), :] = h_low[:, pl.ds(start, step)].T

    put_in_order(flat, h_turned, spot, pieces.depth, pieces.rows)


def project(spot, tokens, cosines, sines, pieces, q_width, kv_width, head_dim, late=()):
    length, width = tokens.shape
    count = len(pieces.arrays)
    shape = jax.ShapeDtypeStruct
    return kernel_call(
        functools.partial(project_body, pieces, q_width, kv_width, head_dim),
        (
            shape((width, length), bf16),
            shape((length, q_width), bf16),
            shape((length, kv_width), bf16),
            shape((8, width), f32),
        ),
        [
            pltpu.VMEM((width, pieces.columns), bf16),
            pltpu.VMEM((length, width), bf16),
            pltpu.VMEM((width, length), bf16),
            pltpu.SemaphoreType.DMA,
        ],
        [smem_spec(), vmem_spec(), vmem_spec(), vmem_spec()] + [any_spec()] * count,
    )(spot, tokens, cosines, sines, *pieces.arrays, *late)


def attend_body(depth, rows, head_dim, spot, q_low, kv_low, prob_out, attended_out, turned, flat):
    length, q_width = q_low.shape
    scale = head_dim ** (-0.5)
    keys = kv_low[:, :head_dim]
    values_turned = kv_low[:, head_dim:].T
    allowed = lax.broadcasted_iota(jnp.int32, (length, length), 0) <= lax.broadcasted_iota(
        jnp.int32, (length, length), 1
    )
    heads = step // head_dim

    @pl.loop(0, q_width // step)
    def _(block):
        for head in range(heads):
            column = pl.multiple_of(block * step + head * head_dim, head_dim)
            queries = q_low[:, pl.ds(column, head_dim)]
            logits = jnp.where(allowed, contract_last(keys, queries) * scale, -1e30)
            exp_vals = jnp.exp(logits - jnp.max(logits, axis=0, keepdims=True))
            prob = (exp_vals / jnp.sum(exp_vals, axis=0, keepdims=True)).astype(bf16)
            prob_out[block * heads + head] = prob
            mixed = jnp.dot(values_turned, prob, preferred_element_type=f32)
            flat[pl.ds(column, head_dim), :] = mixed.astype(bf16)
            attended_out[:, pl.ds(column, head_dim)] = mixed.T.astype(bf16)

    put_in_order(flat, turned, spot, depth, rows)


def attend(spot, q_low, kv_low, depth, rows, late=()):
    length, q_width = q_low.shape
    head_dim = kv_low.shape[1] // 2
    shape = jax.ShapeDtypeStruct
    return kernel_call(
        functools.partial(attend_body, depth, rows, head_dim),
        (
            shape((q_width // head_dim, length, length), bf16),
            shape((length, q_width), bf16),
            shape((q_width, length), bf16),
        ),
        [pltpu.VMEM((q_width, length), bf16)],
        [smem_spec(), vmem_spec(), vmem_spec()],
    )(spot, q_low, kv_low, *late)


def mix_body(pieces, *refs):
    count = len(pieces.arrays)
    spot, tokens, attended, gains = refs[:4]
    shards = refs[4 : 4 + count]
    mid_out, first_out, second_out = refs[4 + count : 7 + count]
    whole, sem = refs[7 + count :]
    pieces.start(shards, spot, whole, sem, True)
    length, width = tokens.shape
    mid_out[...] = tokens[...].astype(f32)

    @pl.loop(0, 4)
    def _(index):
        row, size, flip = pieces.group(whole, spot, index)
        rows = pl.ds(row, size)
        wait_all(whole.at[rows], sem.at[flip])

        @pl.loop(0, width // (2 * step))
        def _(block):
            columns = pl.ds(pl.multiple_of(block * 2 * step, 2 * step), 2 * step)
            mid_out[:, columns] += jnp.dot(
                attended[:, rows], whole[rows, columns], preferred_element_type=f32
            )

    x_mid = mid_out[...]
    inverse = lax.rsqrt(jnp.mean(x_mid * x_mid, axis=-1, keepdims=True) + epsilon)
    h_two = (x_mid * inverse * gains[1:2, :]).astype(bf16)
    first_out[...] = h_two[: length // 2]
    second_out[...] = h_two[length // 2 :]


def mix(spot, tokens, attended, gains, pieces, late=()):
    length, width = tokens.shape
    shape = jax.ShapeDtypeStruct
    half = shape((length // 2, width), bf16)
    rows = attended.shape[1]
    return kernel_call(
        functools.partial(mix_body, pieces),
        (shape((length, width), f32), half, half),
        [pltpu.VMEM((rows, width), bf16), pltpu.SemaphoreType.DMA((4,))],
        [smem_spec(), vmem_spec(), vmem_spec(), vmem_spec()] + [any_spec()] * len(pieces.arrays),
    )(spot, tokens, attended, gains, *pieces.arrays, *late)


def norm_back_body(factor, gains, mid, grad_out, *refs):
    sums, outs = refs[:6], refs[6:9]
    mid_in, grad_in, own, middle, last, d_mid_held, low_held, gain_held = refs[9:17]
    in_sems, out_sem = refs[17], refs[18]
    length = mid.shape[0]
    half = length // 2
    blocks = in_sems.shape[0]
    size = length // blocks

    @pl.loop(0, blocks)
    def _(block):
        rows = pl.ds(pl.multiple_of(block * size, size), size)
        for source, target in ((mid, mid_in), (grad_out, grad_in)):
            pltpu.make_async_copy(source.at[rows], target.at[rows], in_sems.at[block]).start()
        for part in range(2):

            @pl.when(block // (blocks // 2) == part)
            def _():
                start = pl.multiple_of((block - part * (blocks // 2)) * size, size)
                for source, target, skip in zip(sums[3 * part :], (own, middle, last), (0, half, 0)):
                    pltpu.make_async_copy(
                        source.at[pl.ds(skip + start, size)], target.at[rows], in_sems.at[block]
                    ).start()

    gain = gains[1:2, :]
    gain_held[...] = jnp.zeros_like(gain_held)

    @pl.loop(0, blocks)
    def _(block):
        rows = pl.ds(pl.multiple_of(block * size, size), size)
        for held in (mid_in, grad_in, own, middle, last):
            wait_all(held.at[rows], in_sems.at[block])
        d_h = own[rows, :].astype(f32) + middle[rows, :].astype(f32) + last[rows, :].astype(f32)
        x_mid = mid_in[rows, :]
        inverse = lax.rsqrt(jnp.mean(x_mid * x_mid, axis=-1, keepdims=True) + epsilon)
        normed = x_mid * inverse
        product = d_h * normed
        gain_held[0:1, :] += jnp.sum(product, axis=0, keepdims=True)
        mean = jnp.mean(product * gain, axis=-1, keepdims=True)
        grad_top = grad_in[rows, :].astype(f32) * factor[0]
        d_mid = grad_top + inverse * (d_h * gain - normed * mean)
        d_mid_held[rows, :] = d_mid
        low_held[rows, :] = d_mid.astype(bf16)
        for held, target in zip((d_mid_held, low_held), outs):
            pltpu.make_async_copy(held.at[rows], target.at[rows], out_sem).start()

    pltpu.make_async_copy(gain_held, outs[2], out_sem).start()
    for held in (d_mid_held, low_held, gain_held):
        wait_all(held, out_sem)


def norm_back(factor, mid, gains, grad_out, sums, late=()):
    length, width = mid.shape
    shape = jax.ShapeDtypeStruct
    whole = pltpu.VMEM((length, width), bf16)
    wide = pltpu.VMEM((length, width), f32)
    return kernel_call(
        norm_back_body,
        (shape((length, width), f32), shape((length, width), bf16), shape((8, width), f32)),
        [wide, whole, whole, whole, whole, wide, whole, pltpu.VMEM((8, width), f32)]
        + [pltpu.SemaphoreType.DMA((8,)), pltpu.SemaphoreType.DMA],
        [smem_spec(), vmem_spec()] + [any_spec()] * 8,
        any_spec,
    )(factor, gains, mid, grad_out, *sums, *late)


def attend_back_body(pieces, head_dim, *refs):
    count = len(pieces.arrays)
    (spot, factor, d_mid_low, grad_kv, q_low, kv_low, prob_ref, cosines, sines) = refs[:9]
    shards = refs[9 : 9 + count]
    joined, d_kv_out = refs[9 + count : 11 + count]
    whole, sem = refs[11 + count :]
    pieces.start(shards, spot, whole, sem, True)
    length = d_mid_low.shape[0]
    q_width = q_low.shape[1]
    scale = head_dim ** (-0.5)
    cos, sin = cosines[...], sines[...]
    keys, values = kv_low[:, :head_dim], kv_low[:, head_dim:]
    d_kv_out[...] = grad_kv[...].astype(f32) * factor[0]
    heads = step // head_dim

    @pl.loop(0, q_width // step)
    def _(block):
        row, size, flip = pieces.group(whole, spot, block // (whole.shape[0] // 4 // step))
        inside = block % (size // step)

        @pl.when(inside == 0)
        def _():
            wait_all(whole.at[pl.ds(row, size)], sem.at[flip])

        start = pl.multiple_of(row + inside * step, step)
        d_att = contract_last(d_mid_low[...], whole[pl.ds(start, step), :]).astype(bf16)
        d_k = jnp.zeros((length, head_dim), f32)
        d_v = jnp.zeros((length, head_dim), f32)
        for head in range(heads):
            own = d_att[:, head * head_dim : (head + 1) * head_dim]
            column = pl.multiple_of(start + head * head_dim, head_dim)
            low = prob_ref[start // head_dim + head]
            prob = low.astype(f32)
            d_prob = contract_last(values, own)
            centre = jnp.sum(prob * d_prob, axis=0, keepdims=True)
            d_raw = (prob * (d_prob - centre) * scale).astype(bf16)
            d_v += jnp.dot(low, own, preferred_element_type=f32)
            d_k += jnp.dot(d_raw, q_low[:, pl.ds(column, head_dim)], preferred_element_type=f32)
            d_q = contract_first(d_raw, keys)
            joined[:, pl.ds(column, head_dim)] = (d_q * cos - swap_halves(d_q) * sin).astype(bf16)
        d_kv_out[:, :head_dim] += d_k
        d_kv_out[:, head_dim:] += d_v

    d_k = d_kv_out[:, :head_dim]
    joined[:, q_width : q_width + head_dim] = (d_k * cos - swap_halves(d_k) * sin).astype(bf16)
    joined[:, q_width + head_dim :] = d_kv_out[:, head_dim:].astype(bf16)


def attend_back(spot, factor, d_mid_low, grad_kv, q_low, kv_low, prob, cosines, sines, pieces, late=()):
    length, width = d_mid_low.shape
    q_width, kv_width = q_low.shape[1], kv_low.shape[1]
    head_dim = kv_width // 2
    shape = jax.ShapeDtypeStruct
    return kernel_call(
        functools.partial(attend_back_body, pieces, head_dim),
        (shape((length, q_width + kv_width), bf16), shape((length, kv_width), f32)),
        [pltpu.VMEM((q_width, width), bf16), pltpu.SemaphoreType.DMA((4,))],
        [smem_spec()] * 2 + [vmem_spec()] * 7 + [any_spec()] * len(pieces.arrays),
    )(spot, factor, d_mid_low, grad_kv, q_low, kv_low, prob, cosines, sines, *pieces.arrays, *late)


def finish_body(pieces, *refs):
    count = len(pieces.arrays)
    spot, tokens, gains, joined, d_mid = refs[:5]
    shards = refs[5 : 5 + count]
    d_tokens, gain_out = refs[5 + count : 7 + count]
    whole, sem = refs[7 + count :]
    pieces.start(shards, spot, whole, sem)
    length, width = tokens.shape
    used = joined.shape[1]
    x_full = tokens[...].astype(f32)
    inverse = lax.rsqrt(jnp.mean(x_full * x_full, axis=-1, keepdims=True) + epsilon)
    pieces.wait(whole, sem)

    def add(block, total):
        start = pl.multiple_of(block * step, step)
        columns = pl.ds(start, step)
        d_h = contract_last(joined[...], whole[columns, :used])
        normed = tokens[:, columns].astype(f32) * inverse
        gain_out[:, columns] = jnp.broadcast_to(
            jnp.sum(d_h * normed, axis=0, keepdims=True), (8, step)
        )
        d_normed = d_h * gains[0:1, columns]
        d_tokens[:, columns] = d_normed
        return total + jnp.sum(d_normed * normed, axis=-1, keepdims=True)

    total = lax.fori_loop(0, width // step, add, jnp.zeros((length, 1), f32))
    d_tokens[...] = d_mid[...] + inverse * (d_tokens[...] - x_full * inverse * (total / width))


def finish(spot, tokens, gains, joined, d_mid, pieces, late=()):
    length, width = tokens.shape
    shape = jax.ShapeDtypeStruct
    return kernel_call(
        functools.partial(finish_body, pieces),
        (shape((length, width), f32), shape((8, width), f32)),
        [pltpu.VMEM((width, pieces.columns), bf16), pltpu.SemaphoreType.DMA],
        [smem_spec()] + [vmem_spec()] * 4 + [any_spec()] * len(pieces.arrays),
    )(spot, tokens, gains, joined, d_mid, *pieces.arrays, *late)


def fetch_rows(parts, whole, sem):
    start = 0
    for part in parts:
        pltpu.make_async_copy(part, whole.at[pl.ds(start, part.shape[0])], sem).start()
        start += part.shape[0]
    return pltpu.make_async_copy(whole, whole, sem).wait


def fetch_gate_up(both, shard, first, second, first_sem, second_sem):
    waits = []
    for place, (whole, sem) in enumerate(((first, first_sem), (second, second_sem))):
        for outer in range(both.shape[0] // (2 * shard)):
            source = both.at[pl.ds((2 * outer + place) * shard, shard)]
            pltpu.make_async_copy(source, whole.at[pl.ds(outer * shard, shard)], sem).start()
        waits.append(pltpu.make_async_copy(whole, whole, sem).wait)
    return waits


def fetch_row_blocks(parts, whole, sems):
    size = parts[0].shape[0]
    for place, part in enumerate(parts):
        sem = sems.at[place * size // step]
        pltpu.make_async_copy(part, whole.at[pl.ds(place * size, size)], sem).start()


def gate_body(shard, count, *refs):
    parts, both, outs = refs[:count], refs[count], refs[count + 1 : count + 4]
    held, refs = refs[count + 4 : count + 7], refs[count + 7 :]
    rows, gate_w, up_w, row_sems, gate_sem, up_sem, out_sem = refs
    waits = fetch_gate_up(both, shard, gate_w, up_w, gate_sem, up_sem)
    fetch_row_blocks(parts, rows, row_sems)
    for wait in waits:
        wait()

    @pl.loop(0, rows.shape[0] // step)
    def _(block):
        own = pl.ds(pl.multiple_of(block * step, step), step)
        wait_all(rows.at[own], row_sems.at[block])
        gate = contract_last(rows[own, :], gate_w[...])
        up = contract_last(rows[own, :], up_w[...])
        sigma = 1.0 / (1.0 + jnp.exp(-gate))
        silu = gate * sigma
        held[0][own, :] = (silu * up).astype(bf16)
        held[1][own, :] = (up * sigma * (1.0 + gate * (1.0 - sigma))).astype(bf16)
        held[2][own, :] = silu.astype(bf16)
        for source, out in zip(held, outs):
            pltpu.make_async_copy(source.at[own], out.at[own], out_sem).start()

    for source in held:
        wait_all(source, out_sem)


def gate(parts, both, shard, late=()):
    total, width = sum(part.shape[0] for part in parts), parts[0].shape[1]
    hidden = both.shape[0] // 2
    out = jax.ShapeDtypeStruct((total, hidden), bf16)
    return kernel_call(
        functools.partial(gate_body, shard, len(parts)),
        (out, out, out),
        [pltpu.VMEM((total, hidden), bf16)] * 3
        + [pltpu.VMEM((total, width), bf16)]
        + [pltpu.VMEM((hidden, width), bf16)] * 2
        + [pltpu.SemaphoreType.DMA((total // step,))]
        + [pltpu.SemaphoreType.DMA] * 3,
        [any_spec()] * (len(parts) + 1),
        any_spec,
    )(*parts, both, *late)


def gate_back_body(count, *refs):
    parts, weight, scales, grads = refs[:count], refs[count], refs[count + 1 : count + 3], refs[count + 3 : count + 5]
    rows, weight_in, first, second, row_sems, weight_sem, out_sem = refs[count + 5 :]
    wait = fetch_rows([weight], weight_in, weight_sem)
    scaled = (first, second)
    for source, held in zip(scales, scaled):
        for block in range(rows.shape[0] // step):
            own = pl.ds(block * step, step)
            pltpu.make_async_copy(source.at[own], held.at[own], row_sems.at[block]).start()
    fetch_row_blocks(parts, rows, row_sems)
    wait()

    @pl.loop(0, rows.shape[0] // step)
    def _(block):
        own = pl.ds(pl.multiple_of(block * step, step), step)
        for whole in (rows, first, second):
            wait_all(whole.at[own], row_sems.at[block])
        d_hid = contract_last(rows[own, :], weight_in[...])
        for held, grad in zip(scaled, grads):
            held[own, :] = (d_hid * held[own, :].astype(f32)).astype(bf16)
            pltpu.make_async_copy(held.at[own], grad.at[own], out_sem).start()

    for held in scaled:
        wait_all(held, out_sem)


def gate_back(parts, weight, scales, late=()):
    count = len(parts)
    total, width = sum(part.shape[0] for part in parts), parts[0].shape[1]
    hidden = weight.shape[0]
    grad = jax.ShapeDtypeStruct((total, hidden), bf16)
    return kernel_call(
        functools.partial(gate_back_body, count),
        (grad, grad),
        [pltpu.VMEM((total, width), bf16), pltpu.VMEM((hidden, width), bf16)]
        + [pltpu.VMEM((total, hidden), bf16)] * 2
        + [pltpu.SemaphoreType.DMA((total // step,))]
        + [pltpu.SemaphoreType.DMA] * 2,
        [any_spec()] * (count + 3),
        any_spec,
    )(*parts, weight, *scales, *late)


def rows_back_body(shard, *refs):
    grads, boths, outs = refs[:4], refs[4:6], refs[6:12]
    weights, held, sems, out_sem = refs[12:16], refs[16], refs[17], refs[18]
    size, chunk = held.shape[0] // 8, 2 * step
    chunks = held.shape[1] // chunk

    @pl.loop(0, chunks)
    def _(block):
        columns = pl.ds(pl.multiple_of(block * chunk, chunk), chunk)
        for place, weight in enumerate(weights):
            for outer in range(weight.shape[0] // shard):
                source = boths[place // 2].at[pl.ds((2 * outer + place % 2) * shard, shard), columns]
                target = weight.at[pl.ds(outer * shard, shard), columns]
                pltpu.make_async_copy(source, target, sems.at[block]).start()

    @pl.loop(0, chunks)
    def _(block):
        columns = pl.ds(pl.multiple_of(block * chunk, chunk), chunk)
        for weight in weights:
            wait_all(weight.at[:, columns], sems.at[block])

        @pl.loop(0, 4)
        def _(index):
            own = pl.ds(pl.multiple_of(index * 2 * size, 2 * size), 2 * size)
            total = jnp.dot(grads[0][own, :], weights[0][:, columns], preferred_element_type=f32)
            for grad, piece in zip(grads[1:], weights[1:]):
                total += jnp.dot(grad[own, :], piece[:, columns], preferred_element_type=f32)
            held[own, columns] = total.astype(bf16)

        for blocks, out in zip(row_route, outs):
            for spot, place in enumerate(blocks):
                source = held.at[pl.ds(place * size, size), columns]
                target = out.at[pl.ds(spot * size, size), columns]
                pltpu.make_async_copy(source, target, out_sem).start()

    wait_all(held, out_sem)


def rows_back(grads, boths, shard, late=()):
    total, hidden = grads[0].shape
    width = boths[0].shape[1]
    return kernel_call(
        functools.partial(rows_back_body, shard),
        routed(total // 8, width),
        [pltpu.VMEM((hidden, width), bf16)] * 4
        + [
            pltpu.VMEM((total, width), bf16),
            pltpu.SemaphoreType.DMA((width // (2 * step),)),
            pltpu.SemaphoreType.DMA,
        ],
        [vmem_spec()] * 4 + [any_spec()] * 2,
        any_spec,
    )(*grads, *boths, *late)


def down_body(*refs):
    hids, downs, outs, held, sem = refs[:2], refs[2:4], refs[4:10], refs[10], refs[11]
    size = held.shape[0] // 8

    @pl.loop(0, 4)
    def _(index):
        own = pl.ds(pl.multiple_of(index * 2 * size, 2 * size), 2 * size)
        total = jnp.dot(hids[0][own, :], downs[0][...], preferred_element_type=f32)
        total += jnp.dot(hids[1][own, :], downs[1][...], preferred_element_type=f32)
        held[own, :] = total.astype(bf16)
        send_blocks(row_route, outs, held, index, size, sem)

    wait_all(held, sem)


def down(hids, downs, late=()):
    total, width = hids[0].shape[0], downs[0].shape[1]
    return kernel_call(
        down_body,
        routed(total // 8, width),
        [pltpu.VMEM((total, width), bf16), pltpu.SemaphoreType.DMA],
        [vmem_spec()] * 4,
        any_spec,
    )(*hids, *downs, *late)


def hidden_sums_body(count, pairs, shard, pieces, received, *refs):
    lefts, parts = refs[:pairs], refs[pairs : pairs + count]
    others = refs[pairs + count : pairs + count + pieces * received]
    refs = refs[pairs + count + pieces * received :]
    if received:
        refs, arrived, other_sem, out_sem = refs[:-3], refs[-3], refs[-2], refs[-1]
    outs, turned, rows, sem = refs[: -pairs - 2], refs[-pairs - 2 : -2], refs[-2], refs[-1]
    waits = [fetch_rows(parts, rows, sem)]
    if received:
        waits.append(fetch_rows(others, arrived, other_sem))

    @pl.loop(0, rows.shape[0] // step)
    def _(block):
        own = pl.ds(pl.multiple_of(block * step, step), step)
        for left, flat in zip(lefts, turned):
            flat[:, own] = left[own, :].T

    for wait in waits:
        wait()

    @pl.loop(0, rows.shape[1] // step)
    def _(block):
        columns = pl.ds(pl.multiple_of(block * step, step), step)
        for place, flat in enumerate(turned):
            product = jnp.dot(flat[...], rows[:, columns], preferred_element_type=f32)
            for outer in range(flat.shape[0] // shard):
                start = (pairs * outer + place) * shard
                own = product[outer * shard : (outer + 1) * shard]
                if received:
                    here = pl.ds(start, shard)
                    arrived[here, columns] = (own + arrived[here, columns].astype(f32)).astype(bf16)
                else:
                    piece, row = start // outs[0].shape[0], start % outs[0].shape[0]
                    outs[piece][row : row + shard, columns] = own.astype(bf16)
        if received:
            pltpu.make_async_copy(
                arrived.at[:, columns], outs[0].at[:, columns], out_sem
            ).start()

    if received:
        wait_all(arrived, out_sem)


def hidden_sums(lefts, parts, shard, pieces, others=None, late=()):
    total, width = lefts[0].shape[0], parts[0].shape[1]
    hidden = lefts[0].shape[1] * len(lefts)
    received = others is not None
    count = 1 if received else pieces
    scratch = [pltpu.VMEM((left.shape[1], total), bf16) for left in lefts]
    scratch += [pltpu.VMEM((total, width), bf16), pltpu.SemaphoreType.DMA]
    if received:
        scratch += [pltpu.VMEM((hidden, width), bf16)] + [pltpu.SemaphoreType.DMA] * 2
    outs = kernel_call(
        functools.partial(hidden_sums_body, len(parts), len(lefts), shard, pieces, received),
        (jax.ShapeDtypeStruct((hidden // count, width), bf16),) * count,
        scratch,
        [vmem_spec()] * len(lefts) + [any_spec()] * (len(parts) + pieces * received),
        any_spec if received else vmem_spec,
    )(*lefts, *parts, *(others or ()), *late)
    return outs[0] if received else outs


def send_sums_body(turned, right, first, second, held, sem):
    middle = turned.shape[0] // 2
    size = middle // 4

    @pl.loop(0, 4)
    def _(index):
        start = pl.multiple_of(index * size, size)
        own = turned[pl.ds(middle + start, size), :]
        held[pl.ds(start, size), :] = jnp.dot(own, right[...], preferred_element_type=f32).astype(bf16)
        for place, out in enumerate((first, first, second, second)):

            @pl.when(index == place)
            def _():
                target = out.at[pl.ds((place % 2) * size, size)]
                pltpu.make_async_copy(held.at[pl.ds(place * size, size)], target, sem).start()

    wait_all(held, sem)


def send_sums(turned, right, late=()):
    rows, columns = turned.shape[0] // 2, right.shape[1]
    return kernel_call(
        send_sums_body,
        (jax.ShapeDtypeStruct((rows // 2, columns), bf16),) * 2,
        [pltpu.VMEM((rows, columns), bf16), pltpu.SemaphoreType.DMA],
        [vmem_spec()] * 2,
        any_spec,
    )(turned, right, *late)


def keep_sums_body(turned, right, first, second, *refs):
    outs, arrived, held, in_sems, out_sem = refs[:6], refs[6], refs[7], refs[8], refs[9]
    size = turned.shape[0] // 16
    for place, part in enumerate((first, first, second, second)):
        source = part.at[pl.ds((place % 2) * 2 * size, 2 * size)]
        target = arrived.at[pl.ds(place * 2 * size, 2 * size)]
        pltpu.make_async_copy(source, target, in_sems.at[place]).start()

    @pl.loop(0, 4)
    def _(index):
        own = pl.ds(pl.multiple_of(index * 2 * size, 2 * size), 2 * size)
        product = jnp.dot(turned[own, :], right[...], preferred_element_type=f32)
        wait_all(arrived.at[own], in_sems.at[index])
        held[own, :] = (product + arrived[own, :].astype(f32)).astype(bf16)
        send_blocks(column_route, outs, held, index, size, out_sem)

    wait_all(held, out_sem)


def keep_sums(turned, right, others, late=()):
    rows, columns = turned.shape[0] // 2, right.shape[1]
    return kernel_call(
        keep_sums_body,
        routed(rows // 8, columns),
        [pltpu.VMEM((rows, columns), bf16)] * 2
        + [pltpu.SemaphoreType.DMA((4,)), pltpu.SemaphoreType.DMA],
        [vmem_spec()] * 2 + [any_spec()] * 2,
        any_spec,
    )(turned, right, *others, *late)


def alternate_body(both, out):
    rows = out.shape[0]

    @pl.loop(0, rows // 8)
    def _(block):
        start = pl.multiple_of(block * 8, 8)
        for place in range(2):
            out[pl.ds(start, 8), place, :] = both[pl.ds(place * rows + start, 8), :].astype(f32)


def alternate(both):
    rows, columns = both.shape[0] // 2, both.shape[1]
    out = jax.ShapeDtypeStruct((rows, 2, columns), f32)
    return kernel_call(alternate_body, out, [], [vmem_spec()])(both)


def widen_body(rows, first, second, gain_one, gain_two):
    columns, more = first.shape[1], second.shape[1]
    first[...] = rows[:, :columns].astype(f32)
    second[...] = rows[:, columns : columns + more].astype(f32)
    turned = rows[:, columns + more :].astype(f32).T
    gain_one[...] = turned[0:1, :]
    gain_two[...] = turned[1:2, :]


def widen(rows, first, second):
    shape = jax.ShapeDtypeStruct
    size = rows.shape[0]
    outs = (
        shape((size, first), f32),
        shape((size, second), f32),
        shape((1, size), f32),
        shape((1, size), f32),
    )
    *wide, gain_one, gain_two = kernel_call(widen_body, outs, [], [vmem_spec()])(rows)
    return *wide, gain_one.reshape(size), gain_two.reshape(size)


def pass_body(keep_x, keep_y, from_x, from_y, for_x, for_y, *refs):
    held, in_sems, out_sem = refs[:4], refs[4], refs[5]
    blocks = in_sems.shape[0]
    size = keep_x.shape[0] // blocks

    @pl.loop(0, blocks)
    def _(block):
        rows = pl.ds(pl.multiple_of(block * size, size), size)
        for source, target in zip((keep_x, from_y, keep_y, from_x), held):
            pltpu.make_async_copy(source.at[rows], target.at[rows], in_sems.at[block]).start()

    @pl.loop(0, blocks)
    def _(block):
        rows = pl.ds(pl.multiple_of(block * size, size), size)
        for target in held:
            wait_all(target.at[rows], in_sems.at[block])
        for keep, come, out in ((held[0], held[1], for_x), (held[2], held[3], for_y)):
            keep[rows, :] = (keep[rows, :].astype(f32) + come[rows, :].astype(f32)).astype(bf16)
            pltpu.make_async_copy(keep.at[rows], out.at[rows], out_sem).start()

    wait_all(held[0], out_sem)
    wait_all(held[2], out_sem)


def pass_on(keep_x, keep_y, from_x, from_y, late=()):
    out = jax.ShapeDtypeStruct(keep_x.shape, bf16)
    return kernel_call(
        pass_body,
        (out, out),
        [pltpu.VMEM(keep_x.shape, bf16)] * 4
        + [pltpu.SemaphoreType.DMA((4,)), pltpu.SemaphoreType.DMA],
        [any_spec()] * 4,
        any_spec,
    )(keep_x, keep_y, from_x, from_y, *late)


class Grid:
    def __init__(self, dp, fsdp):
        self.dp, self.fsdp = dp, fsdp
        self.depth = fsdp // 2
        self.groups = [[f for f in range(fsdp) if f % 2 == y] for y in range(2)]
        self.dp_index = lax.axis_index("dp")
        self.y = lax.axis_index("fsdp") % 2
        self.spot = jnp.stack([self.dp_index, self.y]).astype(jnp.int32)
        self.outer = lax.axis_index("fsdp") // 2

    def core(self, value):
        return lax.ppermute(value, "dp", [(i, i ^ 1) for i in range(self.dp)])

    def cores(self, values):
        return [self.core(value) for value in values]

    def echo(self, value, times):
        for _ in range(times):
            value = self.core(value)
        return value

    def x_swap(self, value):
        return lax.ppermute(value, "dp", [(i, i ^ 2) for i in range(self.dp)])

    def y_swap(self, value):
        return lax.ppermute(value, "fsdp", [(i, i ^ 1) for i in range(self.fsdp)])

    def plane_sum(self, value):
        value = value + self.core(value)
        pairs = [
            (dp * self.fsdp + f, (dp ^ 2) * self.fsdp + (f ^ 1))
            for dp in range(self.dp)
            for f in range(self.fsdp)
        ]
        across = lax.ppermute(value, ("dp", "fsdp"), pairs)
        return value + self.x_swap(value) + self.y_swap(value) + across

    def shift(self, value, low, high, by):
        pairs = [
            (2 * outer + y, 2 * (outer + by) + y) for outer in range(low, high) for y in range(2)
        ]
        return lax.ppermute(value, "fsdp", pairs)

    def gather_outer(self, value):
        return lax.all_gather(value, "fsdp", axis=0, tiled=True, axis_index_groups=self.groups)

    def scatter_outer(self, value):
        return lax.psum_scatter(
            value, "fsdp", scatter_dimension=0, tiled=True, axis_index_groups=self.groups
        )

    def spread_first(self, first, second):
        return first, second, self.x_swap(first), self.y_swap(second)

    def spread_second(self, first, second, first_x, second_y):
        first, second, first_x, second_y = lax.optimization_barrier(
            (first, second, first_x, second_y)
        )
        first_xy = self.y_swap(first_x)
        second_xy = self.x_swap(second_y)
        first_y = self.y_swap(first)
        second_x = self.x_swap(second)
        return {
            (0, 0): (first, second),
            (1, 0): (first_x, second_x),
            (0, 1): (first_y, second_y),
            (1, 1): (first_xy, second_xy),
        }

    def collect_first(self, parts, late=()):
        _, _, keep_x, keep_y, to_x, to_y = parts
        from_x, from_y = self.x_swap(to_x), self.y_swap(to_y)
        return (*pass_on(keep_x, keep_y, from_x, from_y, late), from_x, from_y)

    def collect_second(self, parts, passed):
        for_x, for_y, from_x, from_y = passed
        return (parts[0], from_y, self.x_swap(for_x)), (parts[1], from_x, self.y_swap(for_y))

    def pieces(self, planes, rows, token=None):
        keys = [(dx, dy) for dx in range(2) for dy in range(2)]
        mine = [half for key in keys for half in planes[key]]
        sent = mine if token is None else after(mine, token)
        theirs = [self.core(half) for half in sent]
        return Pieces(self.depth, rows, mine[0].shape[-1], mine + theirs)

    def total(self, sums):
        halves = []
        for own, middle, last in sums:
            middle = middle[own.shape[0] :]
            halves.append(own.astype(f32) + middle.astype(f32) + last.astype(f32))
        return jnp.concatenate(halves, axis=0)


def local(
    tokens,
    w_q,
    w_kv,
    g_attn,
    g_mlp,
    w_o,
    w_gu,
    w_down,
    grad_out,
    grad_kv,
    group_id,
    group_size,
    group_weight,
):
    grid = Grid(lax.axis_size("dp"), lax.axis_size("fsdp"))
    length, width = tokens.shape
    kv_width = w_kv.shape[1]
    head_dim = kv_width // 2
    q_width = w_q.shape[1]
    shard_rows = w_q.shape[0]
    hidden_rows = w_down.shape[0]
    half = length // 2

    matches = jnp.arange(group_size.shape[0], dtype=jnp.int32) == group_id[0]
    factor = jnp.sum(jnp.where(matches, group_weight / group_size.astype(jnp.float32), 0.0))
    grad_low = (grad_out.astype(jnp.float32) * factor).astype(jnp.bfloat16)
    cosines, sines = rope_tables(length, head_dim)

    plane_keys = ((0, 0), (1, 0), (0, 1), (1, 1))

    def in_order(planes):
        return [piece for key in plane_keys for piece in planes[key]]

    gains = jnp.stack([g_attn, g_mlp], axis=1)
    w_in = jnp.concatenate([w_q, w_kv, jnp.pad(gains, ((0, 0), (0, lanes - 2)))], axis=1)
    w_in_column = grid.gather_outer(w_in)
    w_o_column = grid.gather_outer(w_o)
    grad_first = grid.spread_first(grad_low[:half], grad_low[half:])
    pairs = jnp.swapaxes(w_gu, 0, 1).reshape(2 * hidden_rows, width)
    gu_mine = grid.gather_outer(pairs)
    grad_planes = grid.spread_second(*grad_first)
    grad_rows = in_order(grad_planes)
    cut = grid.depth // 2
    w_in_column = after(w_in_column, grad_planes[1, 1]).reshape(grid.depth, shard_rows, -1)
    in_planes = grid.spread_second(*grid.spread_first(w_in_column[:cut], w_in_column[cut:]))
    in_pieces = grid.pieces(in_planes, shard_rows)
    down_mine = grid.gather_outer(w_down)
    w_o_column = after(w_o_column, in_planes[1, 1]).reshape(grid.depth, shard_rows, -1)
    o_first = grid.spread_first(w_o_column[:cut], w_o_column[cut:])
    h_turned, q_low, kv_out, gain_rows = project(
        grid.spot, tokens, cosines, sines, in_pieces, q_width, kv_width, head_dim
    )
    o_planes = grid.spread_second(*after(o_first, q_low))
    prob, attended, turned = attend(grid.spot, q_low, kv_out, grid.depth, shard_rows)
    o_pieces = grid.pieces(o_planes, shard_rows, attended)
    x_mid, h_first, h_second = mix(grid.spot, tokens, attended, gain_rows, o_pieces)

    ff_rows = in_order(grid.spread_second(*grid.spread_first(h_first, h_second)))
    gu_mine = after(gu_mine, ff_rows)
    by_shard = hidden_rows % 8 == 0
    run_rows = hidden_rows if by_shard else grid.depth * hidden_rows

    def turn(both, rows):
        return both.reshape(-1, rows, hidden_rows, width).swapaxes(0, 1).reshape(both.shape)

    if not by_shard:
        gu_mine = turn(gu_mine, 2)
    gu_other = grid.core(gu_mine)
    hid_mine, *scales_mine = gate(ff_rows, gu_mine, run_rows)
    hid_other, *scales_other = gate(ff_rows, gu_other, run_rows, [hid_mine])
    runs = grid.depth if by_shard else 1
    sent = hidden_sums([hid_other], grad_rows, run_rows, runs)
    down_sum = hidden_sums([hid_mine], grad_rows, run_rows, runs, grid.cores(sent), [sent[0]])
    down_sum, down_mine = lax.optimization_barrier((down_sum, down_mine))
    d_w_down = grid.scatter_outer(down_sum)
    down_other = grid.core(down_mine)
    pair_mine = gate_back(grad_rows, down_mine, scales_mine)
    pair_other = gate_back(grad_rows, down_other, scales_other, [pair_mine[0]])
    d_h_parts = rows_back((*pair_mine, *pair_other), (gu_mine, gu_other), run_rows)
    sent = hidden_sums(pair_other, ff_rows, run_rows, 2*runs, late=[d_h_parts[0]])
    d_h_passed = grid.collect_first(d_h_parts, [sent[0]])
    pair_sum = hidden_sums(
        pair_mine, ff_rows, run_rows, 2*runs, grid.cores(sent), [d_h_passed[0]]
    )
    pair_sum, d_w_down = lax.optimization_barrier((pair_sum, d_w_down))
    d_w_gu = grid.scatter_outer(pair_sum if by_shard else turn(pair_sum, grid.depth))
    d_h_first, d_h_second = grid.collect_second(d_h_parts, d_h_passed)
    d_h_sums = [*d_h_first, *d_h_second]

    d_mid, d_mid_low, gain_two_sum = norm_back(
        factor.reshape(1), x_mid, gain_rows, grad_out, d_h_sums, [pair_sum]
    )
    sent = send_sums(turned, d_mid_low)
    o_parts = keep_sums(turned, d_mid_low, grid.cores(sent))
    joined, d_kv = attend_back(
        grid.spot, factor.reshape(1), d_mid_low, grad_kv, q_low, kv_out,
        prob, cosines, sines, o_pieces, [o_parts[0]],
    )
    o_passed = grid.collect_first(o_parts, [joined])
    sent = send_sums(h_turned, joined, [o_passed[0]])
    d_w_o = grid.total(grid.collect_second(o_parts, o_passed)).astype(bf16)
    d_w_o = grid.scatter_outer(d_w_o).astype(f32)
    in_parts = keep_sums(h_turned, joined, grid.cores(sent), [o_passed[0]])
    d_tokens, gain_one_sum = finish(
        grid.spot, tokens, gain_rows, joined, d_mid, in_pieces, [in_parts[0]]
    )
    in_passed = grid.collect_first(in_parts, [gain_one_sum, d_w_gu])
    d_w_in = grid.total(grid.collect_second(in_parts, in_passed)).astype(bf16)
    if by_shard:
        d_w_gu = alternate(d_w_gu)
    else:
        d_w_gu = jnp.stack([d_w_gu[:hidden_rows], d_w_gu[hidden_rows:]], axis=1).astype(f32)
    d_w_down = d_w_down.astype(f32)
    mlp_parts = down((hid_mine, hid_other), (down_mine, down_other), [in_passed[0]])
    d_w_in, mlp_parts = lax.optimization_barrier((d_w_in, mlp_parts))
    mlp_sum = grid.total(grid.collect_second(mlp_parts, grid.collect_first(mlp_parts)))
    output = (x_mid + mlp_sum).astype(jnp.bfloat16)
    gain_sums = jnp.stack([gain_one_sum[0], gain_two_sum[0]], axis=0)
    gain_sums = grid.plane_sum(gain_sums)
    own_gains = lax.dynamic_slice(
        gain_sums.reshape(2, grid.dp, grid.depth, 2, shard_rows),
        (0, grid.dp_index, 0, grid.y, 0),
        (2, 1, grid.depth, 1, shard_rows),
    ).reshape(2, grid.depth * shard_rows)
    extra = jnp.pad(own_gains.T, ((0, 0), (0, lanes - 2))).astype(bf16)
    d_w_in = grid.scatter_outer(jnp.concatenate([d_w_in, extra], axis=1))
    return (
        output,
        d_tokens,
        kv_out,
        d_kv,
        *widen(d_w_in, q_width, kv_width),
        d_w_o,
        d_w_gu,
        d_w_down,
    )


def solution(mesh):
    placed = (
        P(("dp", "fsdp"), None),
        P(("dp", "fsdp"), None),
        P(("dp", "fsdp"), None),
        P(("dp", "fsdp")),
        P(("dp", "fsdp")),
        P(("dp", "fsdp"), None),
        P(("dp", "fsdp"), None, None),
        P(("dp", "fsdp"), None),
        P(("dp", "fsdp"), None),
        P(("dp", "fsdp"), None),
        P(("dp", "fsdp")),
        P(),
        P(),
    )
    return jax.shard_map(
        local,
        mesh=mesh,
        in_specs=placed,
        out_specs=(
            P(("dp", "fsdp"), None),
            P(("dp", "fsdp"), None),
            P(("dp", "fsdp"), None),
            P(("dp", "fsdp"), None),
            P(("dp", "fsdp"), None),
            P(("dp", "fsdp"), None),
            P(("dp", "fsdp")),
            P(("dp", "fsdp")),
            P(("dp", "fsdp"), None),
            P(("dp", "fsdp"), None, None),
            P(("dp", "fsdp"), None),
        ),
        check_vma=False,
    )
```

```python
import functools

import jax
import jax.numpy as jnp
from jax import lax
from jax.experimental import pallas as pl
from jax.experimental.pallas import tpu as pltpu
from jax.sharding import PartitionSpec as P

epsilon = 1e-05
theta_base = 10000.0
bf16 = jnp.bfloat16
f32 = jnp.float32
lanes = 128
step = 256
vmem_limit = 60 * 1024 * 1024


def rope_tables(length, width):
    halfway = width // 2
    freqs = theta_base ** (-(jnp.arange(halfway, dtype=jnp.float32) * 2.0 / width))
    angles = jnp.arange(length, dtype=jnp.float32)[:, None] * freqs[None, :]
    cosines, sine_part = jnp.cos(angles), jnp.sin(angles)
    return (
        jnp.concatenate([cosines, cosines], axis=1),
        jnp.concatenate([-sine_part, sine_part], axis=1),
    )


def contract(left, right, left_axis, right_axis):
    return lax.dot_general(
        left, right, (((left_axis,), (right_axis,)), ((), ())), preferred_element_type=jnp.float32
    )


def contract_last(left, right):
    return contract(left, right, left.ndim - 1, right.ndim - 1)


def contract_first(left, right):
    return contract(left, right, 0, 0)


def after(value, token):
    value, _ = lax.optimization_barrier((value, token))
    return value


def vmem_spec():
    return pl.BlockSpec(memory_space=pltpu.VMEM)


def any_spec():
    return pl.BlockSpec(memory_space=pl.ANY)


def smem_spec():
    return pl.BlockSpec(memory_space=pltpu.SMEM)


def kernel_call(body, out_shapes, scratch, in_specs, out_spec=vmem_spec):
    def run(*operands):
        known, late = len(in_specs), len(operands) - len(in_specs)

        def whole_body(*refs):
            body(*refs[:known], *refs[known + late :])

        return pl.pallas_call(
            whole_body,
            out_shape=out_shapes,
            in_specs=in_specs + [any_spec()] * late,
            out_specs=jax.tree.map(lambda _: out_spec(), out_shapes),
            scratch_shapes=scratch,
            compiler_params=pltpu.CompilerParams(vmem_limit_bytes=vmem_limit),
            cost_estimate=pl.CostEstimate(flops=1, bytes_accessed=1, transcendentals=0),
            name=getattr(body, "func", body).__name__[: -len("_body")],
        )(*operands)

    return run


def route(keys):
    place = {(key, half): 2 * i + half for i, key in enumerate(keys) for half in range(2)}
    own, x, y, both = (0, 0), (1, 0), (0, 1), (1, 1)
    return (
        (place[own, 0],),
        (place[own, 1],),
        (place[x, 0],),
        (place[y, 1],),
        (place[both, 1], place[x, 1]),
        (place[both, 0], place[y, 0]),
    )


row_route = route(((0, 0), (1, 0), (0, 1), (1, 1)))
column_route = route(((0, 0), (0, 1), (1, 0), (1, 1)))


def routed(size, columns):
    return tuple(
        jax.ShapeDtypeStruct((size * len(blocks), columns), bf16) for blocks in row_route
    )


def send_blocks(way, outs, held, index, size, sem):
    for blocks, out in zip(way, outs):
        for spot, place in enumerate(blocks):

            @pl.when(index == place // 2)
            def _():
                pltpu.make_async_copy(
                    held.at[pl.ds(place * size, size)], out.at[pl.ds(spot * size, size)], sem
                ).start()


def wait_all(whole, sem):
    pltpu.make_async_copy(whole, whole, sem).wait()


class Pieces:
    def __init__(self, depth, rows, columns, arrays):
        self.depth, self.rows, self.columns, self.arrays = depth, rows, columns, arrays

    def start(self, refs, spot, whole, sem, apart=False):
        cut = self.depth // 2
        place = 0
        for flip in range(2):
            for dx in range(2):
                for dy in range(2):
                    for low, high in ((0, cut), (cut, self.depth)):
                        for outer in range(low, high):
                            block = (
                                (spot[0] ^ (2 * dx + flip)) * self.depth + outer
                            ) * 2 + (spot[1] ^ dy)
                            row = pl.multiple_of(block * self.rows, self.rows)
                            pltpu.make_async_copy(
                                refs[place].at[outer - low],
                                whole.at[pl.ds(row, self.rows)],
                                sem.at[2 * dx + flip] if apart else sem,
                            ).start()
                        place += 1

    def wait(self, whole, sem):
        pltpu.make_async_copy(whole, whole, sem).wait()

    def group(self, whole, spot, index):
        flip = (index % 2) * 2 + index // 2
        size = whole.shape[0] // 4
        return pl.multiple_of((spot[0] ^ flip) * size, size), size, flip


def swap_halves(value):
    return pltpu.roll(value, value.shape[-1] // 2, 1)


def relative_place(block, spot, depth):
    side = block % 2
    outer = (block // 2) % depth
    flips = (block // (2 * depth)) ^ spot[0]
    return (((flips % 2) * 2 + flips // 2) * 2 + (side ^ spot[1])) * depth + outer


def put_in_order(source, target, spot, depth, rows):
    @pl.loop(0, source.shape[0] // rows)
    def _(block):
        place = pl.multiple_of(relative_place(block, spot, depth) * rows, rows)
        target[pl.ds(place, rows), :] = source[pl.ds(pl.multiple_of(block * rows, rows), rows), :]


def project_body(pieces, q_width, kv_width, head_dim, *refs):
    count = len(pieces.arrays)
    spot, tokens, cosines, sines = refs[:4]
    shards = refs[4 : 4 + count]
    h_low, q_out, kv_out, gain_out = refs[4 + count : 8 + count]
    whole, sem = refs[8 + count :]
    pieces.start(shards, spot, whole, sem)
    width = tokens.shape[1]
    x_full = tokens[...].astype(f32)
    inverse = lax.rsqrt(jnp.mean(x_full * x_full, axis=-1, keepdims=True) + epsilon)
    pieces.wait(whole, sem)
    pick = (
        lax.broadcasted_iota(jnp.int32, (8, lanes), 0) == lax.broadcasted_iota(jnp.int32, (8, lanes), 1)
    ).astype(bf16)
    gains = contract_last(pick, whole[:, q_width + kv_width :])
    gain_out[...] = gains
    h_low[...] = (x_full * inverse * gains[0:1]).astype(bf16)
    cos, sin = cosines[...], sines[...]
    kv_pre = jnp.dot(h_low[...], whole[:, q_width : q_width + kv_width], preferred_element_type=f32)
    key_part = kv_pre[:, :head_dim]
    kv_out[:, :head_dim] = (key_part * cos + swap_halves(key_part) * sin).astype(bf16)
    kv_out[:, head_dim:] = kv_pre[:, head_dim:].astype(bf16)

    @pl.loop(0, q_width // step)
    def _(block):
        start = pl.multiple_of(block * step, step)
        q_pre = jnp.dot(h_low[...], whole[:, pl.ds(start, step)], preferred_element_type=f32)
        for head in range(step // head_dim):
            own = q_pre[:, head * head_dim : (head + 1) * head_dim]
            column = pl.multiple_of(start + head * head_dim, head_dim)
            q_out[:, pl.ds(column, head_dim)] = (own * cos + swap_halves(own) * sin).astype(bf16)


def project(spot, tokens, cosines, sines, pieces, q_width, kv_width, head_dim, late=()):
    length, width = tokens.shape
    count = len(pieces.arrays)
    shape = jax.ShapeDtypeStruct
    return kernel_call(
        functools.partial(project_body, pieces, q_width, kv_width, head_dim),
        (
            shape((length, width), bf16),
            shape((length, q_width), bf16),
            shape((length, kv_width), bf16),
            shape((8, width), f32),
        ),
        [
            pltpu.VMEM((width, pieces.columns), bf16),
            pltpu.SemaphoreType.DMA,
        ],
        [smem_spec(), vmem_spec(), vmem_spec(), vmem_spec()] + [any_spec()] * count,
    )(spot, tokens, cosines, sines, *pieces.arrays, *late)


def attend_body(depth, rows, head_dim, *refs):
    spot, q_low, kv_low, h_low, prob_out, attended_out, turned, h_turned, flat = refs
    length, q_width = q_low.shape
    scale = head_dim ** (-0.5)
    keys = kv_low[:, :head_dim]
    values_turned = kv_low[:, head_dim:].T
    allowed = lax.broadcasted_iota(jnp.int32, (length, length), 0) <= lax.broadcasted_iota(
        jnp.int32, (length, length), 1
    )
    heads = step // head_dim

    @pl.loop(0, q_width // step)
    def _(block):
        for head in range(heads):
            column = pl.multiple_of(block * step + head * head_dim, head_dim)
            queries = q_low[:, pl.ds(column, head_dim)]
            logits = jnp.where(allowed, contract_last(keys, queries) * scale, -1e30)
            exp_vals = jnp.exp(logits - jnp.max(logits, axis=0, keepdims=True))
            prob = (exp_vals / jnp.sum(exp_vals, axis=0, keepdims=True)).astype(bf16)
            prob_out[block * heads + head] = prob
            mixed = jnp.dot(values_turned, prob, preferred_element_type=f32)
            flat[pl.ds(column, head_dim), :] = mixed.astype(bf16)
            attended_out[:, pl.ds(column, head_dim)] = mixed.T.astype(bf16)

    put_in_order(flat.at[pl.ds(0, q_width)], turned, spot, depth, rows)

    @pl.loop(0, h_low.shape[1] // step)
    def _(block):
        start = pl.multiple_of(block * step, step)
        flat[pl.ds(start, step), :] = h_low[:, pl.ds(start, step)].T

    put_in_order(flat.at[pl.ds(0, h_turned.shape[0])], h_turned, spot, depth, rows)


def attend(spot, q_low, kv_low, h_low, depth, rows, late=()):
    length, q_width = q_low.shape
    head_dim = kv_low.shape[1] // 2
    shape = jax.ShapeDtypeStruct
    return kernel_call(
        functools.partial(attend_body, depth, rows, head_dim),
        (
            shape((q_width // head_dim, length, length), bf16),
            shape((length, q_width), bf16),
            shape((q_width, length), bf16),
            shape((h_low.shape[1], length), bf16),
        ),
        [pltpu.VMEM((max(q_width, h_low.shape[1]), length), bf16)],
        [smem_spec(), vmem_spec(), vmem_spec(), vmem_spec()],
    )(spot, q_low, kv_low, h_low, *late)


def mix_body(pieces, *refs):
    count = len(pieces.arrays)
    spot, tokens, attended, gains = refs[:4]
    shards = refs[4 : 4 + count]
    mid_out, first_out, second_out = refs[4 + count : 7 + count]
    whole, sem = refs[7 + count :]
    pieces.start(shards, spot, whole, sem, True)
    length, width = tokens.shape
    mid_out[...] = tokens[...].astype(f32)

    @pl.loop(0, 4)
    def _(index):
        row, size, flip = pieces.group(whole, spot, index)
        rows = pl.ds(row, size)
        wait_all(whole.at[rows], sem.at[flip])

        @pl.loop(0, width // (2 * step))
        def _(block):
            columns = pl.ds(pl.multiple_of(block * 2 * step, 2 * step), 2 * step)
            mid_out[:, columns] += jnp.dot(
                attended[:, rows], whole[rows, columns], preferred_element_type=f32
            )

    x_mid = mid_out[...]
    inverse = lax.rsqrt(jnp.mean(x_mid * x_mid, axis=-1, keepdims=True) + epsilon)
    h_two = (x_mid * inverse * gains[1:2, :]).astype(bf16)
    first_out[...] = h_two[: length // 2]
    second_out[...] = h_two[length // 2 :]


def mix(spot, tokens, attended, gains, pieces, late=()):
    length, width = tokens.shape
    shape = jax.ShapeDtypeStruct
    half = shape((length // 2, width), bf16)
    rows = attended.shape[1]
    return kernel_call(
        functools.partial(mix_body, pieces),
        (shape((length, width), f32), half, half),
        [pltpu.VMEM((rows, width), bf16), pltpu.SemaphoreType.DMA((4,))],
        [smem_spec(), vmem_spec(), vmem_spec(), vmem_spec()] + [any_spec()] * len(pieces.arrays),
    )(spot, tokens, attended, gains, *pieces.arrays, *late)


def norm_back_body(factor, gains, mid, grad_out, *refs):
    sums, outs = refs[:6], refs[6:9]
    mid_in, grad_in, own, middle, last, d_mid_held, low_held, gain_held = refs[9:17]
    in_sems, out_sem = refs[17], refs[18]
    length = mid.shape[0]
    half = length // 2
    blocks = in_sems.shape[0]
    size = length // blocks

    @pl.loop(0, blocks)
    def _(block):
        rows = pl.ds(pl.multiple_of(block * size, size), size)
        for source, target in ((mid, mid_in), (grad_out, grad_in)):
            pltpu.make_async_copy(source.at[rows], target.at[rows], in_sems.at[block]).start()
        for part in range(2):

            @pl.when(block // (blocks // 2) == part)
            def _():
                start = pl.multiple_of((block - part * (blocks // 2)) * size, size)
                for source, target, skip in zip(sums[3 * part :], (own, middle, last), (0, half, 0)):
                    pltpu.make_async_copy(
                        source.at[pl.ds(skip + start, size)], target.at[rows], in_sems.at[block]
                    ).start()

    gain = gains[1:2, :]
    gain_held[...] = jnp.zeros_like(gain_held)

    @pl.loop(0, blocks)
    def _(block):
        rows = pl.ds(pl.multiple_of(block * size, size), size)
        for held in (mid_in, grad_in, own, middle, last):
            wait_all(held.at[rows], in_sems.at[block])
        d_h = own[rows, :].astype(f32) + middle[rows, :].astype(f32) + last[rows, :].astype(f32)
        x_mid = mid_in[rows, :]
        inverse = lax.rsqrt(jnp.mean(x_mid * x_mid, axis=-1, keepdims=True) + epsilon)
        normed = x_mid * inverse
        product = d_h * normed
        gain_held[0:1, :] += jnp.sum(product, axis=0, keepdims=True)
        mean = jnp.mean(product * gain, axis=-1, keepdims=True)
        grad_top = grad_in[rows, :].astype(f32) * factor[0]
        d_mid = grad_top + inverse * (d_h * gain - normed * mean)
        d_mid_held[rows, :] = d_mid
        low_held[rows, :] = d_mid.astype(bf16)
        for held, target in zip((d_mid_held, low_held), outs):
            pltpu.make_async_copy(held.at[rows], target.at[rows], out_sem).start()

    pltpu.make_async_copy(gain_held, outs[2], out_sem).start()
    for held in (d_mid_held, low_held, gain_held):
        wait_all(held, out_sem)


def norm_back(factor, mid, gains, grad_out, sums, late=()):
    length, width = mid.shape
    shape = jax.ShapeDtypeStruct
    whole = pltpu.VMEM((length, width), bf16)
    wide = pltpu.VMEM((length, width), f32)
    return kernel_call(
        norm_back_body,
        (shape((length, width), f32), shape((length, width), bf16), shape((8, width), f32)),
        [wide, whole, whole, whole, whole, wide, whole, pltpu.VMEM((8, width), f32)]
        + [pltpu.SemaphoreType.DMA((8,)), pltpu.SemaphoreType.DMA],
        [smem_spec(), vmem_spec()] + [any_spec()] * 8,
        any_spec,
    )(factor, gains, mid, grad_out, *sums, *late)


def attend_back_body(pieces, head_dim, *refs):
    count = len(pieces.arrays)
    (spot, factor, d_mid_low, grad_kv, q_low, kv_low, prob_ref, cosines, sines) = refs[:9]
    shards = refs[9 : 9 + count]
    joined, d_kv_out = refs[9 + count : 11 + count]
    whole, sem = refs[11 + count :]
    pieces.start(shards, spot, whole, sem, True)
    length = d_mid_low.shape[0]
    q_width = q_low.shape[1]
    scale = head_dim ** (-0.5)
    cos, sin = cosines[...], sines[...]
    keys, values = kv_low[:, :head_dim], kv_low[:, head_dim:]
    d_kv_out[...] = grad_kv[...].astype(f32) * factor[0]
    heads = step // head_dim

    @pl.loop(0, q_width // step)
    def _(block):
        row, size, flip = pieces.group(whole, spot, block // (whole.shape[0] // 4 // step))
        inside = block % (size // step)

        @pl.when(inside == 0)
        def _():
            wait_all(whole.at[pl.ds(row, size)], sem.at[flip])

        start = pl.multiple_of(row + inside * step, step)
        d_att = contract_last(d_mid_low[...], whole[pl.ds(start, step), :]).astype(bf16)
        d_k = jnp.zeros((length, head_dim), f32)
        d_v = jnp.zeros((length, head_dim), f32)
        for head in range(heads):
            own = d_att[:, head * head_dim : (head + 1) * head_dim]
            column = pl.multiple_of(start + head * head_dim, head_dim)
            low = prob_ref[start // head_dim + head]
            prob = low.astype(f32)
            d_prob = contract_last(values, own)
            centre = jnp.sum(prob * d_prob, axis=0, keepdims=True)
            d_raw = (prob * (d_prob - centre) * scale).astype(bf16)
            d_v += jnp.dot(low, own, preferred_element_type=f32)
            d_k += jnp.dot(d_raw, q_low[:, pl.ds(column, head_dim)], preferred_element_type=f32)
            d_q = contract_first(d_raw, keys)
            joined[:, pl.ds(column, head_dim)] = (d_q * cos - swap_halves(d_q) * sin).astype(bf16)
        d_kv_out[:, :head_dim] += d_k
        d_kv_out[:, head_dim:] += d_v

    d_k = d_kv_out[:, :head_dim]
    joined[:, q_width : q_width + head_dim] = (d_k * cos - swap_halves(d_k) * sin).astype(bf16)
    joined[:, q_width + head_dim :] = d_kv_out[:, head_dim:].astype(bf16)


def attend_back(spot, factor, d_mid_low, grad_kv, q_low, kv_low, prob, cosines, sines, pieces, late=()):
    length, width = d_mid_low.shape
    q_width, kv_width = q_low.shape[1], kv_low.shape[1]
    head_dim = kv_width // 2
    shape = jax.ShapeDtypeStruct
    return kernel_call(
        functools.partial(attend_back_body, pieces, head_dim),
        (shape((length, q_width + kv_width), bf16), shape((length, kv_width), f32)),
        [pltpu.VMEM((q_width, width), bf16), pltpu.SemaphoreType.DMA((4,))],
        [smem_spec()] * 2 + [vmem_spec()] * 7 + [any_spec()] * len(pieces.arrays),
    )(spot, factor, d_mid_low, grad_kv, q_low, kv_low, prob, cosines, sines, *pieces.arrays, *late)


def finish_body(pieces, *refs):
    count = len(pieces.arrays)
    spot, tokens, gains, joined, d_mid = refs[:5]
    shards = refs[5 : 5 + count]
    d_tokens, gain_out = refs[5 + count : 7 + count]
    whole, sem = refs[7 + count :]
    pieces.start(shards, spot, whole, sem)
    length, width = tokens.shape
    used = joined.shape[1]
    x_full = tokens[...].astype(f32)
    inverse = lax.rsqrt(jnp.mean(x_full * x_full, axis=-1, keepdims=True) + epsilon)
    pieces.wait(whole, sem)

    def add(block, total):
        start = pl.multiple_of(block * step, step)
        columns = pl.ds(start, step)
        d_h = contract_last(joined[...], whole[columns, :used])
        normed = tokens[:, columns].astype(f32) * inverse
        gain_out[:, columns] = jnp.broadcast_to(
            jnp.sum(d_h * normed, axis=0, keepdims=True), (8, step)
        )
        d_normed = d_h * gains[0:1, columns]
        d_tokens[:, columns] = d_normed
        return total + jnp.sum(d_normed * normed, axis=-1, keepdims=True)

    total = lax.fori_loop(0, width // step, add, jnp.zeros((length, 1), f32))
    d_tokens[...] = d_mid[...] + inverse * (d_tokens[...] - x_full * inverse * (total / width))


def finish(spot, tokens, gains, joined, d_mid, pieces, late=()):
    length, width = tokens.shape
    shape = jax.ShapeDtypeStruct
    return kernel_call(
        functools.partial(finish_body, pieces),
        (shape((length, width), f32), shape((8, width), f32)),
        [pltpu.VMEM((width, pieces.columns), bf16), pltpu.SemaphoreType.DMA],
        [smem_spec()] + [vmem_spec()] * 4 + [any_spec()] * len(pieces.arrays),
    )(spot, tokens, gains, joined, d_mid, *pieces.arrays, *late)


def fetch_rows(parts, whole, sem):
    start = 0
    for part in parts:
        pltpu.make_async_copy(part, whole.at[pl.ds(start, part.shape[0])], sem).start()
        start += part.shape[0]
    return pltpu.make_async_copy(whole, whole, sem).wait


def fetch_gate_up(both, shard, first, second, first_sem, second_sem):
    waits = []
    for place, (whole, sem) in enumerate(((first, first_sem), (second, second_sem))):
        for outer in range(both.shape[0] // (2 * shard)):
            source = both.at[pl.ds((2 * outer + place) * shard, shard)]
            pltpu.make_async_copy(source, whole.at[pl.ds(outer * shard, shard)], sem).start()
        waits.append(pltpu.make_async_copy(whole, whole, sem).wait)
    return waits


def fetch_row_blocks(parts, whole, sems):
    size = parts[0].shape[0]
    for place, part in enumerate(parts):
        sem = sems.at[place * size // step]
        pltpu.make_async_copy(part, whole.at[pl.ds(place * size, size)], sem).start()


def gate_body(shard, count, *refs):
    parts, both, outs = refs[:count], refs[count], refs[count + 1 : count + 4]
    held, refs = refs[count + 4 : count + 7], refs[count + 7 :]
    rows, gate_w, up_w, row_sems, gate_sem, up_sem, out_sem = refs
    waits = fetch_gate_up(both, shard, gate_w, up_w, gate_sem, up_sem)
    fetch_row_blocks(parts, rows, row_sems)
    for wait in waits:
        wait()

    @pl.loop(0, rows.shape[0] // step)
    def _(block):
        own = pl.ds(pl.multiple_of(block * step, step), step)
        wait_all(rows.at[own], row_sems.at[block])
        gate = contract_last(rows[own, :], gate_w[...])
        up = contract_last(rows[own, :], up_w[...])
        sigma = 1.0 / (1.0 + jnp.exp(-gate))
        silu = gate * sigma
        held[0][own, :] = (silu * up).astype(bf16)
        held[1][own, :] = (up * sigma * (1.0 + gate * (1.0 - sigma))).astype(bf16)
        held[2][own, :] = silu.astype(bf16)
        for source, out in zip(held, outs):
            pltpu.make_async_copy(source.at[own], out.at[own], out_sem).start()

    for source in held:
        wait_all(source, out_sem)


def gate(parts, both, shard, late=()):
    total, width = sum(part.shape[0] for part in parts), parts[0].shape[1]
    hidden = both.shape[0] // 2
    out = jax.ShapeDtypeStruct((total, hidden), bf16)
    return kernel_call(
        functools.partial(gate_body, shard, len(parts)),
        (out, out, out),
        [pltpu.VMEM((total, hidden), bf16)] * 3
        + [pltpu.VMEM((total, width), bf16)]
        + [pltpu.VMEM((hidden, width), bf16)] * 2
        + [pltpu.SemaphoreType.DMA((total // step,))]
        + [pltpu.SemaphoreType.DMA] * 3,
        [any_spec()] * (len(parts) + 1),
        any_spec,
    )(*parts, both, *late)


def gate_back_body(count, *refs):
    parts, weight, scales, grads = refs[:count], refs[count], refs[count + 1 : count + 3], refs[count + 3 : count + 5]
    rows, weight_in, first, second, row_sems, weight_sem, out_sem = refs[count + 5 :]
    wait = fetch_rows([weight], weight_in, weight_sem)
    scaled = (first, second)
    for source, held in zip(scales, scaled):
        for block in range(rows.shape[0] // step):
            own = pl.ds(block * step, step)
            pltpu.make_async_copy(source.at[own], held.at[own], row_sems.at[block]).start()
    fetch_row_blocks(parts, rows, row_sems)
    wait()

    @pl.loop(0, rows.shape[0] // step)
    def _(block):
        own = pl.ds(pl.multiple_of(block * step, step), step)
        for whole in (rows, first, second):
            wait_all(whole.at[own], row_sems.at[block])
        d_hid = contract_last(rows[own, :], weight_in[...])
        for held, grad in zip(scaled, grads):
            held[own, :] = (d_hid * held[own, :].astype(f32)).astype(bf16)
            pltpu.make_async_copy(held.at[own], grad.at[own], out_sem).start()

    for held in scaled:
        wait_all(held, out_sem)


def gate_back(parts, weight, scales, late=()):
    count = len(parts)
    total, width = sum(part.shape[0] for part in parts), parts[0].shape[1]
    hidden = weight.shape[0]
    grad = jax.ShapeDtypeStruct((total, hidden), bf16)
    return kernel_call(
        functools.partial(gate_back_body, count),
        (grad, grad),
        [pltpu.VMEM((total, width), bf16), pltpu.VMEM((hidden, width), bf16)]
        + [pltpu.VMEM((total, hidden), bf16)] * 2
        + [pltpu.SemaphoreType.DMA((total // step,))]
        + [pltpu.SemaphoreType.DMA] * 2,
        [any_spec()] * (count + 3),
        any_spec,
    )(*parts, weight, *scales, *late)


def rows_back_body(shard, *refs):
    grads, boths, outs = refs[:4], refs[4:6], refs[6:12]
    weights, held, sems, out_sem = refs[12:16], refs[16], refs[17], refs[18]
    size, chunk = held.shape[0] // 8, 2 * step
    chunks = held.shape[1] // chunk

    @pl.loop(0, chunks)
    def _(block):
        columns = pl.ds(pl.multiple_of(block * chunk, chunk), chunk)
        for place, weight in enumerate(weights):
            for outer in range(weight.shape[0] // shard):
                source = boths[place // 2].at[pl.ds((2 * outer + place % 2) * shard, shard), columns]
                target = weight.at[pl.ds(outer * shard, shard), columns]
                pltpu.make_async_copy(source, target, sems.at[block]).start()

    @pl.loop(0, chunks)
    def _(block):
        columns = pl.ds(pl.multiple_of(block * chunk, chunk), chunk)
        for weight in weights:
            wait_all(weight.at[:, columns], sems.at[block])

        @pl.loop(0, 4)
        def _(index):
            own = pl.ds(pl.multiple_of(index * 2 * size, 2 * size), 2 * size)
            total = jnp.dot(grads[0][own, :], weights[0][:, columns], preferred_element_type=f32)
            for grad, piece in zip(grads[1:], weights[1:]):
                total += jnp.dot(grad[own, :], piece[:, columns], preferred_element_type=f32)
            held[own, columns] = total.astype(bf16)

        for blocks, out in zip(row_route, outs):
            for spot, place in enumerate(blocks):
                source = held.at[pl.ds(place * size, size), columns]
                target = out.at[pl.ds(spot * size, size), columns]
                pltpu.make_async_copy(source, target, out_sem).start()

    wait_all(held, out_sem)


def rows_back(grads, boths, shard, late=()):
    total, hidden = grads[0].shape
    width = boths[0].shape[1]
    return kernel_call(
        functools.partial(rows_back_body, shard),
        routed(total // 8, width),
        [pltpu.VMEM((hidden, width), bf16)] * 4
        + [
            pltpu.VMEM((total, width), bf16),
            pltpu.SemaphoreType.DMA((width // (2 * step),)),
            pltpu.SemaphoreType.DMA,
        ],
        [vmem_spec()] * 4 + [any_spec()] * 2,
        any_spec,
    )(*grads, *boths, *late)


def down_body(*refs):
    hids, downs, outs, held, sem = refs[:2], refs[2:4], refs[4:10], refs[10], refs[11]
    size = held.shape[0] // 8

    @pl.loop(0, 4)
    def _(index):
        own = pl.ds(pl.multiple_of(index * 2 * size, 2 * size), 2 * size)
        total = jnp.dot(hids[0][own, :], downs[0][...], preferred_element_type=f32)
        total += jnp.dot(hids[1][own, :], downs[1][...], preferred_element_type=f32)
        held[own, :] = total.astype(bf16)
        send_blocks(row_route, outs, held, index, size, sem)

    wait_all(held, sem)


def down(hids, downs, late=()):
    total, width = hids[0].shape[0], downs[0].shape[1]
    return kernel_call(
        down_body,
        routed(total // 8, width),
        [pltpu.VMEM((total, width), bf16), pltpu.SemaphoreType.DMA],
        [vmem_spec()] * 4,
        any_spec,
    )(*hids, *downs, *late)


def hidden_sums_body(count, pairs, shard, pieces, received, *refs):
    lefts, parts = refs[:pairs], refs[pairs : pairs + count]
    others = refs[pairs + count : pairs + count + pieces * received]
    refs = refs[pairs + count + pieces * received :]
    if received:
        refs, arrived, other_sem, out_sem = refs[:-3], refs[-3], refs[-2], refs[-1]
    outs, turned, rows, sem = refs[: -pairs - 2], refs[-pairs - 2 : -2], refs[-2], refs[-1]
    waits = [fetch_rows(parts, rows, sem)]
    if received:
        waits.append(fetch_rows(others, arrived, other_sem))

    @pl.loop(0, rows.shape[0] // step)
    def _(block):
        own = pl.ds(pl.multiple_of(block * step, step), step)
        for left, flat in zip(lefts, turned):
            flat[:, own] = left[own, :].T

    for wait in waits:
        wait()

    @pl.loop(0, rows.shape[1] // step)
    def _(block):
        columns = pl.ds(pl.multiple_of(block * step, step), step)
        for place, flat in enumerate(turned):
            product = jnp.dot(flat[...], rows[:, columns], preferred_element_type=f32)
            for outer in range(flat.shape[0] // shard):
                start = (pairs * outer + place) * shard
                own = product[outer * shard : (outer + 1) * shard]
                if received:
                    here = pl.ds(start, shard)
                    arrived[here, columns] = (own + arrived[here, columns].astype(f32)).astype(bf16)
                else:
                    piece, row = start // outs[0].shape[0], start % outs[0].shape[0]
                    outs[piece][row : row + shard, columns] = own.astype(bf16)
        if received:
            pltpu.make_async_copy(
                arrived.at[:, columns], outs[0].at[:, columns], out_sem
            ).start()

    if received:
        wait_all(arrived, out_sem)


def hidden_sums(lefts, parts, shard, pieces, others=None, late=()):
    total, width = lefts[0].shape[0], parts[0].shape[1]
    hidden = lefts[0].shape[1] * len(lefts)
    received = others is not None
    count = 1 if received else pieces
    scratch = [pltpu.VMEM((left.shape[1], total), bf16) for left in lefts]
    scratch += [pltpu.VMEM((total, width), bf16), pltpu.SemaphoreType.DMA]
    if received:
        scratch += [pltpu.VMEM((hidden, width), bf16)] + [pltpu.SemaphoreType.DMA] * 2
    outs = kernel_call(
        functools.partial(hidden_sums_body, len(parts), len(lefts), shard, pieces, received),
        (jax.ShapeDtypeStruct((hidden // count, width), bf16),) * count,
        scratch,
        [vmem_spec()] * len(lefts) + [any_spec()] * (len(parts) + pieces * received),
        any_spec if received else vmem_spec,
    )(*lefts, *parts, *(others or ()), *late)
    return outs[0] if received else outs


def send_sums_body(turned, right, first, second, held, sem):
    middle = turned.shape[0] // 2
    size = middle // 4

    @pl.loop(0, 4)
    def _(index):
        start = pl.multiple_of(index * size, size)
        own = turned[pl.ds(middle + start, size), :]
        held[pl.ds(start, size), :] = jnp.dot(own, right[...], preferred_element_type=f32).astype(bf16)
        for place, out in enumerate((first, first, second, second)):

            @pl.when(index == place)
            def _():
                target = out.at[pl.ds((place % 2) * size, size)]
                pltpu.make_async_copy(held.at[pl.ds(place * size, size)], target, sem).start()

    wait_all(held, sem)


def send_sums(turned, right, late=()):
    rows, columns = turned.shape[0] // 2, right.shape[1]
    return kernel_call(
        send_sums_body,
        (jax.ShapeDtypeStruct((rows // 2, columns), bf16),) * 2,
        [pltpu.VMEM((rows, columns), bf16), pltpu.SemaphoreType.DMA],
        [vmem_spec()] * 2,
        any_spec,
    )(turned, right, *late)


def keep_sums_body(turned, right, first, second, *refs):
    outs, arrived, held, in_sems, out_sem = refs[:6], refs[6], refs[7], refs[8], refs[9]
    size = turned.shape[0] // 16
    for place, part in enumerate((first, first, second, second)):
        source = part.at[pl.ds((place % 2) * 2 * size, 2 * size)]
        target = arrived.at[pl.ds(place * 2 * size, 2 * size)]
        pltpu.make_async_copy(source, target, in_sems.at[place]).start()

    @pl.loop(0, 4)
    def _(index):
        own = pl.ds(pl.multiple_of(index * 2 * size, 2 * size), 2 * size)
        product = jnp.dot(turned[own, :], right[...], preferred_element_type=f32)
        wait_all(arrived.at[own], in_sems.at[index])
        held[own, :] = (product + arrived[own, :].astype(f32)).astype(bf16)
        send_blocks(column_route, outs, held, index, size, out_sem)

    wait_all(held, out_sem)


def keep_sums(turned, right, others, late=()):
    rows, columns = turned.shape[0] // 2, right.shape[1]
    return kernel_call(
        keep_sums_body,
        routed(rows // 8, columns),
        [pltpu.VMEM((rows, columns), bf16)] * 2
        + [pltpu.SemaphoreType.DMA((4,)), pltpu.SemaphoreType.DMA],
        [vmem_spec()] * 2 + [any_spec()] * 2,
        any_spec,
    )(turned, right, *others, *late)


def alternate_body(both, out):
    rows = out.shape[0]

    @pl.loop(0, rows // 8)
    def _(block):
        start = pl.multiple_of(block * 8, 8)
        for place in range(2):
            out[pl.ds(start, 8), place, :] = both[pl.ds(place * rows + start, 8), :].astype(f32)


def alternate(both):
    rows, columns = both.shape[0] // 2, both.shape[1]
    out = jax.ShapeDtypeStruct((rows, 2, columns), f32)
    return kernel_call(alternate_body, out, [], [vmem_spec()])(both)


def widen_body(rows, first, second, gain_one, gain_two):
    columns, more = first.shape[1], second.shape[1]
    first[...] = rows[:, :columns].astype(f32)
    second[...] = rows[:, columns : columns + more].astype(f32)
    turned = rows[:, columns + more :].astype(f32).T
    gain_one[...] = turned[0:1, :]
    gain_two[...] = turned[1:2, :]


def widen(rows, first, second):
    shape = jax.ShapeDtypeStruct
    size = rows.shape[0]
    outs = (
        shape((size, first), f32),
        shape((size, second), f32),
        shape((1, size), f32),
        shape((1, size), f32),
    )
    *wide, gain_one, gain_two = kernel_call(widen_body, outs, [], [vmem_spec()])(rows)
    return *wide, gain_one.reshape(size), gain_two.reshape(size)


def pass_body(keep_x, keep_y, from_x, from_y, for_x, for_y, *refs):
    held, in_sems, out_sem = refs[:4], refs[4], refs[5]
    blocks = in_sems.shape[0]
    size = keep_x.shape[0] // blocks

    @pl.loop(0, blocks)
    def _(block):
        rows = pl.ds(pl.multiple_of(block * size, size), size)
        for source, target in zip((keep_x, from_y, keep_y, from_x), held):
            pltpu.make_async_copy(source.at[rows], target.at[rows], in_sems.at[block]).start()

    @pl.loop(0, blocks)
    def _(block):
        rows = pl.ds(pl.multiple_of(block * size, size), size)
        for target in held:
            wait_all(target.at[rows], in_sems.at[block])
        for keep, come, out in ((held[0], held[1], for_x), (held[2], held[3], for_y)):
            keep[rows, :] = (keep[rows, :].astype(f32) + come[rows, :].astype(f32)).astype(bf16)
            pltpu.make_async_copy(keep.at[rows], out.at[rows], out_sem).start()

    wait_all(held[0], out_sem)
    wait_all(held[2], out_sem)


def pass_on(keep_x, keep_y, from_x, from_y, late=()):
    out = jax.ShapeDtypeStruct(keep_x.shape, bf16)
    return kernel_call(
        pass_body,
        (out, out),
        [pltpu.VMEM(keep_x.shape, bf16)] * 4
        + [pltpu.SemaphoreType.DMA((4,)), pltpu.SemaphoreType.DMA],
        [any_spec()] * 4,
        any_spec,
    )(keep_x, keep_y, from_x, from_y, *late)


class Grid:
    def __init__(self, dp, fsdp):
        self.dp, self.fsdp = dp, fsdp
        self.depth = fsdp // 2
        self.groups = [[f for f in range(fsdp) if f % 2 == y] for y in range(2)]
        self.dp_index = lax.axis_index("dp")
        self.y = lax.axis_index("fsdp") % 2
        self.spot = jnp.stack([self.dp_index, self.y]).astype(jnp.int32)
        self.outer = lax.axis_index("fsdp") // 2

    def core(self, value):
        return lax.ppermute(value, "dp", [(i, i ^ 1) for i in range(self.dp)])

    def cores(self, values):
        return [self.core(value) for value in values]

    def echo(self, value, times):
        for _ in range(times):
            value = self.core(value)
        return value

    def x_swap(self, value):
        return lax.ppermute(value, "dp", [(i, i ^ 2) for i in range(self.dp)])

    def y_swap(self, value):
        return lax.ppermute(value, "fsdp", [(i, i ^ 1) for i in range(self.fsdp)])

    def plane_sum(self, value):
        value = value + self.core(value)
        pairs = [
            (dp * self.fsdp + f, (dp ^ 2) * self.fsdp + (f ^ 1))
            for dp in range(self.dp)
            for f in range(self.fsdp)
        ]
        across = lax.ppermute(value, ("dp", "fsdp"), pairs)
        return value + self.x_swap(value) + self.y_swap(value) + across

    def shift(self, value, low, high, by):
        pairs = [
            (2 * outer + y, 2 * (outer + by) + y) for outer in range(low, high) for y in range(2)
        ]
        return lax.ppermute(value, "fsdp", pairs)

    def gather_outer(self, value):
        return lax.all_gather(value, "fsdp", axis=0, tiled=True, axis_index_groups=self.groups)

    def scatter_outer(self, value):
        return lax.psum_scatter(
            value, "fsdp", scatter_dimension=0, tiled=True, axis_index_groups=self.groups
        )

    def spread_first(self, first, second):
        return first, second, self.x_swap(first), self.y_swap(second)

    def spread_second(self, first, second, first_x, second_y):
        first, second, first_x, second_y = lax.optimization_barrier(
            (first, second, first_x, second_y)
        )
        first_xy = self.y_swap(first_x)
        second_xy = self.x_swap(second_y)
        first_y = self.y_swap(first)
        second_x = self.x_swap(second)
        return {
            (0, 0): (first, second),
            (1, 0): (first_x, second_x),
            (0, 1): (first_y, second_y),
            (1, 1): (first_xy, second_xy),
        }

    def collect_first(self, parts, late=()):
        _, _, keep_x, keep_y, to_x, to_y = parts
        from_x, from_y = self.x_swap(to_x), self.y_swap(to_y)
        return (*pass_on(keep_x, keep_y, from_x, from_y, late), from_x, from_y)

    def collect_second(self, parts, passed):
        for_x, for_y, from_x, from_y = passed
        return (parts[0], from_y, self.x_swap(for_x)), (parts[1], from_x, self.y_swap(for_y))

    def pieces(self, planes, rows, token=None):
        keys = [(dx, dy) for dx in range(2) for dy in range(2)]
        mine = [half for key in keys for half in planes[key]]
        sent = mine if token is None else after(mine, token)
        theirs = [self.core(half) for half in sent]
        return Pieces(self.depth, rows, mine[0].shape[-1], mine + theirs)

    def total(self, sums):
        halves = []
        for own, middle, last in sums:
            middle = middle[own.shape[0] :]
            halves.append(own.astype(f32) + middle.astype(f32) + last.astype(f32))
        return jnp.concatenate(halves, axis=0)


def local(
    tokens,
    w_q,
    w_kv,
    g_attn,
    g_mlp,
    w_o,
    w_gu,
    w_down,
    grad_out,
    grad_kv,
    group_id,
    group_size,
    group_weight,
):
    grid = Grid(lax.axis_size("dp"), lax.axis_size("fsdp"))
    length, width = tokens.shape
    kv_width = w_kv.shape[1]
    head_dim = kv_width // 2
    q_width = w_q.shape[1]
    shard_rows = w_q.shape[0]
    hidden_rows = w_down.shape[0]
    half = length // 2

    matches = jnp.arange(group_size.shape[0], dtype=jnp.int32) == group_id[0]
    factor = jnp.sum(jnp.where(matches, group_weight / group_size.astype(jnp.float32), 0.0))
    grad_low = (grad_out.astype(jnp.float32) * factor).astype(jnp.bfloat16)
    cosines, sines = rope_tables(length, head_dim)

    plane_keys = ((0, 0), (1, 0), (0, 1), (1, 1))

    def in_order(planes):
        return [piece for key in plane_keys for piece in planes[key]]

    gains = jnp.stack([g_attn, g_mlp], axis=1)
    w_in = jnp.concatenate([w_q, w_kv, jnp.pad(gains, ((0, 0), (0, lanes - 2)))], axis=1)
    w_in_column = grid.gather_outer(w_in)
    w_o_column = grid.gather_outer(w_o)
    grad_first = grid.spread_first(grad_low[:half], grad_low[half:])
    pairs = jnp.swapaxes(w_gu, 0, 1).reshape(2 * hidden_rows, width)
    gu_mine = grid.gather_outer(pairs)
    grad_planes = grid.spread_second(*grad_first)
    grad_rows = in_order(grad_planes)
    cut = grid.depth // 2
    w_in_column = after(w_in_column, grad_planes[1, 1]).reshape(grid.depth, shard_rows, -1)
    in_planes = grid.spread_second(*grid.spread_first(w_in_column[:cut], w_in_column[cut:]))
    in_pieces = grid.pieces(in_planes, shard_rows)
    down_mine = grid.gather_outer(w_down)
    w_o_column = after(w_o_column, in_planes[1, 1]).reshape(grid.depth, shard_rows, -1)
    o_first = grid.spread_first(w_o_column[:cut], w_o_column[cut:])
    h_one, q_low, kv_out, gain_rows = project(
        grid.spot, tokens, cosines, sines, in_pieces, q_width, kv_width, head_dim
    )
    o_planes = grid.spread_second(*after(o_first, q_low))
    prob, attended, turned, h_turned = attend(
        grid.spot, q_low, kv_out, h_one, grid.depth, shard_rows
    )
    o_pieces = grid.pieces(o_planes, shard_rows, attended)
    x_mid, h_first, h_second = mix(grid.spot, tokens, attended, gain_rows, o_pieces)

    ff_rows = in_order(grid.spread_second(*grid.spread_first(h_first, h_second)))
    gu_mine = after(gu_mine, ff_rows)
    by_shard = hidden_rows % 8 == 0
    run_rows = hidden_rows if by_shard else grid.depth * hidden_rows

    def turn(both, rows):
        return both.reshape(-1, rows, hidden_rows, width).swapaxes(0, 1).reshape(both.shape)

    if not by_shard:
        gu_mine = turn(gu_mine, 2)
    gu_other = grid.core(gu_mine)
    hid_mine, *scales_mine = gate(ff_rows, gu_mine, run_rows)
    hid_other, *scales_other = gate(ff_rows, gu_other, run_rows, [hid_mine])
    runs = grid.depth if by_shard else 1
    sent = hidden_sums([hid_other], grad_rows, run_rows, runs)
    down_sum = hidden_sums([hid_mine], grad_rows, run_rows, runs, grid.cores(sent), [sent[0]])
    down_sum, down_mine = lax.optimization_barrier((down_sum, down_mine))
    d_w_down = grid.scatter_outer(down_sum)
    down_other = grid.core(down_mine)
    pair_mine = gate_back(grad_rows, down_mine, scales_mine)
    pair_other = gate_back(grad_rows, down_other, scales_other, [pair_mine[0]])
    d_h_parts = rows_back((*pair_mine, *pair_other), (gu_mine, gu_other), run_rows)
    sent = hidden_sums(pair_other, ff_rows, run_rows, 2*runs, late=[d_h_parts[0]])
    d_h_passed = grid.collect_first(d_h_parts, [sent[0]])
    pair_sum = hidden_sums(
        pair_mine, ff_rows, run_rows, 2*runs, grid.cores(sent), [d_h_passed[0]]
    )
    pair_sum, d_w_down = lax.optimization_barrier((pair_sum, d_w_down))
    d_w_gu = grid.scatter_outer(pair_sum if by_shard else turn(pair_sum, grid.depth))
    d_h_first, d_h_second = grid.collect_second(d_h_parts, d_h_passed)
    d_h_sums = [*d_h_first, *d_h_second]

    d_mid, d_mid_low, gain_two_sum = norm_back(
        factor.reshape(1), x_mid, gain_rows, grad_out, d_h_sums, [pair_sum]
    )
    sent = send_sums(turned, d_mid_low)
    o_parts = keep_sums(turned, d_mid_low, grid.cores(sent))
    joined, d_kv = attend_back(
        grid.spot, factor.reshape(1), d_mid_low, grad_kv, q_low, kv_out,
        prob, cosines, sines, o_pieces, [o_parts[0]],
    )
    o_passed = grid.collect_first(o_parts, [joined])
    sent = send_sums(h_turned, joined, [o_passed[0]])
    d_w_o = grid.total(grid.collect_second(o_parts, o_passed)).astype(bf16)
    d_w_o = grid.scatter_outer(d_w_o).astype(f32)
    in_parts = keep_sums(h_turned, joined, grid.cores(sent), [o_passed[0]])
    d_tokens, gain_one_sum = finish(
        grid.spot, tokens, gain_rows, joined, d_mid, in_pieces, [in_parts[0]]
    )
    in_passed = grid.collect_first(in_parts, [gain_one_sum, d_w_gu])
    d_w_in = grid.total(grid.collect_second(in_parts, in_passed)).astype(bf16)
    if by_shard:
        d_w_gu = alternate(d_w_gu)
    else:
        d_w_gu = jnp.stack([d_w_gu[:hidden_rows], d_w_gu[hidden_rows:]], axis=1).astype(f32)
    d_w_down = d_w_down.astype(f32)
    mlp_parts = down((hid_mine, hid_other), (down_mine, down_other), [in_passed[0]])
    d_w_in, mlp_parts = lax.optimization_barrier((d_w_in, mlp_parts))
    mlp_sum = grid.total(grid.collect_second(mlp_parts, grid.collect_first(mlp_parts)))
    output = (x_mid + mlp_sum).astype(jnp.bfloat16)
    gain_sums = jnp.stack([gain_one_sum[0], gain_two_sum[0]], axis=0)
    gain_sums = grid.plane_sum(gain_sums)
    own_gains = lax.dynamic_slice(
        gain_sums.reshape(2, grid.dp, grid.depth, 2, shard_rows),
        (0, grid.dp_index, 0, grid.y, 0),
        (2, 1, grid.depth, 1, shard_rows),
    ).reshape(2, grid.depth * shard_rows)
    extra = jnp.pad(own_gains.T, ((0, 0), (0, lanes - 2))).astype(bf16)
    d_w_in = grid.scatter_outer(jnp.concatenate([d_w_in, extra], axis=1))
    return (
        output,
        d_tokens,
        kv_out,
        d_kv,
        *widen(d_w_in, q_width, kv_width),
        d_w_o,
        d_w_gu,
        d_w_down,
    )


def solution(mesh):
    placed = (
        P(("dp", "fsdp"), None),
        P(("dp", "fsdp"), None),
        P(("dp", "fsdp"), None),
        P(("dp", "fsdp")),
        P(("dp", "fsdp")),
        P(("dp", "fsdp"), None),
        P(("dp", "fsdp"), None, None),
        P(("dp", "fsdp"), None),
        P(("dp", "fsdp"), None),
        P(("dp", "fsdp"), None),
        P(("dp", "fsdp")),
        P(),
        P(),
    )
    return jax.shard_map(
        local,
        mesh=mesh,
        in_specs=placed,
        out_specs=(
            P(("dp", "fsdp"), None),
            P(("dp", "fsdp"), None),
            P(("dp", "fsdp"), None),
            P(("dp", "fsdp"), None),
            P(("dp", "fsdp"), None),
            P(("dp", "fsdp"), None),
            P(("dp", "fsdp")),
            P(("dp", "fsdp")),
            P(("dp", "fsdp"), None),
            P(("dp", "fsdp"), None, None),
            P(("dp", "fsdp"), None),
        ),
        check_vma=False,
    )
```

```python
import functools

import jax
import jax.numpy as jnp
from jax import lax
from jax.experimental import pallas as pl
from jax.experimental.pallas import tpu as pltpu
from jax.sharding import PartitionSpec as P

epsilon = 1e-05
theta_base = 10000.0
bf16 = jnp.bfloat16
f32 = jnp.float32
lanes = 128
step = 256
vmem_limit = 60 * 1024 * 1024


def rope_tables(length, width):
    halfway = width // 2
    freqs = theta_base ** (-(jnp.arange(halfway, dtype=jnp.float32) * 2.0 / width))
    angles = jnp.arange(length, dtype=jnp.float32)[:, None] * freqs[None, :]
    cosines, sine_part = jnp.cos(angles), jnp.sin(angles)
    return (
        jnp.concatenate([cosines, cosines], axis=1),
        jnp.concatenate([-sine_part, sine_part], axis=1),
    )


def contract(left, right, left_axis, right_axis):
    return lax.dot_general(
        left, right, (((left_axis,), (right_axis,)), ((), ())), preferred_element_type=jnp.float32
    )


def contract_last(left, right):
    return contract(left, right, left.ndim - 1, right.ndim - 1)


def contract_first(left, right):
    return contract(left, right, 0, 0)


def after(value, token):
    value, _ = lax.optimization_barrier((value, token))
    return value


def vmem_spec():
    return pl.BlockSpec(memory_space=pltpu.VMEM)


def any_spec():
    return pl.BlockSpec(memory_space=pl.ANY)


def smem_spec():
    return pl.BlockSpec(memory_space=pltpu.SMEM)


def kernel_call(body, out_shapes, scratch, in_specs, out_spec=vmem_spec):
    def run(*operands):
        known, late = len(in_specs), len(operands) - len(in_specs)

        def whole_body(*refs):
            body(*refs[:known], *refs[known + late :])

        return pl.pallas_call(
            whole_body,
            out_shape=out_shapes,
            in_specs=in_specs + [any_spec()] * late,
            out_specs=jax.tree.map(lambda _: out_spec(), out_shapes),
            scratch_shapes=scratch,
            compiler_params=pltpu.CompilerParams(vmem_limit_bytes=vmem_limit),
            cost_estimate=pl.CostEstimate(flops=1, bytes_accessed=1, transcendentals=0),
            name=getattr(body, "func", body).__name__[: -len("_body")],
        )(*operands)

    return run


def route(keys):
    place = {(key, half): 2 * i + half for i, key in enumerate(keys) for half in range(2)}
    own, x, y, both = (0, 0), (1, 0), (0, 1), (1, 1)
    return (
        (place[own, 0],),
        (place[own, 1],),
        (place[x, 0],),
        (place[y, 1],),
        (place[both, 1], place[x, 1]),
        (place[both, 0], place[y, 0]),
    )


row_route = route(((0, 0), (1, 0), (0, 1), (1, 1)))
column_route = route(((0, 0), (0, 1), (1, 0), (1, 1)))


def routed(size, columns):
    return tuple(
        jax.ShapeDtypeStruct((size * len(blocks), columns), bf16) for blocks in row_route
    )


def send_blocks(way, outs, held, index, size, sem):
    for blocks, out in zip(way, outs):
        for spot, place in enumerate(blocks):

            @pl.when(index == place // 2)
            def _():
                pltpu.make_async_copy(
                    held.at[pl.ds(place * size, size)], out.at[pl.ds(spot * size, size)], sem
                ).start()


def wait_all(whole, sem):
    pltpu.make_async_copy(whole, whole, sem).wait()


class Pieces:
    def __init__(self, depth, rows, columns, arrays):
        self.depth, self.rows, self.columns, self.arrays = depth, rows, columns, arrays

    def start(self, refs, spot, whole, sem, apart=False):
        cut = self.depth // 2
        place = 0
        for flip in range(2):
            for dx in range(2):
                for dy in range(2):
                    for low, high in ((0, cut), (cut, self.depth)):
                        for outer in range(low, high):
                            block = (
                                (spot[0] ^ (2 * dx + flip)) * self.depth + outer
                            ) * 2 + (spot[1] ^ dy)
                            row = pl.multiple_of(block * self.rows, self.rows)
                            pltpu.make_async_copy(
                                refs[place].at[outer - low],
                                whole.at[pl.ds(row, self.rows)],
                                sem.at[2 * dx + flip] if apart else sem,
                            ).start()
                        place += 1

    def wait(self, whole, sem):
        pltpu.make_async_copy(whole, whole, sem).wait()

    def group(self, whole, spot, index):
        flip = (index % 2) * 2 + index // 2
        size = whole.shape[0] // 4
        return pl.multiple_of((spot[0] ^ flip) * size, size), size, flip


def swap_halves(value):
    return pltpu.roll(value, value.shape[-1] // 2, 1)


def relative_place(block, spot, depth):
    side = block % 2
    outer = (block // 2) % depth
    flips = (block // (2 * depth)) ^ spot[0]
    return (((flips % 2) * 2 + flips // 2) * 2 + (side ^ spot[1])) * depth + outer


def put_in_order(source, target, spot, depth, rows):
    @pl.loop(0, source.shape[0] // rows)
    def _(block):
        place = pl.multiple_of(relative_place(block, spot, depth) * rows, rows)
        target[pl.ds(place, rows), :] = source[pl.ds(pl.multiple_of(block * rows, rows), rows), :]


def project_body(pieces, q_width, kv_width, head_dim, *refs):
    count = len(pieces.arrays)
    spot, tokens, cosines, sines = refs[:4]
    shards = refs[4 : 4 + count]
    h_low, q_out, kv_out, gain_out = refs[4 + count : 8 + count]
    whole, sem = refs[8 + count :]
    pieces.start(shards, spot, whole, sem)
    width = tokens.shape[1]
    x_full = tokens[...].astype(f32)
    inverse = lax.rsqrt(jnp.mean(x_full * x_full, axis=-1, keepdims=True) + epsilon)
    pieces.wait(whole, sem)
    pick = (
        lax.broadcasted_iota(jnp.int32, (8, lanes), 0) == lax.broadcasted_iota(jnp.int32, (8, lanes), 1)
    ).astype(bf16)
    gains = contract_last(pick, whole[:, q_width + kv_width :])
    gain_out[...] = gains
    h_low[...] = (x_full * inverse * gains[0:1]).astype(bf16)
    cos, sin = cosines[...], sines[...]
    kv_pre = jnp.dot(h_low[...], whole[:, q_width : q_width + kv_width], preferred_element_type=f32)
    key_part = kv_pre[:, :head_dim]
    kv_out[:, :head_dim] = (key_part * cos + swap_halves(key_part) * sin).astype(bf16)
    kv_out[:, head_dim:] = kv_pre[:, head_dim:].astype(bf16)

    @pl.loop(0, q_width // step)
    def _(block):
        start = pl.multiple_of(block * step, step)
        q_pre = jnp.dot(h_low[...], whole[:, pl.ds(start, step)], preferred_element_type=f32)
        for head in range(step // head_dim):
            own = q_pre[:, head * head_dim : (head + 1) * head_dim]
            column = pl.multiple_of(start + head * head_dim, head_dim)
            q_out[:, pl.ds(column, head_dim)] = (own * cos + swap_halves(own) * sin).astype(bf16)


def project(spot, tokens, cosines, sines, pieces, q_width, kv_width, head_dim, late=()):
    length, width = tokens.shape
    count = len(pieces.arrays)
    shape = jax.ShapeDtypeStruct
    return kernel_call(
        functools.partial(project_body, pieces, q_width, kv_width, head_dim),
        (
            shape((length, width), bf16),
            shape((length, q_width), bf16),
            shape((length, kv_width), bf16),
            shape((8, width), f32),
        ),
        [
            pltpu.VMEM((width, pieces.columns), bf16),
            pltpu.SemaphoreType.DMA,
        ],
        [smem_spec(), vmem_spec(), vmem_spec(), vmem_spec()] + [any_spec()] * count,
    )(spot, tokens, cosines, sines, *pieces.arrays, *late)


def attend_body(depth, rows, head_dim, *refs):
    spot, q_low, kv_low, h_low, prob_out, attended_out, turned, h_turned, flat = refs
    length, q_width = q_low.shape
    scale = head_dim ** (-0.5)
    keys = kv_low[:, :head_dim]
    values_turned = kv_low[:, head_dim:].T
    allowed = lax.broadcasted_iota(jnp.int32, (length, length), 0) <= lax.broadcasted_iota(
        jnp.int32, (length, length), 1
    )
    heads = step // head_dim

    @pl.loop(0, q_width // step)
    def _(block):
        for head in range(heads):
            column = pl.multiple_of(block * step + head * head_dim, head_dim)
            queries = q_low[:, pl.ds(column, head_dim)]
            logits = jnp.where(allowed, contract_last(keys, queries) * scale, -1e30)
            exp_vals = jnp.exp(logits - jnp.max(logits, axis=0, keepdims=True))
            prob = (exp_vals / jnp.sum(exp_vals, axis=0, keepdims=True)).astype(bf16)
            prob_out[block * heads + head] = prob
            mixed = jnp.dot(values_turned, prob, preferred_element_type=f32)
            flat[pl.ds(column, head_dim), :] = mixed.astype(bf16)
            attended_out[:, pl.ds(column, head_dim)] = mixed.T.astype(bf16)

    put_in_order(flat.at[pl.ds(0, q_width)], turned, spot, depth, rows)

    @pl.loop(0, h_low.shape[1] // step)
    def _(block):
        start = pl.multiple_of(block * step, step)
        flat[pl.ds(start, step), :] = h_low[:, pl.ds(start, step)].T

    put_in_order(flat.at[pl.ds(0, h_turned.shape[0])], h_turned, spot, depth, rows)


def attend(spot, q_low, kv_low, h_low, depth, rows, late=()):
    length, q_width = q_low.shape
    head_dim = kv_low.shape[1] // 2
    shape = jax.ShapeDtypeStruct
    return kernel_call(
        functools.partial(attend_body, depth, rows, head_dim),
        (
            shape((q_width // head_dim, length, length), bf16),
            shape((length, q_width), bf16),
            shape((q_width, length), bf16),
            shape((h_low.shape[1], length), bf16),
        ),
        [pltpu.VMEM((max(q_width, h_low.shape[1]), length), bf16)],
        [smem_spec(), vmem_spec(), vmem_spec(), vmem_spec()],
    )(spot, q_low, kv_low, h_low, *late)


def mix_body(pieces, *refs):
    count = len(pieces.arrays)
    spot, tokens, attended, gains = refs[:4]
    shards = refs[4 : 4 + count]
    mid_out, first_out, second_out = refs[4 + count : 7 + count]
    whole, sem = refs[7 + count :]
    pieces.start(shards, spot, whole, sem, True)
    length, width = tokens.shape
    mid_out[...] = tokens[...].astype(f32)

    @pl.loop(0, 4)
    def _(index):
        row, size, flip = pieces.group(whole, spot, index)
        rows = pl.ds(row, size)
        wait_all(whole.at[rows], sem.at[flip])

        @pl.loop(0, width // (2 * step))
        def _(block):
            columns = pl.ds(pl.multiple_of(block * 2 * step, 2 * step), 2 * step)
            mid_out[:, columns] += jnp.dot(
                attended[:, rows], whole[rows, columns], preferred_element_type=f32
            )

    x_mid = mid_out[...]
    inverse = lax.rsqrt(jnp.mean(x_mid * x_mid, axis=-1, keepdims=True) + epsilon)
    h_two = (x_mid * inverse * gains[1:2, :]).astype(bf16)
    first_out[...] = h_two[: length // 2]
    second_out[...] = h_two[length // 2 :]


def mix(spot, tokens, attended, gains, pieces, late=()):
    length, width = tokens.shape
    shape = jax.ShapeDtypeStruct
    half = shape((length // 2, width), bf16)
    rows = attended.shape[1]
    return kernel_call(
        functools.partial(mix_body, pieces),
        (shape((length, width), f32), half, half),
        [pltpu.VMEM((rows, width), bf16), pltpu.SemaphoreType.DMA((4,))],
        [smem_spec(), vmem_spec(), vmem_spec(), vmem_spec()] + [any_spec()] * len(pieces.arrays),
    )(spot, tokens, attended, gains, *pieces.arrays, *late)


def norm_back_body(factor, gains, mid, grad_out, *refs):
    sums, outs = refs[:6], refs[6:9]
    mid_in, grad_in, own, middle, last, d_mid_held, low_held, gain_held = refs[9:17]
    in_sems, out_sem = refs[17], refs[18]
    length = mid.shape[0]
    half = length // 2
    blocks = in_sems.shape[0]
    size = length // blocks

    @pl.loop(0, blocks)
    def _(block):
        rows = pl.ds(pl.multiple_of(block * size, size), size)
        for source, target in ((mid, mid_in), (grad_out, grad_in)):
            pltpu.make_async_copy(source.at[rows], target.at[rows], in_sems.at[block]).start()
        for part in range(2):

            @pl.when(block // (blocks // 2) == part)
            def _():
                start = pl.multiple_of((block - part * (blocks // 2)) * size, size)
                for source, target, skip in zip(sums[3 * part :], (own, middle, last), (0, half, 0)):
                    pltpu.make_async_copy(
                        source.at[pl.ds(skip + start, size)], target.at[rows], in_sems.at[block]
                    ).start()

    gain = gains[1:2, :]
    gain_held[...] = jnp.zeros_like(gain_held)

    @pl.loop(0, blocks)
    def _(block):
        rows = pl.ds(pl.multiple_of(block * size, size), size)
        for held in (mid_in, grad_in, own, middle, last):
            wait_all(held.at[rows], in_sems.at[block])
        d_h = own[rows, :].astype(f32) + middle[rows, :].astype(f32) + last[rows, :].astype(f32)
        x_mid = mid_in[rows, :]
        inverse = lax.rsqrt(jnp.mean(x_mid * x_mid, axis=-1, keepdims=True) + epsilon)
        normed = x_mid * inverse
        product = d_h * normed
        gain_held[0:1, :] += jnp.sum(product, axis=0, keepdims=True)
        mean = jnp.mean(product * gain, axis=-1, keepdims=True)
        grad_top = grad_in[rows, :].astype(f32) * factor[0]
        d_mid = grad_top + inverse * (d_h * gain - normed * mean)
        d_mid_held[rows, :] = d_mid
        low_held[rows, :] = d_mid.astype(bf16)
        for held, target in zip((d_mid_held, low_held), outs):
            pltpu.make_async_copy(held.at[rows], target.at[rows], out_sem).start()

    pltpu.make_async_copy(gain_held, outs[2], out_sem).start()
    for held in (d_mid_held, low_held, gain_held):
        wait_all(held, out_sem)


def norm_back(factor, mid, gains, grad_out, sums, late=()):
    length, width = mid.shape
    shape = jax.ShapeDtypeStruct
    whole = pltpu.VMEM((length, width), bf16)
    wide = pltpu.VMEM((length, width), f32)
    return kernel_call(
        norm_back_body,
        (shape((length, width), f32), shape((length, width), bf16), shape((8, width), f32)),
        [wide, whole, whole, whole, whole, wide, whole, pltpu.VMEM((8, width), f32)]
        + [pltpu.SemaphoreType.DMA((8,)), pltpu.SemaphoreType.DMA],
        [smem_spec(), vmem_spec()] + [any_spec()] * 8,
        any_spec,
    )(factor, gains, mid, grad_out, *sums, *late)


def attend_back_body(pieces, head_dim, *refs):
    count = len(pieces.arrays)
    (spot, factor, d_mid_low, grad_kv, q_low, kv_low, prob_ref, cosines, sines) = refs[:9]
    shards = refs[9 : 9 + count]
    joined, d_kv_out = refs[9 + count : 11 + count]
    whole, sem = refs[11 + count :]
    pieces.start(shards, spot, whole, sem, True)
    length = d_mid_low.shape[0]
    q_width = q_low.shape[1]
    scale = head_dim ** (-0.5)
    cos, sin = cosines[...], sines[...]
    keys, values = kv_low[:, :head_dim], kv_low[:, head_dim:]
    d_kv_out[...] = grad_kv[...].astype(f32) * factor[0]
    heads = step // head_dim

    @pl.loop(0, q_width // step)
    def _(block):
        row, size, flip = pieces.group(whole, spot, block // (whole.shape[0] // 4 // step))
        inside = block % (size // step)

        @pl.when(inside == 0)
        def _():
            wait_all(whole.at[pl.ds(row, size)], sem.at[flip])

        start = pl.multiple_of(row + inside * step, step)
        d_att = contract_last(d_mid_low[...], whole[pl.ds(start, step), :]).astype(bf16)
        d_k = jnp.zeros((length, head_dim), f32)
        d_v = jnp.zeros((length, head_dim), f32)
        for head in range(heads):
            own = d_att[:, head * head_dim : (head + 1) * head_dim]
            column = pl.multiple_of(start + head * head_dim, head_dim)
            low = prob_ref[start // head_dim + head]
            prob = low.astype(f32)
            d_prob = contract_last(values, own)
            centre = jnp.sum(prob * d_prob, axis=0, keepdims=True)
            d_raw = (prob * (d_prob - centre) * scale).astype(bf16)
            d_v += jnp.dot(low, own, preferred_element_type=f32)
            d_k += jnp.dot(d_raw, q_low[:, pl.ds(column, head_dim)], preferred_element_type=f32)
            d_q = contract_first(d_raw, keys)
            joined[:, pl.ds(column, head_dim)] = (d_q * cos - swap_halves(d_q) * sin).astype(bf16)
        d_kv_out[:, :head_dim] += d_k
        d_kv_out[:, head_dim:] += d_v

    d_k = d_kv_out[:, :head_dim]
    joined[:, q_width : q_width + head_dim] = (d_k * cos - swap_halves(d_k) * sin).astype(bf16)
    joined[:, q_width + head_dim :] = d_kv_out[:, head_dim:].astype(bf16)


def attend_back(spot, factor, d_mid_low, grad_kv, q_low, kv_low, prob, cosines, sines, pieces, late=()):
    length, width = d_mid_low.shape
    q_width, kv_width = q_low.shape[1], kv_low.shape[1]
    head_dim = kv_width // 2
    shape = jax.ShapeDtypeStruct
    return kernel_call(
        functools.partial(attend_back_body, pieces, head_dim),
        (shape((length, q_width + kv_width), bf16), shape((length, kv_width), f32)),
        [pltpu.VMEM((q_width, width), bf16), pltpu.SemaphoreType.DMA((4,))],
        [smem_spec()] * 2 + [vmem_spec()] * 7 + [any_spec()] * len(pieces.arrays),
    )(spot, factor, d_mid_low, grad_kv, q_low, kv_low, prob, cosines, sines, *pieces.arrays, *late)


def finish_body(pieces, *refs):
    count = len(pieces.arrays)
    spot, tokens, gains, joined, d_mid = refs[:5]
    shards = refs[5 : 5 + count]
    d_tokens, gain_out = refs[5 + count : 7 + count]
    whole, sem = refs[7 + count :]
    pieces.start(shards, spot, whole, sem)
    length, width = tokens.shape
    used = joined.shape[1]
    x_full = tokens[...].astype(f32)
    inverse = lax.rsqrt(jnp.mean(x_full * x_full, axis=-1, keepdims=True) + epsilon)
    pieces.wait(whole, sem)

    def add(block, total):
        start = pl.multiple_of(block * step, step)
        columns = pl.ds(start, step)
        d_h = contract_last(joined[...], whole[columns, :used])
        normed = tokens[:, columns].astype(f32) * inverse
        gain_out[:, columns] = jnp.broadcast_to(
            jnp.sum(d_h * normed, axis=0, keepdims=True), (8, step)
        )
        d_normed = d_h * gains[0:1, columns]
        d_tokens[:, columns] = d_normed
        return total + jnp.sum(d_normed * normed, axis=-1, keepdims=True)

    total = lax.fori_loop(0, width // step, add, jnp.zeros((length, 1), f32))
    d_tokens[...] = d_mid[...] + inverse * (d_tokens[...] - x_full * inverse * (total / width))


def finish(spot, tokens, gains, joined, d_mid, pieces, late=()):
    length, width = tokens.shape
    shape = jax.ShapeDtypeStruct
    return kernel_call(
        functools.partial(finish_body, pieces),
        (shape((length, width), f32), shape((8, width), f32)),
        [pltpu.VMEM((width, pieces.columns), bf16), pltpu.SemaphoreType.DMA],
        [smem_spec()] + [vmem_spec()] * 4 + [any_spec()] * len(pieces.arrays),
    )(spot, tokens, gains, joined, d_mid, *pieces.arrays, *late)


def fetch_rows(parts, whole, sem):
    start = 0
    for part in parts:
        pltpu.make_async_copy(part, whole.at[pl.ds(start, part.shape[0])], sem).start()
        start += part.shape[0]
    return pltpu.make_async_copy(whole, whole, sem).wait


def fetch_gate_up(both, shard, first, second, first_sem, second_sem):
    waits = []
    for place, (whole, sem) in enumerate(((first, first_sem), (second, second_sem))):
        for outer in range(both.shape[0] // (2 * shard)):
            source = both.at[pl.ds((2 * outer + place) * shard, shard)]
            pltpu.make_async_copy(source, whole.at[pl.ds(outer * shard, shard)], sem).start()
        waits.append(pltpu.make_async_copy(whole, whole, sem).wait)
    return waits


def fetch_row_blocks(parts, whole, sems):
    size = parts[0].shape[0]
    for place, part in enumerate(parts):
        sem = sems.at[place * size // step]
        pltpu.make_async_copy(part, whole.at[pl.ds(place * size, size)], sem).start()


def gate_body(shard, count, *refs):
    parts, both, outs = refs[:count], refs[count], refs[count + 1 : count + 4]
    held, refs = refs[count + 4 : count + 7], refs[count + 7 :]
    rows, gate_w, up_w, row_sems, gate_sem, up_sem, out_sem = refs
    waits = fetch_gate_up(both, shard, gate_w, up_w, gate_sem, up_sem)
    fetch_row_blocks(parts, rows, row_sems)
    for wait in waits:
        wait()

    @pl.loop(0, rows.shape[0] // step)
    def _(block):
        own = pl.ds(pl.multiple_of(block * step, step), step)
        wait_all(rows.at[own], row_sems.at[block])
        gate = contract_last(rows[own, :], gate_w[...])
        up = contract_last(rows[own, :], up_w[...])
        sigma = 1.0 / (1.0 + jnp.exp(-gate))
        silu = gate * sigma
        held[0][own, :] = (silu * up).astype(bf16)
        held[1][own, :] = (up * sigma * (1.0 + gate * (1.0 - sigma))).astype(bf16)
        held[2][own, :] = silu.astype(bf16)
        for source, out in zip(held, outs):
            pltpu.make_async_copy(source.at[own], out.at[own], out_sem).start()

    for source in held:
        wait_all(source, out_sem)


def gate(parts, both, shard, late=()):
    total, width = sum(part.shape[0] for part in parts), parts[0].shape[1]
    hidden = both.shape[0] // 2
    out = jax.ShapeDtypeStruct((total, hidden), bf16)
    return kernel_call(
        functools.partial(gate_body, shard, len(parts)),
        (out, out, out),
        [pltpu.VMEM((total, hidden), bf16)] * 3
        + [pltpu.VMEM((total, width), bf16)]
        + [pltpu.VMEM((hidden, width), bf16)] * 2
        + [pltpu.SemaphoreType.DMA((total // step,))]
        + [pltpu.SemaphoreType.DMA] * 3,
        [any_spec()] * (len(parts) + 1),
        any_spec,
    )(*parts, both, *late)


def gate_back_body(count, *refs):
    parts, weight, scales, grads = refs[:count], refs[count], refs[count + 1 : count + 3], refs[count + 3 : count + 5]
    rows, weight_in, first, second, row_sems, weight_sem, out_sem = refs[count + 5 :]
    wait = fetch_rows([weight], weight_in, weight_sem)
    scaled = (first, second)
    for source, held in zip(scales, scaled):
        for block in range(rows.shape[0] // step):
            own = pl.ds(block * step, step)
            pltpu.make_async_copy(source.at[own], held.at[own], row_sems.at[block]).start()
    fetch_row_blocks(parts, rows, row_sems)
    wait()

    @pl.loop(0, rows.shape[0] // step)
    def _(block):
        own = pl.ds(pl.multiple_of(block * step, step), step)
        for whole in (rows, first, second):
            wait_all(whole.at[own], row_sems.at[block])
        d_hid = contract_last(rows[own, :], weight_in[...])
        for held, grad in zip(scaled, grads):
            held[own, :] = (d_hid * held[own, :].astype(f32)).astype(bf16)
            pltpu.make_async_copy(held.at[own], grad.at[own], out_sem).start()

    for held in scaled:
        wait_all(held, out_sem)


def gate_back(parts, weight, scales, late=()):
    count = len(parts)
    total, width = sum(part.shape[0] for part in parts), parts[0].shape[1]
    hidden = weight.shape[0]
    grad = jax.ShapeDtypeStruct((total, hidden), bf16)
    return kernel_call(
        functools.partial(gate_back_body, count),
        (grad, grad),
        [pltpu.VMEM((total, width), bf16), pltpu.VMEM((hidden, width), bf16)]
        + [pltpu.VMEM((total, hidden), bf16)] * 2
        + [pltpu.SemaphoreType.DMA((total // step,))]
        + [pltpu.SemaphoreType.DMA] * 2,
        [any_spec()] * (count + 3),
        any_spec,
    )(*parts, weight, *scales, *late)


def rows_back_body(shard, *refs):
    grads, boths, outs = refs[:4], refs[4:6], refs[6:12]
    weights, held, sems, out_sem = refs[12:16], refs[16], refs[17], refs[18]
    size, chunk = held.shape[0] // 8, 4 * step
    chunks = held.shape[1] // chunk

    @pl.loop(0, chunks)
    def _(block):
        columns = pl.ds(pl.multiple_of(block * chunk, chunk), chunk)
        for place, weight in enumerate(weights):
            for outer in range(weight.shape[0] // shard):
                source = boths[place // 2].at[pl.ds((2 * outer + place % 2) * shard, shard), columns]
                target = weight.at[pl.ds(outer * shard, shard), columns]
                pltpu.make_async_copy(source, target, sems.at[block]).start()

    @pl.loop(0, chunks)
    def _(block):
        columns = pl.ds(pl.multiple_of(block * chunk, chunk), chunk)
        for weight in weights:
            wait_all(weight.at[:, columns], sems.at[block])

        @pl.loop(0, 4)
        def _(index):
            own = pl.ds(pl.multiple_of(index * 2 * size, 2 * size), 2 * size)
            total = jnp.dot(grads[0][own, :], weights[0][:, columns], preferred_element_type=f32)
            for grad, piece in zip(grads[1:], weights[1:]):
                total += jnp.dot(grad[own, :], piece[:, columns], preferred_element_type=f32)
            held[own, columns] = total.astype(bf16)

        for blocks, out in zip(row_route, outs):
            for spot, place in enumerate(blocks):
                source = held.at[pl.ds(place * size, size), columns]
                target = out.at[pl.ds(spot * size, size), columns]
                pltpu.make_async_copy(source, target, out_sem).start()

    wait_all(held, out_sem)


def rows_back(grads, boths, shard, late=()):
    total, hidden = grads[0].shape
    width = boths[0].shape[1]
    return kernel_call(
        functools.partial(rows_back_body, shard),
        routed(total // 8, width),
        [pltpu.VMEM((hidden, width), bf16)] * 4
        + [
            pltpu.VMEM((total, width), bf16),
            pltpu.SemaphoreType.DMA((width // (4 * step),)),
            pltpu.SemaphoreType.DMA,
        ],
        [vmem_spec()] * 4 + [any_spec()] * 2,
        any_spec,
    )(*grads, *boths, *late)


def down_body(*refs):
    hids, downs, outs, held, sem = refs[:2], refs[2:4], refs[4:10], refs[10], refs[11]
    size = held.shape[0] // 8

    @pl.loop(0, 4)
    def _(index):
        own = pl.ds(pl.multiple_of(index * 2 * size, 2 * size), 2 * size)
        total = jnp.dot(hids[0][own, :], downs[0][...], preferred_element_type=f32)
        total += jnp.dot(hids[1][own, :], downs[1][...], preferred_element_type=f32)
        held[own, :] = total.astype(bf16)
        send_blocks(row_route, outs, held, index, size, sem)

    wait_all(held, sem)


def down(hids, downs, late=()):
    total, width = hids[0].shape[0], downs[0].shape[1]
    return kernel_call(
        down_body,
        routed(total // 8, width),
        [pltpu.VMEM((total, width), bf16), pltpu.SemaphoreType.DMA],
        [vmem_spec()] * 4,
        any_spec,
    )(*hids, *downs, *late)


def hidden_sums_body(count, pairs, shard, pieces, received, *refs):
    lefts, parts = refs[:pairs], refs[pairs : pairs + count]
    others = refs[pairs + count : pairs + count + pieces * received]
    refs = refs[pairs + count + pieces * received :]
    if received:
        refs, arrived, other_sem, out_sem = refs[:-3], refs[-3], refs[-2], refs[-1]
    outs, turned, rows, sem = refs[: -pairs - 2], refs[-pairs - 2 : -2], refs[-2], refs[-1]
    waits = [fetch_rows(parts, rows, sem)]
    if received:
        waits.append(fetch_rows(others, arrived, other_sem))

    @pl.loop(0, rows.shape[0] // step)
    def _(block):
        own = pl.ds(pl.multiple_of(block * step, step), step)
        for left, flat in zip(lefts, turned):
            flat[:, own] = left[own, :].T

    for wait in waits:
        wait()

    @pl.loop(0, rows.shape[1] // step)
    def _(block):
        columns = pl.ds(pl.multiple_of(block * step, step), step)
        for place, flat in enumerate(turned):
            product = jnp.dot(flat[...], rows[:, columns], preferred_element_type=f32)
            for outer in range(flat.shape[0] // shard):
                start = (pairs * outer + place) * shard
                own = product[outer * shard : (outer + 1) * shard]
                if received:
                    here = pl.ds(start, shard)
                    arrived[here, columns] = (own + arrived[here, columns].astype(f32)).astype(bf16)
                else:
                    piece, row = start // outs[0].shape[0], start % outs[0].shape[0]
                    outs[piece][row : row + shard, columns] = own.astype(bf16)
        if received:
            pltpu.make_async_copy(
                arrived.at[:, columns], outs[0].at[:, columns], out_sem
            ).start()

    if received:
        wait_all(arrived, out_sem)


def hidden_sums(lefts, parts, shard, pieces, others=None, late=()):
    total, width = lefts[0].shape[0], parts[0].shape[1]
    hidden = lefts[0].shape[1] * len(lefts)
    received = others is not None
    count = 1 if received else pieces
    scratch = [pltpu.VMEM((left.shape[1], total), bf16) for left in lefts]
    scratch += [pltpu.VMEM((total, width), bf16), pltpu.SemaphoreType.DMA]
    if received:
        scratch += [pltpu.VMEM((hidden, width), bf16)] + [pltpu.SemaphoreType.DMA] * 2
    outs = kernel_call(
        functools.partial(hidden_sums_body, len(parts), len(lefts), shard, pieces, received),
        (jax.ShapeDtypeStruct((hidden // count, width), bf16),) * count,
        scratch,
        [vmem_spec()] * len(lefts) + [any_spec()] * (len(parts) + pieces * received),
        any_spec if received else vmem_spec,
    )(*lefts, *parts, *(others or ()), *late)
    return outs[0] if received else outs


def send_sums_body(turned, right, first, second, held, sem):
    middle = turned.shape[0] // 2
    size = middle // 4

    @pl.loop(0, 4)
    def _(index):
        start = pl.multiple_of(index * size, size)
        own = turned[pl.ds(middle + start, size), :]
        held[pl.ds(start, size), :] = jnp.dot(own, right[...], preferred_element_type=f32).astype(bf16)
        for place, out in enumerate((first, first, second, second)):

            @pl.when(index == place)
            def _():
                target = out.at[pl.ds((place % 2) * size, size)]
                pltpu.make_async_copy(held.at[pl.ds(place * size, size)], target, sem).start()

    wait_all(held, sem)


def send_sums(turned, right, late=()):
    rows, columns = turned.shape[0] // 2, right.shape[1]
    return kernel_call(
        send_sums_body,
        (jax.ShapeDtypeStruct((rows // 2, columns), bf16),) * 2,
        [pltpu.VMEM((rows, columns), bf16), pltpu.SemaphoreType.DMA],
        [vmem_spec()] * 2,
        any_spec,
    )(turned, right, *late)


def keep_sums_body(turned, right, first, second, *refs):
    outs, arrived, held, in_sems, out_sem = refs[:6], refs[6], refs[7], refs[8], refs[9]
    size = turned.shape[0] // 16
    for place, part in enumerate((first, first, second, second)):
        source = part.at[pl.ds((place % 2) * 2 * size, 2 * size)]
        target = arrived.at[pl.ds(place * 2 * size, 2 * size)]
        pltpu.make_async_copy(source, target, in_sems.at[place]).start()

    @pl.loop(0, 4)
    def _(index):
        own = pl.ds(pl.multiple_of(index * 2 * size, 2 * size), 2 * size)
        product = jnp.dot(turned[own, :], right[...], preferred_element_type=f32)
        wait_all(arrived.at[own], in_sems.at[index])
        held[own, :] = (product + arrived[own, :].astype(f32)).astype(bf16)
        send_blocks(column_route, outs, held, index, size, out_sem)

    wait_all(held, out_sem)


def keep_sums(turned, right, others, late=()):
    rows, columns = turned.shape[0] // 2, right.shape[1]
    return kernel_call(
        keep_sums_body,
        routed(rows // 8, columns),
        [pltpu.VMEM((rows, columns), bf16)] * 2
        + [pltpu.SemaphoreType.DMA((4,)), pltpu.SemaphoreType.DMA],
        [vmem_spec()] * 2 + [any_spec()] * 2,
        any_spec,
    )(turned, right, *others, *late)


def alternate_body(both, out):
    rows = out.shape[0]

    @pl.loop(0, rows // 8)
    def _(block):
        start = pl.multiple_of(block * 8, 8)
        for place in range(2):
            out[pl.ds(start, 8), place, :] = both[pl.ds(place * rows + start, 8), :].astype(f32)


def alternate(both):
    rows, columns = both.shape[0] // 2, both.shape[1]
    out = jax.ShapeDtypeStruct((rows, 2, columns), f32)
    return kernel_call(alternate_body, out, [], [vmem_spec()])(both)


def widen_body(rows, first, second, gain_one, gain_two):
    columns, more = first.shape[1], second.shape[1]
    first[...] = rows[:, :columns].astype(f32)
    second[...] = rows[:, columns : columns + more].astype(f32)
    turned = rows[:, columns + more :].astype(f32).T
    gain_one[...] = turned[0:1, :]
    gain_two[...] = turned[1:2, :]


def widen(rows, first, second):
    shape = jax.ShapeDtypeStruct
    size = rows.shape[0]
    outs = (
        shape((size, first), f32),
        shape((size, second), f32),
        shape((1, size), f32),
        shape((1, size), f32),
    )
    *wide, gain_one, gain_two = kernel_call(widen_body, outs, [], [vmem_spec()])(rows)
    return *wide, gain_one.reshape(size), gain_two.reshape(size)


def pass_body(keep_x, keep_y, from_x, from_y, for_x, for_y, *refs):
    held, in_sems, out_sem = refs[:4], refs[4], refs[5]
    blocks = in_sems.shape[0]
    size = keep_x.shape[0] // blocks

    @pl.loop(0, blocks)
    def _(block):
        rows = pl.ds(pl.multiple_of(block * size, size), size)
        for source, target in zip((keep_x, from_y, keep_y, from_x), held):
            pltpu.make_async_copy(source.at[rows], target.at[rows], in_sems.at[block]).start()

    @pl.loop(0, blocks)
    def _(block):
        rows = pl.ds(pl.multiple_of(block * size, size), size)
        for target in held:
            wait_all(target.at[rows], in_sems.at[block])
        for keep, come, out in ((held[0], held[1], for_x), (held[2], held[3], for_y)):
            keep[rows, :] = (keep[rows, :].astype(f32) + come[rows, :].astype(f32)).astype(bf16)
            pltpu.make_async_copy(keep.at[rows], out.at[rows], out_sem).start()

    wait_all(held[0], out_sem)
    wait_all(held[2], out_sem)


def pass_on(keep_x, keep_y, from_x, from_y, late=()):
    out = jax.ShapeDtypeStruct(keep_x.shape, bf16)
    return kernel_call(
        pass_body,
        (out, out),
        [pltpu.VMEM(keep_x.shape, bf16)] * 4
        + [pltpu.SemaphoreType.DMA((4,)), pltpu.SemaphoreType.DMA],
        [any_spec()] * 4,
        any_spec,
    )(keep_x, keep_y, from_x, from_y, *late)


class Grid:
    def __init__(self, dp, fsdp):
        self.dp, self.fsdp = dp, fsdp
        self.depth = fsdp // 2
        self.groups = [[f for f in range(fsdp) if f % 2 == y] for y in range(2)]
        self.dp_index = lax.axis_index("dp")
        self.y = lax.axis_index("fsdp") % 2
        self.spot = jnp.stack([self.dp_index, self.y]).astype(jnp.int32)
        self.outer = lax.axis_index("fsdp") // 2

    def core(self, value):
        return lax.ppermute(value, "dp", [(i, i ^ 1) for i in range(self.dp)])

    def cores(self, values):
        return [self.core(value) for value in values]

    def echo(self, value, times):
        for _ in range(times):
            value = self.core(value)
        return value

    def x_swap(self, value):
        return lax.ppermute(value, "dp", [(i, i ^ 2) for i in range(self.dp)])

    def y_swap(self, value):
        return lax.ppermute(value, "fsdp", [(i, i ^ 1) for i in range(self.fsdp)])

    def plane_sum(self, value):
        value = value + self.core(value)
        pairs = [
            (dp * self.fsdp + f, (dp ^ 2) * self.fsdp + (f ^ 1))
            for dp in range(self.dp)
            for f in range(self.fsdp)
        ]
        across = lax.ppermute(value, ("dp", "fsdp"), pairs)
        return value + self.x_swap(value) + self.y_swap(value) + across

    def shift(self, value, low, high, by):
        pairs = [
            (2 * outer + y, 2 * (outer + by) + y) for outer in range(low, high) for y in range(2)
        ]
        return lax.ppermute(value, "fsdp", pairs)

    def gather_outer(self, value):
        return lax.all_gather(value, "fsdp", axis=0, tiled=True, axis_index_groups=self.groups)

    def scatter_outer(self, value):
        return lax.psum_scatter(
            value, "fsdp", scatter_dimension=0, tiled=True, axis_index_groups=self.groups
        )

    def spread_first(self, first, second):
        return first, second, self.x_swap(first), self.y_swap(second)

    def spread_second(self, first, second, first_x, second_y):
        first, second, first_x, second_y = lax.optimization_barrier(
            (first, second, first_x, second_y)
        )
        first_xy = self.y_swap(first_x)
        second_xy = self.x_swap(second_y)
        first_y = self.y_swap(first)
        second_x = self.x_swap(second)
        return {
            (0, 0): (first, second),
            (1, 0): (first_x, second_x),
            (0, 1): (first_y, second_y),
            (1, 1): (first_xy, second_xy),
        }

    def collect_first(self, parts, late=()):
        _, _, keep_x, keep_y, to_x, to_y = parts
        from_x, from_y = self.x_swap(to_x), self.y_swap(to_y)
        return (*pass_on(keep_x, keep_y, from_x, from_y, late), from_x, from_y)

    def collect_second(self, parts, passed):
        for_x, for_y, from_x, from_y = passed
        return (parts[0], from_y, self.x_swap(for_x)), (parts[1], from_x, self.y_swap(for_y))

    def pieces(self, planes, rows, token=None):
        keys = [(dx, dy) for dx in range(2) for dy in range(2)]
        mine = [half for key in keys for half in planes[key]]
        sent = mine if token is None else after(mine, token)
        theirs = [self.core(half) for half in sent]
        return Pieces(self.depth, rows, mine[0].shape[-1], mine + theirs)

    def total(self, sums):
        halves = []
        for own, middle, last in sums:
            middle = middle[own.shape[0] :]
            halves.append(own.astype(f32) + middle.astype(f32) + last.astype(f32))
        return jnp.concatenate(halves, axis=0)


def local(
    tokens,
    w_q,
    w_kv,
    g_attn,
    g_mlp,
    w_o,
    w_gu,
    w_down,
    grad_out,
    grad_kv,
    group_id,
    group_size,
    group_weight,
):
    grid = Grid(lax.axis_size("dp"), lax.axis_size("fsdp"))
    length, width = tokens.shape
    kv_width = w_kv.shape[1]
    head_dim = kv_width // 2
    q_width = w_q.shape[1]
    shard_rows = w_q.shape[0]
    hidden_rows = w_down.shape[0]
    half = length // 2

    matches = jnp.arange(group_size.shape[0], dtype=jnp.int32) == group_id[0]
    factor = jnp.sum(jnp.where(matches, group_weight / group_size.astype(jnp.float32), 0.0))
    grad_low = (grad_out.astype(jnp.float32) * factor).astype(jnp.bfloat16)
    cosines, sines = rope_tables(length, head_dim)

    plane_keys = ((0, 0), (1, 0), (0, 1), (1, 1))

    def in_order(planes):
        return [piece for key in plane_keys for piece in planes[key]]

    gains = jnp.stack([g_attn, g_mlp], axis=1)
    w_in = jnp.concatenate([w_q, w_kv, jnp.pad(gains, ((0, 0), (0, lanes - 2)))], axis=1)
    w_in_column = grid.gather_outer(w_in)
    w_o_column = grid.gather_outer(w_o)
    grad_first = grid.spread_first(grad_low[:half], grad_low[half:])
    pairs = jnp.swapaxes(w_gu, 0, 1).reshape(2 * hidden_rows, width)
    gu_mine = grid.gather_outer(pairs)
    grad_planes = grid.spread_second(*grad_first)
    grad_rows = in_order(grad_planes)
    cut = grid.depth // 2
    w_in_column = after(w_in_column, grad_planes[1, 1]).reshape(grid.depth, shard_rows, -1)
    in_planes = grid.spread_second(*grid.spread_first(w_in_column[:cut], w_in_column[cut:]))
    in_pieces = grid.pieces(in_planes, shard_rows)
    down_mine = grid.gather_outer(w_down)
    w_o_column = after(w_o_column, in_planes[1, 1]).reshape(grid.depth, shard_rows, -1)
    o_first = grid.spread_first(w_o_column[:cut], w_o_column[cut:])
    h_one, q_low, kv_out, gain_rows = project(
        grid.spot, tokens, cosines, sines, in_pieces, q_width, kv_width, head_dim
    )
    o_planes = grid.spread_second(*after(o_first, q_low))
    prob, attended, turned, h_turned = attend(
        grid.spot, q_low, kv_out, h_one, grid.depth, shard_rows
    )
    o_pieces = grid.pieces(o_planes, shard_rows, attended)
    x_mid, h_first, h_second = mix(grid.spot, tokens, attended, gain_rows, o_pieces)

    ff_rows = in_order(grid.spread_second(*grid.spread_first(h_first, h_second)))
    gu_mine = after(gu_mine, ff_rows)
    by_shard = hidden_rows % 8 == 0
    run_rows = hidden_rows if by_shard else grid.depth * hidden_rows

    def turn(both, rows):
        return both.reshape(-1, rows, hidden_rows, width).swapaxes(0, 1).reshape(both.shape)

    if not by_shard:
        gu_mine = turn(gu_mine, 2)
    gu_other = grid.core(gu_mine)
    hid_mine, *scales_mine = gate(ff_rows, gu_mine, run_rows)
    hid_other, *scales_other = gate(ff_rows, gu_other, run_rows, [hid_mine])
    runs = grid.depth if by_shard else 1
    sent = hidden_sums([hid_other], grad_rows, run_rows, runs)
    down_sum = hidden_sums([hid_mine], grad_rows, run_rows, runs, grid.cores(sent), [sent[0]])
    down_sum, down_mine = lax.optimization_barrier((down_sum, down_mine))
    d_w_down = grid.scatter_outer(down_sum)
    down_other = grid.core(down_mine)
    pair_mine = gate_back(grad_rows, down_mine, scales_mine)
    pair_other = gate_back(grad_rows, down_other, scales_other, [pair_mine[0]])
    d_h_parts = rows_back((*pair_mine, *pair_other), (gu_mine, gu_other), run_rows)
    sent = hidden_sums(pair_other, ff_rows, run_rows, 2*runs, late=[d_h_parts[0]])
    d_h_passed = grid.collect_first(d_h_parts, [sent[0]])
    pair_sum = hidden_sums(
        pair_mine, ff_rows, run_rows, 2*runs, grid.cores(sent), [d_h_passed[0]]
    )
    pair_sum, d_w_down = lax.optimization_barrier((pair_sum, d_w_down))
    d_w_gu = grid.scatter_outer(pair_sum if by_shard else turn(pair_sum, grid.depth))
    d_h_first, d_h_second = grid.collect_second(d_h_parts, d_h_passed)
    d_h_sums = [*d_h_first, *d_h_second]

    d_mid, d_mid_low, gain_two_sum = norm_back(
        factor.reshape(1), x_mid, gain_rows, grad_out, d_h_sums, [pair_sum]
    )
    sent = send_sums(turned, d_mid_low)
    o_parts = keep_sums(turned, d_mid_low, grid.cores(sent))
    joined, d_kv = attend_back(
        grid.spot, factor.reshape(1), d_mid_low, grad_kv, q_low, kv_out,
        prob, cosines, sines, o_pieces, [o_parts[0]],
    )
    o_passed = grid.collect_first(o_parts, [joined])
    sent = send_sums(h_turned, joined, [o_passed[0]])
    d_w_o = grid.total(grid.collect_second(o_parts, o_passed)).astype(bf16)
    d_w_o = grid.scatter_outer(d_w_o).astype(f32)
    in_parts = keep_sums(h_turned, joined, grid.cores(sent), [o_passed[0]])
    d_tokens, gain_one_sum = finish(
        grid.spot, tokens, gain_rows, joined, d_mid, in_pieces, [in_parts[0]]
    )
    in_passed = grid.collect_first(in_parts, [gain_one_sum, d_w_gu])
    d_w_in = grid.total(grid.collect_second(in_parts, in_passed)).astype(bf16)
    if by_shard:
        d_w_gu = alternate(d_w_gu)
    else:
        d_w_gu = jnp.stack([d_w_gu[:hidden_rows], d_w_gu[hidden_rows:]], axis=1).astype(f32)
    d_w_down = d_w_down.astype(f32)
    mlp_parts = down((hid_mine, hid_other), (down_mine, down_other), [in_passed[0]])
    d_w_in, mlp_parts = lax.optimization_barrier((d_w_in, mlp_parts))
    mlp_sum = grid.total(grid.collect_second(mlp_parts, grid.collect_first(mlp_parts)))
    output = (x_mid + mlp_sum).astype(jnp.bfloat16)
    gain_sums = jnp.stack([gain_one_sum[0], gain_two_sum[0]], axis=0)
    gain_sums = grid.plane_sum(gain_sums)
    own_gains = lax.dynamic_slice(
        gain_sums.reshape(2, grid.dp, grid.depth, 2, shard_rows),
        (0, grid.dp_index, 0, grid.y, 0),
        (2, 1, grid.depth, 1, shard_rows),
    ).reshape(2, grid.depth * shard_rows)
    extra = jnp.pad(own_gains.T, ((0, 0), (0, lanes - 2))).astype(bf16)
    d_w_in = grid.scatter_outer(jnp.concatenate([d_w_in, extra], axis=1))
    return (
        output,
        d_tokens,
        kv_out,
        d_kv,
        *widen(d_w_in, q_width, kv_width),
        d_w_o,
        d_w_gu,
        d_w_down,
    )


def solution(mesh):
    placed = (
        P(("dp", "fsdp"), None),
        P(("dp", "fsdp"), None),
        P(("dp", "fsdp"), None),
        P(("dp", "fsdp")),
        P(("dp", "fsdp")),
        P(("dp", "fsdp"), None),
        P(("dp", "fsdp"), None, None),
        P(("dp", "fsdp"), None),
        P(("dp", "fsdp"), None),
        P(("dp", "fsdp"), None),
        P(("dp", "fsdp")),
        P(),
        P(),
    )
    return jax.shard_map(
        local,
        mesh=mesh,
        in_specs=placed,
        out_specs=(
            P(("dp", "fsdp"), None),
            P(("dp", "fsdp"), None),
            P(("dp", "fsdp"), None),
            P(("dp", "fsdp"), None),
            P(("dp", "fsdp"), None),
            P(("dp", "fsdp"), None),
            P(("dp", "fsdp")),
            P(("dp", "fsdp")),
            P(("dp", "fsdp"), None),
            P(("dp", "fsdp"), None, None),
            P(("dp", "fsdp"), None),
        ),
        check_vma=False,
    )
```
